32 devices in a mesh: maps: 8 (over z, x), chan: 4 (over y, core).
Axes of the slice: x: 2, y: 2, z: 4, core: 2. Of those that a mesh axis runs over, the one named last changes fastest.
Arguments:
- input_maps: bfloat16 [16, 18, 24, 512], P('maps', None, None, 'chan'), may hold values from 0 to 2
- valid_mask: int32 [16, 18, 24], P('maps'), may hold values from 0 to 1, as said below
- pool_index: int32 [16, 9, 12, 512], P('maps', None, None, 'chan'), may hold values from 0 to 3
- out_grad: bfloat16 [16, 9, 12, 512], P('maps', None, None, 'chan'), may hold values from -6 to 6
- conv_weights: float32 [3, 9, 512, 512], P(None, None, 'maps', 'chan'), may hold values from -0.09375 to 0.09375
- weight_first: float32 [3, 9, 512, 512], P(None, None, 'maps', 'chan'), may hold values from -86.463976 to 86.463976
- weight_second: float32 [3, 9, 512, 512], P(None, None, 'maps', 'chan'), may hold values from 176.9472 to 1869.0048
- norm_gain: float32 [3, 512], P(None, 'chan'), may hold values from 0.5 to 1.5
- norm_bias: float32 [3, 512], P(None, 'chan'), may hold values from -2.5 to 2.5
- norm_first: float32 [3, 2, 512], P(None, None, 'chan'), may hold values from -86.463976 to 86.463976
- norm_second: float32 [3, 2, 512], P(None, None, 'chan'), may hold values from 223.9488 to 1869.0048
Outputs:
- pooled: bfloat16 [16, 9, 12, 512], P('maps', None, None, 'chan')
- image_grad: float32 [16, 18, 24, 512], P('maps', None, None, 'chan')
- weight_grads: float32 [3, 9, 512, 512], P(None, None, 'maps', 'chan')
- new_weight_first: float32 [3, 9, 512, 512], P(None, None, 'maps', 'chan')
- new_weight_second: float32 [3, 9, 512, 512], P(None, None, 'maps', 'chan')
- new_weights: float32 [3, 9, 512, 512], P(None, None, 'maps', 'chan')
- weight_copy: bfloat16 [3, 9, 512, 512], P(None, None, 'maps', 'chan')
- norm_grads: float32 [3, 2, 512], P(None, None, 'chan')
- new_norm_first: float32 [3, 2, 512], P(None, None, 'chan')
- new_norm_second: float32 [3, 2, 512], P(None, None, 'chan')
- new_norms: float32 [3, 2, 512], P(None, None, 'chan')
The draws below stay inside these ranges and needn't reach their ends.
Inputs may be any that keep to these rules, and one draw needn't show every extreme that they name: `valid_mask`: 1 marks a pixel with valid depth, 0 one without. `pool_index`: 2 r + s for the kept pixel at row r and column s of its window.
All inputs are finite; a program needn't handle non-finite values.
Results may differ from the reference program's by a relative error of at most 0.02.
Values may be sent and summed in bfloat16 or wider, within the bound.
A program may use at most 128 MiB of HBM per device.

```python
from functools import partial
import jax
import jax.numpy as jnp
from jax import lax

C = 512
H = 18
W = 24
LAYERS = 3
TAPS = 9
MAPS = 16
HALF_H = 9
HALF_W = 12


def draw_valid_mask(key, part):
    key_maps = jax.random.fold_in(key, 11)
    key_cells = jax.random.fold_in(key, 23)
    picked = jax.random.randint(key_maps, (MAPS,), 0, 8)
    order = jnp.arange(MAPS, dtype=jnp.int32)
    base_limit = 300 + 650 * order // max(MAPS - 1, 1)
    divisor = jnp.where(picked == 0, 4, jnp.where(picked == 1, 2, 1)).astype(jnp.int32)
    limit = base_limit // divisor
    cells = jax.random.randint(key_cells, (MAPS, H, W), 0, 1000)
    return (cells < limit[:, None, None]).astype(jnp.int32)


def kernel_scale():
    return jnp.array([0.18, 0.16, 0.26], jnp.float32)[:LAYERS] * jnp.float32(MAPS * H * W) ** 0.5


def norm_scale():
    return jnp.array([0.18, 0.21, 0.26], jnp.float32)[:LAYERS] * jnp.float32(MAPS * H * W) ** 0.5


def draw_weight_first(key, part):
    values = jax.random.truncated_normal(jax.random.fold_in(key, 31), -4.0, 4.0, (LAYERS, TAPS, C, C), jnp.float32)
    return values * kernel_scale()[:, None, None, None]


def draw_weight_second(key, part):
    factor = jnp.exp(jax.random.uniform(jax.random.fold_in(key, 37), (LAYERS, TAPS, C, C), jnp.float32, 0.0, 1.3862944))
    scale = kernel_scale()
    return factor * (scale * scale)[:, None, None, None]


def draw_norm_first(key, part):
    values = jax.random.truncated_normal(jax.random.fold_in(key, 41), -4.0, 4.0, (LAYERS, 2, C), jnp.float32)
    return values * norm_scale()[:, None, None]


def draw_norm_second(key, part):
    factor = jnp.exp(jax.random.uniform(jax.random.fold_in(key, 43), (LAYERS, 2, C), jnp.float32, 0.0, 1.3862944))
    scale = norm_scale()
    return factor * (scale * scale)[:, None, None]


def place_ends(drawn, stream_key, least, largest):
    place = [jax.random.randint(jax.random.fold_in(stream_key, axis), (), 0, length) for axis, length in enumerate(drawn.shape)]
    longest = drawn.shape.index(max(drawn.shape))
    next_to = place[:longest] + [(place[longest] + 1) % drawn.shape[longest]] + place[longest + 1:]
    return drawn.at[tuple(place)].set(least).at[tuple(next_to)].set(largest)


def steps_of(own_key, dims, pieces, smallest, top_value):
    loudness, own = 1.0, jax.random.fold_in(own_key, 6)
    for axis_at, parts in pieces:
        draws = jnp.exp(jax.random.uniform(jax.random.fold_in(own, axis_at), (parts,), jnp.float32, smallest / len(pieces), top_value / len(pieces)))
        loudness = loudness * jnp.repeat(draws, dims[axis_at] // parts).reshape([-1 if axis == axis_at else 1 for axis in range(len(dims))])
    return loudness


def noise(stream_key, dims, scale, most, split=(), kind=jnp.bfloat16):
    entries = jax.random.normal(stream_key, dims, jnp.float32) * scale
    if len(split) > 0:
        entries = steps_of(stream_key, dims, split, -0.22, 0.18) * entries
    return jnp.clip(entries, min=-most, max=most).astype(kind)


def setup_inputs(seed: int = 0) -> dict:
    key_list = jax.random.split(jax.random.key(seed), 12)
    input_maps = jnp.clip(2.0 * jax.random.uniform(key_list[0], (MAPS, H, W, C), jnp.float32) ** steps_of(key_list[0], (MAPS, H, W, C), ((0, 8), (3, 4)), -0.2, 0.2), 0.0, 2.0).astype(jnp.bfloat16)
    valid_mask = draw_valid_mask(jax.random.fold_in(key_list[11], 71), 0)
    pool_index = place_ends(jax.random.randint(key_list[2], (MAPS, HALF_H, HALF_W, C), 0, 4), jax.random.fold_in(key_list[2], 1), 0, 3).astype(jnp.int32)
    out_grad = noise(key_list[3], (MAPS, HALF_H, HALF_W, C), 1.0, 6.0, ((0, 8), (3, 4)))
    conv_weights = noise(key_list[4], (LAYERS, TAPS, C, C), (TAPS * C) ** -0.5, 0.09375, ((2, 8), (3, 4)), jnp.float32)
    weight_first = draw_weight_first(jax.random.fold_in(key_list[11], 71), 0)
    weight_second = draw_weight_second(jax.random.fold_in(key_list[11], 71), 0)
    norm_gain = jnp.clip(1.0 + 0.1 * jax.random.normal(key_list[7], (LAYERS, C), jnp.float32), 0.5, 1.5)
    norm_bias = noise(key_list[8], (LAYERS, C), 0.3, 2.5, ((1, 4),), jnp.float32)
    norm_first = draw_norm_first(jax.random.fold_in(key_list[11], 71), 0)
    norm_second = draw_norm_second(jax.random.fold_in(key_list[11], 71), 0)
    return dict(input_maps=input_maps, valid_mask=valid_mask, pool_index=pool_index, out_grad=out_grad, conv_weights=conv_weights, weight_first=weight_first, weight_second=weight_second, norm_gain=norm_gain, norm_bias=norm_bias, norm_first=norm_first, norm_second=norm_second)


@jax.custom_vjp
def low(v):
    return lax.optimization_barrier(v.astype(jnp.bfloat16)).astype(jnp.float32)

@jax.custom_vjp
def low_back(v):
    return v

def low_keep(v):
    return (low(v), None)

def low_pass(kept, grad):
    return (grad,)

def back_keep(v):
    return (v, None)

def back_low(kept, grad):
    return (low(grad),)
low.defvjp(low_keep, low_pass)
low_back.defvjp(back_keep, back_low)
beta_first = 0.5
beta_second = 0.5
rate_conv = 0.01
rate_norm = 0.2
decay_rate = 0.01
adam_epsilon = 1e-08
norm_epsilon = 1e-05
step_count = 5.0

def convolve(activation, kernel):
    shaped = kernel.reshape(3, 3, kernel.shape[1], kernel.shape[2])
    return lax.conv_general_dilated(activation, shaped, (1, 1), 'SAME', dimension_numbers=('NHWC', 'HWIO', 'NHWC'), precision=lax.Precision.HIGHEST)

def select_window(activation, pool_index):
    map_count, height, map_width, channels = activation.shape
    windows = activation.reshape(map_count, height // 2, 2, map_width // 2, 2, channels)
    pooled = jnp.zeros(pool_index.shape, jnp.float32)
    for corner in range(4):
        pooled = pooled + jnp.where(pool_index == corner, windows[:, :, corner // 2, :, corner % 2, :], 0.0)
    return pooled

def forward(input_float, weights, gains, biases, mask_float=None, pool_index=None):
    valid_count = jnp.sum(mask_float)
    activation = input_float * mask_float
    for layer_index in range(LAYERS):
        kernel = low(weights[layer_index])
        if layer_index > 0:
            activation = low(activation)
        conv_out = low_back(convolve(activation, kernel))
        center = lax.optimization_barrier(jnp.sum(conv_out * mask_float, axis=(0, 1, 2))) / valid_count
        centered = conv_out - center
        variance = lax.optimization_barrier(jnp.sum(mask_float * centered * centered, axis=(0, 1, 2))) / valid_count
        normed = centered * lax.rsqrt(variance + norm_epsilon)
        shifted = gains[layer_index] * normed + biases[layer_index]
        activation = jax.nn.silu(shifted) * mask_float
    return select_window(activation, pool_index)

def adamw_update(parameter, gradient, first_moment, second_moment, step_rate):
    first_new = beta_first * first_moment + (1.0 - beta_first) * gradient
    second_new = beta_second * second_moment + (1.0 - beta_second) * gradient * gradient
    first_hat = first_new / (1.0 - beta_first ** step_count)
    second_hat = second_new / (1.0 - beta_second ** step_count)
    updated = parameter - step_rate * (first_hat / (jnp.sqrt(second_hat) + adam_epsilon) + decay_rate * parameter)
    return (updated, first_new, second_new)

def reference(input_maps, valid_mask, pool_index, out_grad, conv_weights, weight_first, weight_second, norm_gain, norm_bias, norm_first, norm_second):
    mask_float = valid_mask.astype(jnp.float32)[..., None]
    input_float = input_maps.astype(jnp.float32)
    pooled, pullback = jax.vjp(partial(forward, mask_float=mask_float, pool_index=pool_index), input_float, conv_weights, norm_gain, norm_bias)
    image_grad, weight_grads, gain_grads, bias_grads = pullback(out_grad.astype(jnp.float32))
    norm_grads = jnp.stack([gain_grads, bias_grads], axis=1)
    new_weights, new_weight_first, new_weight_second = adamw_update(conv_weights, weight_grads, weight_first, weight_second, rate_conv)
    norm_values = jnp.stack([norm_gain, norm_bias], axis=1)
    new_norms, new_norm_first, new_norm_second = adamw_update(norm_values, norm_grads, norm_first, norm_second, rate_norm)
    return (pooled.astype(jnp.bfloat16), image_grad, weight_grads, new_weight_first, new_weight_second, new_weights, new_weights.astype(jnp.bfloat16), norm_grads, new_norm_first, new_norm_second, new_norms)
```

```python
import functools

import jax
import jax.numpy as jnp
from jax import lax
from jax.experimental import pallas as pl
from jax.experimental.pallas import tpu as pltpu
from jax.sharding import PartitionSpec as P

beta_first = 0.5
beta_second = 0.5
rate_conv = 0.01
rate_norm = 0.2
decay_rate = 0.01
adam_epsilon = 1e-08
norm_epsilon = 1e-05
step_count = 5.0

MESH = pl.DeviceIdType.MESH
F32 = jnp.float32
BF16 = jnp.bfloat16
LANES = 128
PAD = 32


def adamw_update(parameter, gradient, first_moment, second_moment, step_rate):
    first_new = beta_first * first_moment + (1.0 - beta_first) * gradient
    second_new = beta_second * second_moment + (1.0 - beta_second) * gradient * gradient
    first_hat = first_new / (1.0 - beta_first**step_count)
    second_hat = second_new / (1.0 - beta_second**step_count)
    updated = parameter - step_rate * (
        first_hat / (jnp.sqrt(second_hat) + adam_epsilon) + decay_rate * parameter
    )
    return (updated, first_new, second_new)


def steps(low, high, body):
    if high - low <= 8:
        for index in range(low, high):
            body(index)
    else:
        pl.loop(low, high)(body)


def tile8(values):
    rows = values.shape[0]
    return jnp.sum(values.reshape(rows // 8, 8, LANES), axis=0)


def block_kernel(
    sizes,
    x_hbm, mask_hbm, index_hbm, grad_hbm, weight_hbm, gain_hbm, bias_hbm,
    pooled_hbm, image_hbm, wgrad_hbm, ngrad_hbm,
    x_in, mask_in, index_in, grad_in, weight_in, gain_in, bias_in,
    mask_ref, wcat, act, prod, conv, normed, slope, back, spread, zpad, dcat,
    grad_w, part, stat, pair_out, pair_in, far_out, far_in,
    gx_out, gx_in, gz_out, gz_in, pooled_ref, wgrad_ref, ngrad_ref,
    in_sem, out_sem,
    zr_s, zl_s, wx_s, w_r, st_s, st_r, ag_s, ag_r, pr_s, pr_r, fr_s, fr_r,
    gx_s, gx_r, gz_s, gz_r,
):
    maps, chans, layers, taps, nm, height, width = sizes
    line = maps // 2
    m = lax.axis_index("maps")
    c = lax.axis_index("chan")
    a = m // 2
    b = m % 2
    core = c + 1 - 2 * (c % 2)
    far = lax.rem(c + 2, 4)
    across = core + 2 - 4 * (core // 2)
    map_rows = height * width
    pixels = nm * map_rows
    rows_w = wcat.shape[2]
    wide = taps * LANES
    chunk = 6 * width
    chunks = pixels // chunk
    per_map = map_rows // chunk

    def rows_of(i):
        return pl.ds(pl.multiple_of(i * chunk, 16), chunk)

    def padded_rows(i, shift):
        n = i // per_map
        return n, pl.ds(pl.multiple_of((i - n * per_map) * chunk, 8) + (PAD + shift), chunk)

    drains = []

    def remote(src, dst, ssem, rsem, dev):
        return pltpu.make_async_remote_copy(
            src_ref=src, dst_ref=dst, send_sem=ssem, recv_sem=rsem,
            device_id=dev, device_id_type=MESH,
        )

    loads = []
    for i, (src, dst) in enumerate(
        (
            (weight_hbm, weight_in), (x_hbm, x_in), (mask_hbm, mask_in),
            (index_hbm, index_in), (grad_hbm, grad_in), (gain_hbm, gain_in), (bias_hbm, bias_in),
        )
    ):
        cp = pltpu.make_async_copy(src, dst, in_sem.at[i])
        cp.start()
        loads.append(cp)

    barrier = pltpu.get_barrier_semaphore()

    def greet(d):
        peer = lax.rem(m + d, maps)
        pl.semaphore_signal(barrier, inc=1, device_id=(peer, c), device_id_type=MESH)

    steps(1, maps, greet)
    for other in (core, far):
        pl.semaphore_signal(barrier, inc=1, device_id=(m, other), device_id_type=MESH)

    loads[0].wait()
    for l in range(layers):
        for t in range(taps):
            wcat[l, m, :, t * LANES : (t + 1) * LANES] = weight_in[l, t].astype(BF16)

    pl.semaphore_wait(barrier, maps + 1)

    def weight_copy(l, slot, dev, ssem):
        return remote(wcat.at[l, slot], wcat.at[l, slot], ssem, w_r.at[l, slot], dev)

    def gather_own(l, drain=False):
        def go(cond, dev, ssem):
            def run():
                cp = weight_copy(l, m, dev, ssem)
                cp.wait_send() if drain else cp.start()

            if cond is None:
                run()
            else:
                pl.when(cond)(run)

        go(a + 1 < line, (jnp.minimum(m + 2, maps - 1), c), zr_s.at[l, a])
        go(a > 0, (jnp.maximum(m - 2, 0), c), zl_s.at[l, a])
        go(None, (m + 1 - 2 * b, c), wx_s.at[l, a])

    def gather_step(l, s, drain=False):
        def piece(cond, src, onward_cond, onward, onward_sem):
            @pl.when(cond)
            def _():
                slot = src * 2 + b
                if not drain:
                    weight_copy(l, slot, (m, c), wx_s.at[l, src]).wait_recv()

                @pl.when(onward_cond)
                def _():
                    cp = weight_copy(l, slot, (onward, c), onward_sem.at[l, src])
                    cp.wait_send() if drain else cp.start()

                cp = weight_copy(l, slot, (m + 1 - 2 * b, c), wx_s.at[l, src])
                cp.wait_send() if drain else cp.start()

        piece(a >= s, jnp.maximum(a - s, 0), a + 1 < line, jnp.minimum(m + 2, maps - 1), zr_s)
        piece(a + s < line, jnp.minimum(a + s, line - 1), a > 0, jnp.maximum(m - 2, 0), zl_s)

    def gather_finish(l):
        def take(z):
            slot = z * 2 + (1 - b)
            weight_copy(l, slot, (m, c), wx_s.at[l, z]).wait_recv()

        steps(0, line, take)

    def gather_drain(l):
        gather_own(l, True)
        steps(1, line, lambda s: gather_step(l, s, True))

    def stat_copy(e, src, dst_dev, ssem):
        return remote(stat.at[e, src], stat.at[e, src], ssem, st_r.at[e, src], dst_dev)

    def stat_send(e, drain=False):
        def go(d):
            peer = lax.rem(m + d, maps)
            cp = stat_copy(e, m, (peer, c), st_s.at[e, peer])
            cp.wait_send() if drain else cp.start()

        steps(1, maps, go)

    def stat_wait(e):
        def go(d):
            src = lax.rem(m + d, maps)
            stat_copy(e, src, (src, c), st_s.at[e, src]).wait_recv()

        steps(1, maps, go)

    lane_own = pl.ds(pl.multiple_of(c * LANES, LANES), LANES)

    def act_copy(l, n, owner, dev, kind):
        view = act.at[l, pl.ds(n * map_rows, map_rows), pl.ds(pl.multiple_of(owner * LANES, LANES), LANES)]
        return remote(view, view, ag_s.at[l, kind, n], ag_r.at[l, kind, n], dev)

    def act_send(l, n):
        act_copy(l, n, c, (m, far), 1).start()
        act_copy(l, n, c, (m, core), 0).start()

    def act_forward(l, n):
        act_copy(l, n, far, (m, far), 1).wait_recv()
        act_copy(l, n, far, (m, core), 2).start()

    def act_finish(l, n):
        act_copy(l, n, core, (m, core), 0).wait_recv()
        act_copy(l, n, across, (m, core), 2).wait_recv()

    def act_drain(l):
        for n in range(nm):
            act_copy(l, n, c, (m, far), 1).wait_send()
            act_copy(l, n, c, (m, core), 0).wait_send()
            act_copy(l, n, far, (m, core), 2).wait_send()

    gather_own(0)

    loads[2].wait()
    row_of = lax.broadcasted_iota(jnp.int32, (height, width, LANES), 0).reshape(map_rows, LANES)
    col_of = lax.broadcasted_iota(jnp.int32, (height, width, LANES), 1).reshape(map_rows, LANES)
    lane_of = lax.broadcasted_iota(jnp.int32, (map_rows, LANES), 1)
    pick_row = jnp.where(row_of == lane_of, 1.0, 0.0).astype(BF16)[:, :height]
    pick_col = jnp.where(col_of == lane_of, 1.0, 0.0)[:, :width]
    ones = jnp.ones((width, LANES), BF16)
    for n in range(nm):
        valid_n = mask_in[n].astype(F32).astype(BF16)
        spread_rows = jnp.dot(pick_row, valid_n, preferred_element_type=F32) * pick_col
        mask_ref[pl.ds(n * map_rows, map_rows), :] = jnp.dot(
            spread_rows.astype(BF16), ones, preferred_element_type=F32
        )
    loads[1].wait()

    @pl.loop(0, chunks)
    def _(i):
        r = rows_of(i)
        act[0, r, lane_own] = (x_in[r, :].astype(F32) * mask_ref[r, :]).astype(BF16)

    for n in range(nm):
        act_send(0, n)

    for n in range(nm):
        for i in range(3):
            for j in range(3):
                prod[i, j, n, 0:PAD, :] = jnp.zeros((PAD, LANES), F32)
                prod[i, j, n, PAD + map_rows :, :] = jnp.zeros((PAD, LANES), F32)
        zpad[n, 0:PAD, :] = jnp.zeros((PAD, LANES), F32)
        zpad[n, PAD + map_rows :, :] = jnp.zeros((PAD, LANES), F32)

    col_chunk = lax.broadcasted_iota(jnp.int32, (6, width, LANES), 1).reshape(chunk, LANES)
    has_left = jnp.where(col_chunk > 0, 1.0, 0.0)
    has_right = jnp.where(col_chunk < width - 1, 1.0, 0.0)

    loads[3].wait()
    loads[4].wait()
    half_h, half_w = height // 2, width // 2

    @pl.loop(0, nm * half_h)
    def _(i):
        n = i // half_h
        h = i - n * half_h
        kept = index_in[n, h]
        value = grad_in[n, h].astype(F32)
        base = n * map_rows + 2 * h * width
        for r in range(2):
            for s in range(2):
                spread[pl.ds(base + r * width + s, half_w, stride=2), :] = jnp.where(
                    kept == 2 * r + s, value, 0.0
                )

    steps(1, line, lambda s: gather_step(0, s))
    for n in range(nm):
        act_forward(0, n)
    gather_finish(0)
    for n in range(nm):
        act_finish(0, n)
    loads[5].wait()
    loads[6].wait()

    for l in range(layers):
        if l > 0:
            steps(1, line, lambda s: gather_step(l, s))
            gather_finish(l)

        @pl.loop(0, 3)
        def _(i):
            cols = pl.ds(pl.multiple_of(i * (3 * LANES), LANES), 3 * LANES)
            w = wcat[l, :, :, cols].reshape(maps * rows_w, 3 * LANES)
            for n in range(nm):
                out = jnp.dot(
                    act[l, pl.ds(n * map_rows, map_rows), :], w, preferred_element_type=F32
                )
                for j in range(3):
                    prod[i, j, n, PAD : PAD + map_rows, :] = out[:, j * LANES : (j + 1) * LANES]

        def conv_chunk(i, carry):
            total, count = carry
            r = rows_of(i)
            value = None
            for j in range(3):
                side = None
                for k in range(3):
                    n, pr = padded_rows(i, width * (k - 1) + (j - 1))
                    term = prod[k, j, n, pr, :]
                    side = term if side is None else side + term
                if j == 0:
                    side = side * has_left
                if j == 2:
                    side = side * has_right
                value = side if value is None else value + side
            conv[r, :] = value
            valid = mask_ref[r, :]
            return total + tile8(value * valid), count + tile8(valid)

        zero8 = jnp.zeros((8, LANES), F32)
        total, count = lax.fori_loop(0, chunks, conv_chunk, (zero8, zero8))
        total = jnp.sum(total, axis=0, keepdims=True)
        count = jnp.sum(count, axis=0, keepdims=True)
        mean = total / jnp.maximum(count, 1.0)

        def dev_chunk(i, carry):
            r = rows_of(i)
            delta = conv[r, :] - mean
            return carry + tile8(delta * delta * mask_ref[r, :])

        spread_sum = jnp.sum(lax.fori_loop(0, chunks, dev_chunk, zero8), axis=0, keepdims=True)
        stat[l, m] = jnp.concatenate(
            [total, spread_sum, count, mean, jnp.zeros((4, LANES), F32)], axis=0
        )
        stat_send(l)
        if l + 1 < layers:
            gather_own(l + 1)
        stat_wait(l)

        def add_totals(s, carry):
            block = stat[l, s]
            return carry[0] + block[0:1, :], carry[1] + block[2:3, :]

        zero1 = jnp.zeros((1, LANES), F32)
        total, count = lax.fori_loop(0, maps, add_totals, (zero1, zero1))
        center = total / count

        def add_spread(s, carry):
            block = stat[l, s]
            delta = block[3:4, :] - center
            return carry + block[1:2, :] + block[2:3, :] * delta * delta

        variance = lax.fori_loop(0, maps, add_spread, zero1) / count
        inv_std = lax.rsqrt(variance + norm_epsilon)
        gain = gain_in[l : l + 1, :]
        bias = bias_in[l : l + 1, :]
        if l == 0:
            count_all = count
            scales = []
        scales.append(gain * inv_std)

        for n in range(nm):

            @pl.loop(n * per_map, (n + 1) * per_map)
            def _(i):
                r = rows_of(i)
                unit = (conv[r, :] - center) * inv_std
                pre = gain * unit + bias
                sigma = 1.0 / (1.0 + jnp.exp(-pre))
                valid = mask_ref[r, :]
                result = pre * sigma * valid
                normed[l, r, :] = unit
                slope[l, r, :] = sigma * (1.0 + pre * (1.0 - sigma)) * valid
                if l + 1 < layers:
                    act[l + 1, r, lane_own] = result.astype(BF16)
                else:
                    back[r, :] = result

            if l + 1 < layers:
                act_send(l + 1, n)
        if l + 1 < layers:
            for n in range(nm):
                act_forward(l + 1, n)
            for n in range(nm):
                act_finish(l + 1, n)

    @pl.loop(0, nm * half_h)
    def _(i):
        n = i // half_h
        h = i - n * half_h
        kept = index_in[n, h]
        base = n * map_rows + 2 * h * width
        total = jnp.zeros((half_w, LANES), F32)
        for r in range(2):
            for s in range(2):
                total = total + jnp.where(
                    kept == 2 * r + s, back[pl.ds(base + r * width + s, half_w, stride=2), :], 0.0
                )
        pooled_ref[n, h] = total.astype(BF16)

    outs = [pltpu.make_async_copy(pooled_ref, pooled_hbm, out_sem.at[0])]
    outs[0].start()

    def gx_copy(l, z):
        return remote(gx_out.at[l, z], gx_in.at[l, z], gx_s.at[l, z], gx_r.at[l, z], (m + 1 - 2 * b, c))

    def gz_send(l, z):
        return remote(gz_out.at[l, z], gz_in.at[l, a], gz_s.at[l, z], gz_r.at[l, a], (z * 2 + b, c))

    def gz_recv(l, z):
        return remote(gz_out.at[l, z], gz_in.at[l, z], gz_s.at[l, z], gz_r.at[l, z], (z * 2 + b, c))

    def shard(l, slot):
        return grad_w[l, pl.ds(pl.multiple_of(slot * rows_w, 8), rows_w), :]

    def scatter_x(l):
        def go(d):
            z = lax.rem(a + d, line)
            gx_out[l, z] = shard(l, z * 2 + 1 - b).astype(BF16)
            gx_copy(l, z).start()

        steps(1, line + 1, go)

    def scatter_z(l):
        def go(d):
            z = lax.rem(a + d, line)
            gx_copy(l, z).wait_recv()
            value = shard(l, z * 2 + b) + gx_in[l, z].astype(F32)
            gz_out[l, z] = value.astype(BF16)
            gz_send(l, z).start()

        steps(1, line, go)
        gx_copy(l, a).wait_recv()
        part_w = shard(l, m) + gx_in[l, a].astype(F32)
        for t in range(taps):
            wgrad_ref[l, t] = part_w[:, t * LANES : (t + 1) * LANES]

    def scatter_finish(l):
        def go(d):
            z = lax.rem(a + d, line)
            gz_recv(l, z).wait_recv()
            for t in range(taps):
                wgrad_ref[l, t] += gz_in[l, z, :, t * LANES : (t + 1) * LANES].astype(F32)

        steps(1, line, go)
        cp = pltpu.make_async_copy(wgrad_ref.at[l], wgrad_hbm.at[l], out_sem.at[3 + l])
        cp.start()
        outs.append(cp)

    def scatter_drain(l):
        def go(d):
            z = lax.rem(a + d, line)
            gx_copy(l, z).wait_send()

        steps(1, line + 1, go)

        def go2(d):
            z = lax.rem(a + d, line)
            gz_send(l, z).wait_send()

        steps(1, line, go2)

    half = 2 * LANES
    own_half = (c // 2) * half
    other_half = half - own_half
    lane_in_half = pl.ds(pl.multiple_of((c % 2) * LANES, LANES), LANES)
    lane_out_half = pl.ds(pl.multiple_of((1 - c % 2) * LANES, LANES), LANES)

    def pair_copy(l, h, n):
        return remote(
            pair_out.at[l, h, pl.ds(n * map_rows, map_rows), :],
            pair_in.at[l, h, pl.ds(n * map_rows, map_rows), :],
            pr_s.at[l, h, n], pr_r.at[l, h, n], (m, core),
        )

    def far_copy(l, n):
        return remote(
            far_out.at[l, pl.ds(n * map_rows, map_rows), :],
            far_in.at[l, pl.ds(n * map_rows, map_rows), :],
            fr_s.at[l, n], fr_r.at[l, n], (m, far),
        )

    for l in reversed(range(layers)):
        e = layers + l
        source = spread if l == layers - 1 else back

        def slope_chunk(i, carry):
            r = rows_of(i)
            value = source[r, :] * slope[l, r, :]
            conv[r, :] = value
            return carry[0] + tile8(value * normed[l, r, :]), carry[1] + tile8(value)

        zero8 = jnp.zeros((8, LANES), F32)
        gain_sum, bias_sum = lax.fori_loop(0, chunks, slope_chunk, (zero8, zero8))
        stat[e, m] = jnp.concatenate(
            [
                jnp.sum(gain_sum, axis=0, keepdims=True),
                jnp.sum(bias_sum, axis=0, keepdims=True),
                jnp.zeros((6, LANES), F32),
            ],
            axis=0,
        )
        stat_send(e)
        if l + 1 < layers:
            scatter_x(l + 1)
        stat_wait(e)

        def add_sums(s, carry):
            return carry + stat[e, s]

        sums = lax.fori_loop(0, maps, add_sums, jnp.zeros((8, LANES), F32))
        ngrad_ref[l] = sums[0:2, :]
        gain_grad = sums[0:1, :]
        bias_grad = sums[1:2, :]
        scale = scales[l]

        @pl.loop(0, chunks)
        def _(i):
            r = rows_of(i)
            value = (
                mask_ref[r, :]
                * scale
                * (conv[r, :] - (bias_grad + normed[l, r, :] * gain_grad) / count_all)
            )
            n, pr = padded_rows(i, 0)
            zpad[n, pr, :] = value

        @pl.loop(0, chunks)
        def _(i):
            r = rows_of(i)
            for k in range(3):
                for j in range(3):
                    n, pr = padded_rows(i, -(width * (k - 1) + (j - 1)))
                    term = zpad[n, pr, :]
                    if j == 0:
                        term = term * has_right
                    if j == 2:
                        term = term * has_left
                    t = 3 * k + j
                    dcat[r, t * LANES : (t + 1) * LANES] = term.astype(BF16)

        def half_grad(n, start):
            w = wcat[l].reshape(maps * rows_w, wide) if False else None
            slots = maps // 2
            first = (start // half) * slots
            w = wcat[l, pl.ds(first, slots), :, :].reshape(half, wide)
            return lax.dot_general(
                dcat[pl.ds(n * map_rows, map_rows), :], w, (((1,), (1,)), ((), ())),
                preferred_element_type=F32,
            )

        for h, start in ((0, other_half), (1, own_half)):
            for n in range(nm):
                r = pl.ds(n * map_rows, map_rows)
                part[h, r, :] = half_grad(n, start)
                pair_out[l, h, r, :] = part[h, r, lane_out_half].astype(BF16)
                pair_copy(l, h, n).start()
            if h == 0:
                for n in range(nm):
                    r = pl.ds(n * map_rows, map_rows)
                    pair_copy(l, h, n).wait_recv()
                    far_out[l, r, :] = (
                        part[h, r, lane_in_half] + pair_in[l, h, r, :].astype(F32)
                    ).astype(BF16)
                    far_copy(l, n).start()
        if l + 1 < layers:
            scatter_z(l + 1)

        slots = 2
        tile = slots * rows_w if rows_w * slots >= LANES else maps * rows_w // 4

        @pl.loop(0, (maps * rows_w) // tile)
        def _(i):
            cols = pl.ds(pl.multiple_of(i * tile, LANES), tile)
            grad_w[l, pl.ds(pl.multiple_of(i * tile, LANES), tile), :] = lax.dot_general(
                act[l, :, cols], dcat[...], (((0,), (0,)), ((), ())), preferred_element_type=F32
            )

        for n in range(nm):
            r = pl.ds(n * map_rows, map_rows)
            pair_copy(l, 1, n).wait_recv()
            far_copy(l, n).wait_recv()

            @pl.loop(n * per_map, (n + 1) * per_map)
            def _(i):
                r = rows_of(i)
                value = (
                    part[1, r, lane_in_half]
                    + pair_in[l, 1, r, :].astype(F32)
                    + far_in[l, r, :].astype(F32)
                )
                if l == 0:
                    value = value * mask_ref[r, :]
                back[r, :] = value

        if l + 1 < layers:
            scatter_finish(l + 1)

    cp = pltpu.make_async_copy(back, image_hbm, out_sem.at[1])
    cp.start()
    outs.append(cp)
    cp = pltpu.make_async_copy(ngrad_ref, ngrad_hbm, out_sem.at[2])
    cp.start()
    outs.append(cp)
    scatter_x(0)
    scatter_z(0)
    scatter_finish(0)

    for l in range(layers):
        gather_drain(l)
        act_drain(l)
        stat_send(l, True)
        stat_send(layers + l, True)
        scatter_drain(l)
        for n in range(nm):
            pair_copy(l, 0, n).wait_send()
            pair_copy(l, 1, n).wait_send()
            far_copy(l, n).wait_send()
    for cp in outs:
        cp.wait()


def block_call(maps, chans, x, mask, index, grad, weights, gain, bias):
    nm, height, width, lanes = x.shape
    layers, taps, rows_w, _ = weights.shape
    pixels = nm * height * width
    line = maps // 2
    wide = taps * LANES
    channels = chans * LANES
    map_rows = height * width
    sizes = (maps, chans, layers, taps, nm, height, width)
    vm = pltpu.VMEM
    dma = pltpu.SemaphoreType.DMA
    any_spec = pl.BlockSpec(memory_space=pl.ANY)
    scratch = [
        vm((pixels, LANES), BF16), vm(mask.shape, jnp.int32), vm(index.shape, jnp.int32),
        vm(grad.shape, BF16), vm(weights.shape, F32), vm(gain.shape, F32), vm(bias.shape, F32),
        vm((pixels, LANES), F32),
        vm((layers, maps, rows_w, wide), BF16),
        vm((layers, pixels, channels), BF16),
        vm((3, 3, nm, map_rows + 2 * PAD, LANES), F32),
        vm((pixels, LANES), F32),
        vm((layers, pixels, LANES), F32),
        vm((layers, pixels, LANES), F32),
        vm((pixels, LANES), F32),
        vm((pixels, LANES), F32),
        vm((nm, map_rows + 2 * PAD, LANES), F32),
        vm((pixels, wide), BF16),
        vm((layers, channels, wide), F32),
        vm((2, pixels, 2 * LANES), F32),
        vm((2 * layers, maps, 8, LANES), F32),
        vm((layers, 2, pixels, LANES), BF16), vm((layers, 2, pixels, LANES), BF16),
        vm((layers, pixels, LANES), BF16), vm((layers, pixels, LANES), BF16),
        vm((layers, line, rows_w, wide), BF16), vm((layers, line, rows_w, wide), BF16),
        vm((layers, line, rows_w, wide), BF16), vm((layers, line, rows_w, wide), BF16),
        vm((nm, height // 2, width // 2, LANES), BF16),
        vm((layers, taps, rows_w, LANES), F32),
        vm((layers, 2, LANES), F32),
        dma((7,)), dma((3 + layers,)),
        dma((layers, line)), dma((layers, line)), dma((layers, line)), dma((layers, maps)),
        dma((2 * layers, maps)), dma((2 * layers, maps)),
        dma((layers, 3, nm)), dma((layers, 3, nm)),
        dma((layers, 2, nm)), dma((layers, 2, nm)),
        dma((layers, nm)), dma((layers, nm)),
        dma((layers, line)), dma((layers, line)), dma((layers, line)), dma((layers, line)),
    ]
    return pl.pallas_call(
        functools.partial(block_kernel, sizes),
        out_shape=(
            jax.ShapeDtypeStruct((nm, height // 2, width // 2, LANES), BF16),
            jax.ShapeDtypeStruct((pixels, LANES), F32),
            jax.ShapeDtypeStruct((layers, taps, rows_w, LANES), F32),
            jax.ShapeDtypeStruct((layers, 2, LANES), F32),
        ),
        in_specs=[any_spec] * 7,
        out_specs=(any_spec,) * 4,
        scratch_shapes=scratch,
        compiler_params=pltpu.CompilerParams(
            collective_id=0, has_side_effects=True, vmem_limit_bytes=60 << 20
        ),
    )(x.reshape(pixels, LANES), mask, index, grad, weights, gain, bias)


def local(
    maps, chans,
    input_maps, valid_mask, pool_index, out_grad, conv_weights, weight_first, weight_second,
    norm_gain, norm_bias, norm_first, norm_second,
):
    pooled, image, weight_grads, norm_grads = block_call(
        maps, chans, input_maps, valid_mask, pool_index, out_grad, conv_weights, norm_gain, norm_bias
    )
    image_grad = image.reshape(input_maps.shape)
    new_weights, new_weight_first, new_weight_second = adamw_update(
        conv_weights, weight_grads, weight_first, weight_second, rate_conv
    )
    norm_values = jnp.stack([norm_gain, norm_bias], axis=1)
    new_norms, new_norm_first, new_norm_second = adamw_update(
        norm_values, norm_grads, norm_first, norm_second, rate_norm
    )
    return (
        pooled,
        image_grad,
        weight_grads,
        new_weight_first,
        new_weight_second,
        new_weights,
        new_weights.astype(BF16),
        norm_grads,
        new_norm_first,
        new_norm_second,
        new_norms,
    )


def solution(mesh):
    return jax.shard_map(
        functools.partial(local, mesh.shape["maps"], mesh.shape["chan"]),
        mesh=mesh,
        in_specs=(
            P("maps", None, None, "chan"),
            P("maps", None, None),
            P("maps", None, None, "chan"),
            P("maps", None, None, "chan"),
            P(None, None, "maps", "chan"),
            P(None, None, "maps", "chan"),
            P(None, None, "maps", "chan"),
            P(None, "chan"),
            P(None, "chan"),
            P(None, None, "chan"),
            P(None, None, "chan"),
        ),
        out_specs=(
            P("maps", None, None, "chan"),
            P("maps", None, None, "chan"),
            P(None, None, "maps", "chan"),
            P(None, None, "maps", "chan"),
            P(None, None, "maps", "chan"),
            P(None, None, "maps", "chan"),
            P(None, None, "maps", "chan"),
            P(None, None, "chan"),
            P(None, None, "chan"),
            P(None, None, "chan"),
            P(None, None, "chan"),
        ),
        check_vma=False,
    )
```

```python
import functools

import jax
import jax.numpy as jnp
from jax import lax
from jax.experimental import pallas as pl
from jax.experimental.pallas import tpu as pltpu
from jax.sharding import PartitionSpec as P

beta_first = 0.5
beta_second = 0.5
rate_conv = 0.01
rate_norm = 0.2
decay_rate = 0.01
adam_epsilon = 1e-08
norm_epsilon = 1e-05
step_count = 5.0

MESH = pl.DeviceIdType.MESH
F32 = jnp.float32
BF16 = jnp.bfloat16
LANES = 128
PAD = 32


def adamw_update(parameter, gradient, first_moment, second_moment, step_rate):
    first_new = beta_first * first_moment + (1.0 - beta_first) * gradient
    second_new = beta_second * second_moment + (1.0 - beta_second) * gradient * gradient
    first_hat = first_new / (1.0 - beta_first**step_count)
    second_hat = second_new / (1.0 - beta_second**step_count)
    updated = parameter - step_rate * (
        first_hat / (jnp.sqrt(second_hat) + adam_epsilon) + decay_rate * parameter
    )
    return (updated, first_new, second_new)


def steps(low, high, body):
    if high - low <= 8:
        for index in range(low, high):
            body(index)
    else:
        pl.loop(low, high)(body)


scope = jax.named_scope


def run(tasks, amount=None):
    for _ in range(len(tasks) if amount is None else min(amount, len(tasks))):
        tasks.pop(0)()


def tile8(values):
    rows = values.shape[0]
    return jnp.sum(values.reshape(rows // 8, 8, LANES), axis=0)


def block_kernel(
    sizes,
    x_hbm, mask_hbm, index_hbm, grad_hbm, weight_hbm, gain_hbm, bias_hbm,
    pooled_hbm, image_hbm, wgrad_hbm, ngrad_hbm,
    x_in, mask_in, index_in, grad_in, weight_in, gain_in, bias_in,
    mask_ref, wcat, act, prod, conv, normed, slope, back, result_ref, spread, pool32, zpad, dcat,
    grad_w, part, stat, pair_out, pair_in, far_out, far_in,
    gx_out, gx_in, gz_out, gz_in, pooled_ref, wgrad_ref, ngrad_ref,
    in_sem, out_sem,
    zr_s, zl_s, wx_s, w_r, st_s, st_r, ag_s, ag_r, pr_s, pr_r, fr_s, fr_r,
    gx_s, gx_r, gz_s, gz_r,
):
    maps, chans, layers, taps, nm, height, width = sizes
    line = maps // 2
    m = lax.axis_index("maps")
    c = lax.axis_index("chan")
    a = m // 2
    b = m % 2
    core = c + 1 - 2 * (c % 2)
    far = lax.rem(c + 2, 4)
    across = core + 2 - 4 * (core // 2)
    map_rows = height * width
    pixels = nm * map_rows
    rows_w = wcat.shape[2]
    wide = taps * LANES
    chunk = 6 * width
    chunks = pixels // chunk
    per_map = map_rows // chunk

    def rows_of(i):
        return pl.ds(pl.multiple_of(i * chunk, 16), chunk)

    def padded_rows(i, shift):
        n = i // per_map
        return n, pl.ds(pl.multiple_of((i - n * per_map) * chunk, 8) + (PAD + shift), chunk)

    drains = []

    def remote(src, dst, ssem, rsem, dev):
        return pltpu.make_async_remote_copy(
            src_ref=src, dst_ref=dst, send_sem=ssem, recv_sem=rsem,
            device_id=dev, device_id_type=MESH,
        )

    loads = []
    for i, (src, dst) in enumerate(
        (
            (weight_hbm, weight_in), (x_hbm, x_in), (mask_hbm, mask_in),
            (index_hbm, index_in), (grad_hbm, grad_in), (gain_hbm, gain_in), (bias_hbm, bias_in),
        )
    ):
        cp = pltpu.make_async_copy(src, dst, in_sem.at[i])
        cp.start()
        loads.append(cp)

    barrier = pltpu.get_barrier_semaphore()

    def greet(d):
        peer = lax.rem(m + d, maps)
        pl.semaphore_signal(barrier, inc=1, device_id=(peer, c), device_id_type=MESH)

    steps(1, maps, greet)
    for other in (core, far):
        pl.semaphore_signal(barrier, inc=1, device_id=(m, other), device_id_type=MESH)

    loads[0].wait()
    for l in range(layers):
        for t in range(taps):
            wcat[l, m, :, t * LANES : (t + 1) * LANES] = weight_in[l, t].astype(BF16)

    pl.semaphore_wait(barrier, maps + 1)

    pieces = w_r.shape[2]
    piece_rows = rows_w // pieces

    def weight_copy(l, slot, g, dev, ssem):
        view = wcat.at[l, slot, pl.ds(g * piece_rows, piece_rows)]
        return remote(view, view, ssem, w_r.at[l, slot, g], dev)

    def gather_own(l, drain=False):
        def go(cond, g, dev, ssem):
            def send():
                cp = weight_copy(l, m, g, dev, ssem)
                cp.wait_send() if drain else cp.start()

            if cond is None:
                send()
            else:
                pl.when(cond)(send)

        for g in range(pieces):
            go(a + 1 < line, g, (jnp.minimum(m + 2, maps - 1), c), zr_s.at[l, a, g])
            go(a > 0, g, (jnp.maximum(m - 2, 0), c), zl_s.at[l, a, g])
            go(None, g, (m + 1 - 2 * b, c), wx_s.at[l, a, g])

    def gather_step(l, s, g, drain=False):
        def piece(cond, src, onward_cond, onward, onward_sem):
            @pl.when(cond)
            def _():
                slot = src * 2 + b
                if not drain:
                    weight_copy(l, slot, g, (m, c), wx_s.at[l, src, g]).wait_recv()

                @pl.when(onward_cond)
                def _():
                    cp = weight_copy(l, slot, g, (onward, c), onward_sem.at[l, src, g])
                    cp.wait_send() if drain else cp.start()

                cp = weight_copy(l, slot, g, (m + 1 - 2 * b, c), wx_s.at[l, src, g])
                cp.wait_send() if drain else cp.start()

        piece(a >= s, jnp.maximum(a - s, 0), a + 1 < line, jnp.minimum(m + 2, maps - 1), zr_s)
        piece(a + s < line, jnp.minimum(a + s, line - 1), a > 0, jnp.maximum(m - 2, 0), zl_s)

    def gather_tasks(l, drain=False):
        if line <= 8:
            return [
                functools.partial(gather_step, l, s, g, drain)
                for s in range(1, line)
                for g in range(pieces)
            ]

        def everything():
            def go(s):
                for g in range(pieces):
                    gather_step(l, s, g, drain)

            steps(1, line, go)

        return [everything]

    def gather_finish(l):
        def take(z):
            for g in range(pieces):
                slot = z * 2 + (1 - b)
                weight_copy(l, slot, g, (m, c), wx_s.at[l, z, g]).wait_recv()

        steps(0, line, take)

    def gather_drain(l):
        gather_own(l, True)
        run(gather_tasks(l, True))

    def stat_copy(e, src, dst_dev, ssem):
        return remote(stat.at[e, src], stat.at[e, src], ssem, st_r.at[e, src], dst_dev)

    def stat_send(e, drain=False):
        def go(d):
            peer = lax.rem(m + d, maps)
            cp = stat_copy(e, m, (peer, c), st_s.at[e, peer])
            cp.wait_send() if drain else cp.start()

        steps(1, maps, go)

    def stat_wait(e):
        def go(d):
            src = lax.rem(m + d, maps)
            stat_copy(e, src, (src, c), st_s.at[e, src]).wait_recv()

        steps(1, maps, go)

    lane_own = pl.ds(pl.multiple_of(c * LANES, LANES), LANES)

    def act_copy(l, n, owner, dev, kind):
        view = act.at[l, pl.ds(n * map_rows, map_rows), pl.ds(pl.multiple_of(owner * LANES, LANES), LANES)]
        return remote(view, view, ag_s.at[l, kind, n], ag_r.at[l, kind, n], dev)

    def act_send(l, n):
        act_copy(l, n, c, (m, far), 1).start()
        act_copy(l, n, c, (m, core), 0).start()

    def act_forward(l, n):
        act_copy(l, n, far, (m, far), 1).wait_recv()
        act_copy(l, n, far, (m, core), 2).start()

    def act_finish(l, n):
        act_copy(l, n, core, (m, core), 0).wait_recv()
        act_copy(l, n, across, (m, core), 2).wait_recv()

    def act_drain(l):
        for n in range(nm):
            act_copy(l, n, c, (m, far), 1).wait_send()
            act_copy(l, n, c, (m, core), 0).wait_send()
            act_copy(l, n, far, (m, core), 2).wait_send()

    gather_own(0)

    loads[2].wait()
    col_of = lax.broadcasted_iota(jnp.int32, (width, width), 0)
    diagonal = col_of == lax.broadcasted_iota(jnp.int32, (width, width), 1)
    for n in range(nm):

        @pl.loop(0, height)
        def _(h):
            line_n = jnp.broadcast_to(mask_in[h, n : n + 1, :].astype(F32), (width, width))
            r = pl.ds(pl.multiple_of(n * map_rows + h * width, 8), width)
            conv[r, 0:width] = jnp.where(diagonal, line_n, 0.0)

    mask_ref[...] = jnp.dot(
        conv[:, 0:width].astype(BF16), jnp.ones((width, LANES), BF16), preferred_element_type=F32
    )
    loads[1].wait()

    @pl.loop(0, chunks)
    def _(i):
        r = rows_of(i)
        act[0, r, lane_own] = (x_in[r, :].astype(F32) * mask_ref[r, :]).astype(BF16)

    for n in range(nm):
        act_send(0, n)

    for n in range(nm):
        for i in range(3):
            for j in range(3):
                prod[i, j, n, 0:PAD, :] = jnp.zeros((PAD, LANES), F32)
                prod[i, j, n, PAD + map_rows :, :] = jnp.zeros((PAD, LANES), F32)
        zpad[n, 0:PAD, :] = jnp.zeros((PAD, LANES), F32)
        zpad[n, PAD + map_rows :, :] = jnp.zeros((PAD, LANES), F32)

    col_chunk = lax.broadcasted_iota(jnp.int32, (6, width, LANES), 1).reshape(chunk, LANES)
    has_left = jnp.where(col_chunk > 0, 1.0, 0.0)
    has_right = jnp.where(col_chunk < width - 1, 1.0, 0.0)

    loads[3].wait()
    loads[4].wait()
    half_h, half_w = height // 2, width // 2

    @pl.loop(0, half_h)
    def _(h):
        pool32[...] = grad_in[h].astype(F32)
        for n in range(nm):
            pick = pl.ds(n, half_w, stride=nm)
            kept = index_in[h, pick, :]
            value = pool32[pick, :]
            base = n * map_rows + 2 * h * width
            for r in range(2):
                for s in range(2):
                    spread[pl.ds(base + r * width + s, half_w, stride=2), :] = jnp.where(
                        kept == 2 * r + s, value, 0.0
                    )

    tasks = gather_tasks(0)
    with scope("gather0"):
        run(tasks)
    for n in range(nm):
        act_forward(0, n)
    with scope("gather0_end"):
        gather_finish(0)
    for n in range(nm):
        act_finish(0, n)
    loads[5].wait()
    loads[6].wait()

    for l in range(layers):
        @pl.loop(0, 3)
        def _(i):
            cols = pl.ds(pl.multiple_of(i * (3 * LANES), LANES), 3 * LANES)
            w = wcat[l, :, :, cols].reshape(maps * rows_w, 3 * LANES)
            for n in range(nm):
                out = jnp.dot(
                    act[l, pl.ds(n * map_rows, map_rows), :], w, preferred_element_type=F32
                )
                for j in range(3):
                    prod[i, j, n, PAD : PAD + map_rows, :] = out[:, j * LANES : (j + 1) * LANES]

        def conv_chunk(i, carry):
            total, count = carry
            r = rows_of(i)
            value = None
            for j in range(3):
                side = None
                for k in range(3):
                    n, pr = padded_rows(i, width * (k - 1) + (j - 1))
                    term = prod[k, j, n, pr, :]
                    side = term if side is None else side + term
                if j == 0:
                    side = side * has_left
                if j == 2:
                    side = side * has_right
                value = side if value is None else value + side
            conv[r, :] = value
            valid = mask_ref[r, :]
            return total + tile8(value * valid), count + tile8(valid)

        zero8 = jnp.zeros((8, LANES), F32)
        total, count = lax.fori_loop(0, chunks, conv_chunk, (zero8, zero8))
        total = jnp.sum(total, axis=0, keepdims=True)
        count = jnp.sum(count, axis=0, keepdims=True)
        mean = total / jnp.maximum(count, 1.0)

        def dev_chunk(i, carry):
            r = rows_of(i)
            delta = conv[r, :] - mean
            return carry + tile8(delta * delta * mask_ref[r, :])

        spread_sum = jnp.sum(lax.fori_loop(0, chunks, dev_chunk, zero8), axis=0, keepdims=True)
        stat[l, m] = jnp.concatenate(
            [total, spread_sum, count, mean, jnp.zeros((4, LANES), F32)], axis=0
        )
        stat_send(l)
        tasks = []
        if l + 1 < layers:
            gather_own(l + 1)
            tasks = gather_tasks(l + 1)
        with scope("stat_wait"):
            stat_wait(l)

        def add_totals(s, carry):
            block = stat[l, s]
            return carry[0] + block[0:1, :], carry[1] + block[2:3, :]

        zero1 = jnp.zeros((1, LANES), F32)
        total, count = lax.fori_loop(0, maps, add_totals, (zero1, zero1))
        center = total / count

        def add_spread(s, carry):
            block = stat[l, s]
            delta = block[3:4, :] - center
            return carry + block[1:2, :] + block[2:3, :] * delta * delta

        variance = lax.fori_loop(0, maps, add_spread, zero1) / count
        inv_std = lax.rsqrt(variance + norm_epsilon)
        gain = gain_in[l : l + 1, :]
        bias = bias_in[l : l + 1, :]
        if l == 0:
            count_all = count
            scales = []
        scales.append(gain * inv_std)

        for n in range(nm):

            @pl.loop(n * per_map, (n + 1) * per_map)
            def _(i):
                r = rows_of(i)
                unit = (conv[r, :] - center) * inv_std
                pre = gain * unit + bias
                sigma = 1.0 / (1.0 + jnp.exp(-pre))
                valid = mask_ref[r, :]
                result = pre * sigma * valid
                normed[l, r, :] = unit
                slope[l, r, :] = sigma * (1.0 + pre * (1.0 - sigma)) * valid
                if l + 1 < layers:
                    act[l + 1, r, lane_own] = result.astype(BF16)
                else:
                    result_ref[r, :] = result

            if l + 1 < layers:
                act_send(l + 1, n)
        if l + 1 < layers:
            with scope("gather_a"):
                run(tasks, pieces + 1)
            for n in range(nm):
                with scope("act_forward"):
                    act_forward(l + 1, n)
                with scope("gather_b"):
                    run(tasks, 1)
            with scope("gather_c"):
                run(tasks)
            with scope("act_finish"):
                for n in range(nm):
                    act_finish(l + 1, n)
            with scope("gather_end"):
                gather_finish(l + 1)

    def pool():
        @pl.loop(0, half_h)
        def _(h):
            for n in range(nm):
                pick = pl.ds(n, half_w, stride=nm)
                kept = index_in[h, pick, :]
                base = n * map_rows + 2 * h * width
                total = jnp.zeros((half_w, LANES), F32)
                for r in range(2):
                    for s in range(2):
                        total = total + jnp.where(
                            kept == 2 * r + s,
                            result_ref[pl.ds(base + r * width + s, half_w, stride=2), :],
                            0.0,
                        )
                pool32[pick, :] = total
            pooled_ref[h] = pool32[...].astype(BF16)

        cp = pltpu.make_async_copy(pooled_ref, pooled_hbm, out_sem.at[0])
        cp.start()
        outs.append(cp)

    outs = []

    def gx_copy(l, z):
        return remote(gx_out.at[l, z], gx_in.at[l, z], gx_s.at[l, z], gx_r.at[l, z], (m + 1 - 2 * b, c))

    def gz_send(l, z):
        return remote(gz_out.at[l, z], gz_in.at[l, a], gz_s.at[l, z], gz_r.at[l, a], (z * 2 + b, c))

    def gz_recv(l, z):
        return remote(gz_out.at[l, z], gz_in.at[l, z], gz_s.at[l, z], gz_r.at[l, z], (z * 2 + b, c))

    def shard(l, slot):
        return grad_w[l, pl.ds(pl.multiple_of(slot * rows_w, 8), rows_w), :]

    tile = 2 * rows_w
    fine = tile % LANES == 0

    def kernel_grad(l, first, amount):
        rows = pl.ds(pl.multiple_of(first, LANES), amount)
        grad_w[l, rows, :] = lax.dot_general(
            act[l, :, rows], dcat[...], (((0,), (0,)), ((), ())), preferred_element_type=F32
        )

    def kernel_grads(l):
        if not fine:
            coarse = (maps * rows_w) // 4
            pl.loop(0, 4)(lambda i: kernel_grad(l, i * coarse, coarse))

        def go(d):
            z = lax.rem(a + d, line)
            if fine:
                kernel_grad(l, z * tile, tile)
            gx_out[l, z] = shard(l, z * 2 + 1 - b).astype(BF16)
            if l == 0:
                gx_copy(l, z).start()

        steps(1, line + 1, go)

    def scatter_x(l):
        steps(1, line + 1, lambda d: gx_copy(l, lax.rem(a + d, line)).start())

    def scatter_z(l, d):
        z = lax.rem(a + d, line)
        gx_copy(l, z).wait_recv()
        value = shard(l, z * 2 + b) + gx_in[l, z].astype(F32)
        gz_out[l, z] = value.astype(BF16)
        gz_send(l, z).start()

    def scatter_own(l):
        gx_copy(l, a).wait_recv()
        part_w = shard(l, m) + gx_in[l, a].astype(F32)
        for t in range(taps):
            wgrad_ref[l, t] = part_w[:, t * LANES : (t + 1) * LANES]

    def scatter_tasks(l):
        if line <= 8:
            return [functools.partial(scatter_z, l, d) for d in range(1, line)] + [
                functools.partial(scatter_own, l)
            ]

        def everything():
            steps(1, line, lambda d: scatter_z(l, d))
            scatter_own(l)

        return [everything]

    def scatter_finish(l):
        def go(d):
            z = lax.rem(a + d, line)
            gz_recv(l, z).wait_recv()
            for t in range(taps):
                wgrad_ref[l, t] += gz_in[l, z, :, t * LANES : (t + 1) * LANES].astype(F32)

        steps(1, line, go)
        cp = pltpu.make_async_copy(wgrad_ref.at[l], wgrad_hbm.at[l], out_sem.at[3 + l])
        cp.start()
        outs.append(cp)

    def scatter_drain(l):
        def go(d):
            z = lax.rem(a + d, line)
            gx_copy(l, z).wait_send()

        steps(1, line + 1, go)

        def go2(d):
            z = lax.rem(a + d, line)
            gz_send(l, z).wait_send()

        steps(1, line, go2)

    half = 2 * LANES
    own_half = (c // 2) * half
    other_half = half - own_half
    lane_in_half = pl.ds(pl.multiple_of((c % 2) * LANES, LANES), LANES)
    lane_out_half = pl.ds(pl.multiple_of((1 - c % 2) * LANES, LANES), LANES)

    def pair_copy(l, h, n):
        return remote(
            pair_out.at[l, h, pl.ds(n * map_rows, map_rows), :],
            pair_in.at[l, h, pl.ds(n * map_rows, map_rows), :],
            pr_s.at[l, h, n], pr_r.at[l, h, n], (m, core),
        )

    def far_copy(l, n):
        return remote(
            far_out.at[l, pl.ds(n * map_rows, map_rows), :],
            far_in.at[l, pl.ds(n * map_rows, map_rows), :],
            fr_s.at[l, n], fr_r.at[l, n], (m, far),
        )

    for l in reversed(range(layers)):
        e = layers + l
        source = spread if l == layers - 1 else back

        def slope_chunk(i, carry):
            r = rows_of(i)
            value = source[r, :] * slope[l, r, :]
            conv[r, :] = value
            return carry[0] + tile8(value * normed[l, r, :]), carry[1] + tile8(value)

        zero8 = jnp.zeros((8, LANES), F32)
        gain_sum, bias_sum = lax.fori_loop(0, chunks, slope_chunk, (zero8, zero8))
        stat[e, m] = jnp.concatenate(
            [
                jnp.sum(gain_sum, axis=0, keepdims=True),
                jnp.sum(bias_sum, axis=0, keepdims=True),
                jnp.zeros((6, LANES), F32),
            ],
            axis=0,
        )
        stat_send(e)
        tasks = []
        if l + 1 < layers:
            scatter_x(l + 1)
            tasks = scatter_tasks(l + 1)
        else:
            pool()
        with scope("stat_wait_back"):
            stat_wait(e)

        def add_sums(s, carry):
            return carry + stat[e, s]

        sums = lax.fori_loop(0, maps, add_sums, jnp.zeros((8, LANES), F32))
        ngrad_ref[l] = sums[0:2, :]
        gain_grad = sums[0:1, :]
        bias_grad = sums[1:2, :]
        scale = scales[l]

        def conv_grad(n):
            @pl.loop(n * per_map, (n + 1) * per_map)
            def _(i):
                r = rows_of(i)
                value = (
                    mask_ref[r, :]
                    * scale
                    * (conv[r, :] - (bias_grad + normed[l, r, :] * gain_grad) / count_all)
                )
                pr = pl.ds(pl.multiple_of((i - n * per_map) * chunk, 16) + PAD, chunk)
                zpad[n, pr, :] = value

            @pl.loop(n * per_map, (n + 1) * per_map)
            def _(i):
                r = rows_of(i)
                for k in range(3):
                    for j in range(3):
                        shift = PAD - (width * (k - 1) + (j - 1))
                        pr = pl.ds(pl.multiple_of((i - n * per_map) * chunk, 16) + shift, chunk)
                        term = zpad[n, pr, :]
                        if j == 0:
                            term = term * has_right
                        if j == 2:
                            term = term * has_left
                        t = 3 * k + j
                        dcat[r, t * LANES : (t + 1) * LANES] = term.astype(BF16)

        def input_grad(h, n):
            start = other_half if h == 0 else own_half
            slots = maps // 2
            w = wcat[l, pl.ds((start // half) * slots, slots), :, :].reshape(half, wide)
            r = pl.ds(n * map_rows, map_rows)
            part[h, r, :] = lax.dot_general(
                dcat[r, :], w, (((1,), (1,)), ((), ())), preferred_element_type=F32
            )
            pair_out[l, h, r, :] = part[h, r, lane_out_half].astype(BF16)
            pair_copy(l, h, n).start()

        def to_far(n):
            r = pl.ds(n * map_rows, map_rows)
            pair_copy(l, 0, n).wait_recv()
            far_out[l, r, :] = (
                part[0, r, lane_in_half] + pair_in[l, 0, r, :].astype(F32)
            ).astype(BF16)
            far_copy(l, n).start()

        if l > 0:
            for n in range(nm):
                with scope("conv_grad"):
                    conv_grad(n)
                with scope("input_grad"):
                    input_grad(0, n)
                if n > 0:
                    with scope("to_far"):
                        to_far(n - 1)
            with scope("scatter_z"):
                run(tasks, 1)
            for n in range(nm):
                with scope("input_grad"):
                    input_grad(1, n)
                if n == 0:
                    with scope("to_far"):
                        to_far(nm - 1)
            with scope("scatter_z"):
                run(tasks, 1)
            with scope("kernel_grad"):
                kernel_grads(l)
            with scope("scatter_z"):
                run(tasks, 1)
        else:
            for n in range(nm):
                conv_grad(n)
            with scope("kernel_grad"):
                kernel_grads(l)
            with scope("scatter_z"):
                run(tasks)
            for n in range(nm):
                with scope("input_grad"):
                    input_grad(0, n)
            tasks = scatter_tasks(0)
            with scope("to_far"):
                for n in range(nm):
                    to_far(n)
            with scope("scatter_z"):
                run(tasks, 1)
            for n in range(nm):
                with scope("input_grad"):
                    input_grad(1, n)
            with scope("scatter_z"):
                run(tasks, 1)

        for n in range(nm):
            r = pl.ds(n * map_rows, map_rows)
            with scope("far_wait"):
                pair_copy(l, 1, n).wait_recv()
                far_copy(l, n).wait_recv()

            @pl.loop(n * per_map, (n + 1) * per_map)
            def _(i):
                r = rows_of(i)
                value = (
                    part[1, r, lane_in_half]
                    + pair_in[l, 1, r, :].astype(F32)
                    + far_in[l, r, :].astype(F32)
                )
                if l == 0:
                    value = value * mask_ref[r, :]
                back[r, :] = value

        with scope("scatter_z"):
            run(tasks)

    cp = pltpu.make_async_copy(back, image_hbm, out_sem.at[1])
    cp.start()
    outs.append(cp)
    cp = pltpu.make_async_copy(ngrad_ref, ngrad_hbm, out_sem.at[2])
    cp.start()
    outs.append(cp)
    with scope("scatter_end"):
        for l in reversed(range(layers)):
            scatter_finish(l)

    for l in range(layers):
        gather_drain(l)
        act_drain(l)
        stat_send(l, True)
        stat_send(layers + l, True)
        scatter_drain(l)
        for n in range(nm):
            pair_copy(l, 0, n).wait_send()
            pair_copy(l, 1, n).wait_send()
            far_copy(l, n).wait_send()
    for cp in outs:
        cp.wait()


def block_call(maps, chans, x, mask, index, grad, weights, gain, bias):
    nm, height, width, lanes = x.shape
    layers, taps, rows_w, _ = weights.shape
    pixels = nm * height * width
    line = maps // 2
    wide = taps * LANES
    channels = chans * LANES
    map_rows = height * width
    sizes = (maps, chans, layers, taps, nm, height, width)
    pieces = 2 if rows_w % 32 == 0 else 1
    vm = pltpu.VMEM
    dma = pltpu.SemaphoreType.DMA
    any_spec = pl.BlockSpec(memory_space=pl.ANY)
    scratch = [
        vm((pixels, LANES), BF16), vm(mask.shape, jnp.int32), vm(index.shape, jnp.int32),
        vm(grad.shape, BF16), vm(weights.shape, F32), vm(gain.shape, F32), vm(bias.shape, F32),
        vm((pixels, LANES), F32),
        vm((layers, maps, rows_w, wide), BF16),
        vm((layers, pixels, channels), BF16),
        vm((3, 3, nm, map_rows + 2 * PAD, LANES), F32),
        vm((pixels, LANES), F32),
        vm((layers, pixels, LANES), F32),
        vm((layers, pixels, LANES), F32),
        vm((pixels, LANES), F32),
        vm((pixels, LANES), F32),
        vm((pixels, LANES), F32),
        vm((nm * (width // 2), LANES), F32),
        vm((nm, map_rows + 2 * PAD, LANES), F32),
        vm((pixels, wide), BF16),
        vm((layers, channels, wide), F32),
        vm((2, pixels, 2 * LANES), F32),
        vm((2 * layers, maps, 8, LANES), F32),
        vm((layers, 2, pixels, LANES), BF16), vm((layers, 2, pixels, LANES), BF16),
        vm((layers, pixels, LANES), BF16), vm((layers, pixels, LANES), BF16),
        vm((layers, line, rows_w, wide), BF16), vm((layers, line, rows_w, wide), BF16),
        vm((layers, line, rows_w, wide), BF16), vm((layers, line, rows_w, wide), BF16),
        vm(index.shape, BF16),
        vm((layers, taps, rows_w, LANES), F32),
        vm((layers, 2, LANES), F32),
        dma((7,)), dma((3 + layers,)),
        dma((layers, line, pieces)), dma((layers, line, pieces)), dma((layers, line, pieces)),
        dma((layers, maps, pieces)),
        dma((2 * layers, maps)), dma((2 * layers, maps)),
        dma((layers, 3, nm)), dma((layers, 3, nm)),
        dma((layers, 2, nm)), dma((layers, 2, nm)),
        dma((layers, nm)), dma((layers, nm)),
        dma((layers, line)), dma((layers, line)), dma((layers, line)), dma((layers, line)),
    ]
    return pl.pallas_call(
        functools.partial(block_kernel, sizes),
        out_shape=(
            jax.ShapeDtypeStruct(index.shape, BF16),
            jax.ShapeDtypeStruct((pixels, LANES), F32),
            jax.ShapeDtypeStruct((layers, taps, rows_w, LANES), F32),
            jax.ShapeDtypeStruct((layers, 2, LANES), F32),
        ),
        in_specs=[any_spec] * 7,
        out_specs=(any_spec,) * 4,
        scratch_shapes=scratch,
        compiler_params=pltpu.CompilerParams(
            collective_id=0, has_side_effects=True, vmem_limit_bytes=60 << 20
        ),
    )(x.reshape(pixels, LANES), mask, index, grad, weights, gain, bias)


def local(
    maps, chans,
    input_maps, valid_mask, pool_index, out_grad, conv_weights, weight_first, weight_second,
    norm_gain, norm_bias, norm_first, norm_second,
):
    nm, half_h, half_w, lanes = pool_index.shape
    by_row = (half_h, half_w * nm, lanes)
    pooled, image, weight_grads, norm_grads = block_call(
        maps, chans, input_maps, valid_mask.transpose(1, 0, 2),
        pool_index.transpose(1, 2, 0, 3).reshape(by_row),
        out_grad.transpose(1, 2, 0, 3).reshape(by_row),
        conv_weights, norm_gain, norm_bias,
    )
    pooled = pooled.reshape(half_h, half_w, nm, lanes).transpose(2, 0, 1, 3)
    image_grad = image.reshape(input_maps.shape)
    new_weights, new_weight_first, new_weight_second = adamw_update(
        conv_weights, weight_grads, weight_first, weight_second, rate_conv
    )
    norm_values = jnp.stack([norm_gain, norm_bias], axis=1)
    new_norms, new_norm_first, new_norm_second = adamw_update(
        norm_values, norm_grads, norm_first, norm_second, rate_norm
    )
    return (
        pooled,
        image_grad,
        weight_grads,
        new_weight_first,
        new_weight_second,
        new_weights,
        new_weights.astype(BF16),
        norm_grads,
        new_norm_first,
        new_norm_second,
        new_norms,
    )


def solution(mesh):
    return jax.shard_map(
        functools.partial(local, mesh.shape["maps"], mesh.shape["chan"]),
        mesh=mesh,
        in_specs=(
            P("maps", None, None, "chan"),
            P("maps", None, None),
            P("maps", None, None, "chan"),
            P("maps", None, None, "chan"),
            P(None, None, "maps", "chan"),
            P(None, None, "maps", "chan"),
            P(None, None, "maps", "chan"),
            P(None, "chan"),
            P(None, "chan"),
            P(None, None, "chan"),
            P(None, None, "chan"),
        ),
        out_specs=(
            P("maps", None, None, "chan"),
            P("maps", None, None, "chan"),
            P(None, None, "maps", "chan"),
            P(None, None, "maps", "chan"),
            P(None, None, "maps", "chan"),
            P(None, None, "maps", "chan"),
            P(None, None, "maps", "chan"),
            P(None, None, "chan"),
            P(None, None, "chan"),
            P(None, None, "chan"),
            P(None, None, "chan"),
        ),
        check_vma=False,
    )
```

```python
import functools

import jax
import jax.numpy as jnp
from jax import lax
from jax.experimental import pallas as pl
from jax.experimental.pallas import tpu as pltpu
from jax.sharding import PartitionSpec as P

beta_first = 0.5
beta_second = 0.5
rate_conv = 0.01
rate_norm = 0.2
decay_rate = 0.01
adam_epsilon = 1e-08
norm_epsilon = 1e-05
step_count = 5.0
first_scale = 1.0 / (1.0 - beta_first**step_count)
second_scale = 1.0 / (1.0 - beta_second**step_count)

MESH = pl.DeviceIdType.MESH
F32 = jnp.float32
BF16 = jnp.bfloat16
LANES = 128
PAD = 32


def adamw_update(parameter, gradient, first_moment, second_moment, step_rate):
    first_new = beta_first * first_moment + (1.0 - beta_first) * gradient
    second_new = beta_second * second_moment + (1.0 - beta_second) * gradient * gradient
    step = first_new * first_scale / (jnp.sqrt(second_new * second_scale) + adam_epsilon)
    return (parameter - step_rate * (step + decay_rate * parameter), first_new, second_new)


def steps(low, high, body):
    if high - low <= 8:
        for index in range(low, high):
            body(index)
    else:
        pl.loop(low, high)(body)


scope = jax.named_scope


def run(tasks, amount=None):
    for _ in range(len(tasks) if amount is None else min(amount, len(tasks))):
        tasks.pop(0)()


def tile8(values):
    rows = values.shape[0]
    return jnp.sum(values.reshape(rows // 8, 8, LANES), axis=0)


def block_kernel(
    sizes,
    x_hbm, mask_hbm, index_hbm, grad_hbm, weight_hbm, gain_hbm, bias_hbm,
    first_hbm, second_hbm, norm_first_hbm, norm_second_hbm,
    pooled_ref, back, wgrad_ref, wfirst_ref, wsecond_ref, wnew_ref, wcopy_ref,
    ngrad_ref, nfirst_ref, nsecond_ref, nnew_ref,
    x_in, mask_in, index_in, grad_in, weight_in, gain_in, bias_in,
    first_in, second_in, norm_first_in, norm_second_in,
    mask_ref, wcat, act, raw, scale_ref, prod, conv, normed, slope, result_ref, spread, pool32, zpad, dcat,
    grad_w, part, stat, pair_out, pair_in, far_out, far_in,
    gx_out, gx_in, gz_out, gz_in, total_w,
    in_sem,
    w_s, wz_r, wx_r, st_s, st_r, ag_s, ag_r, sc_s, sc_r, pr_s, pr_r, fr_s, fr_r,
    gx_s, gx_r, gz_s, gz_r,
):
    maps, chans, layers, taps, nm, height, width = sizes
    line = maps // 2
    m = lax.axis_index("maps")
    c = lax.axis_index("chan")
    a = m // 2
    b = m % 2
    core = c + 1 - 2 * (c % 2)
    far = lax.rem(c + 2, 4)
    across = core + 2 - 4 * (core // 2)
    map_rows = height * width
    pixels = nm * map_rows
    rows_w = wcat.shape[1]
    wide = taps * LANES
    chunk = 6 * width
    chunks = pixels // chunk
    per_map = map_rows // chunk

    def rows_of(i):
        return pl.ds(pl.multiple_of(i * chunk, 16), chunk)

    def padded_rows(i, shift):
        n = i // per_map
        return n, pl.ds(pl.multiple_of((i - n * per_map) * chunk, 8) + (PAD + shift), chunk)

    def remote(src, dst, ssem, rsem, dev):
        return pltpu.make_async_remote_copy(
            src_ref=src, dst_ref=dst, send_sem=ssem, recv_sem=rsem,
            device_id=dev, device_id_type=MESH,
        )

    loads = []
    for i, (src, dst) in enumerate(
        (
            (weight_hbm, weight_in), (x_hbm, x_in), (mask_hbm, mask_in),
            (index_hbm, index_in), (grad_hbm, grad_in), (gain_hbm, gain_in), (bias_hbm, bias_in),
            (first_hbm, first_in), (second_hbm, second_in),
            (norm_first_hbm, norm_first_in), (norm_second_hbm, norm_second_in),
        )
    ):
        cp = pltpu.make_async_copy(src, dst, in_sem.at[i])
        cp.start()
        loads.append(cp)

    barrier = pltpu.get_barrier_semaphore()

    def greet(d):
        peer = lax.rem(m + d, maps)
        pl.semaphore_signal(barrier, inc=1, device_id=(peer, c), device_id_type=MESH)

    steps(1, maps, greet)
    for other in (core, far, across):
        pl.semaphore_signal(barrier, inc=1, device_id=(m, other), device_id_type=MESH)

    loads[0].wait()
    for l in range(layers):
        for t in range(taps):
            wcat[l * maps + m, :, t * LANES : (t + 1) * LANES] = weight_in[l, t].astype(BF16)

    pl.semaphore_wait(barrier, maps + 2)

    pieces = wz_r.shape[2]
    piece_rows = rows_w // pieces
    right = (jnp.minimum(m + 2, maps - 1), c)
    left = (jnp.maximum(m - 2, 0), c)
    beside = (m + 1 - 2 * b, c)

    def weight_view(l, slot, g):
        return wcat.at[l * maps + slot, pl.ds(g * piece_rows, piece_rows)]

    def along(l, z, g, dev):
        view = weight_view(l, z * 2 + b, g)
        return remote(view, view, w_s.at[l, 0], wz_r.at[l, z, g], dev)

    def aside(l, z, g):
        view = weight_view(l, z * 2 + b, g)
        return remote(view, view, w_s.at[l, 1], wx_r.at[l], beside)

    def shards_of(l, count, place):
        view = wcat.at[pl.ds(0, count)]
        return remote(view, view, w_s.at[l, place], wx_r.at[l], beside)

    def gather_own(l):
        for g in range(pieces):
            pl.when(a + 1 < line)(lambda: along(l, a, g, right).start())
            pl.when(a > 0)(lambda: along(l, a, g, left).start())
            aside(l, a, g).start()

    def gather_step(l, s, g):
        def piece(cond, z, onward_cond, onward):
            @pl.when(cond)
            def _():
                along(l, z, g, onward).wait_recv()
                pl.when(onward_cond)(lambda: along(l, z, g, onward).start())
                aside(l, z, g).start()

        piece(a >= s, jnp.maximum(a - s, 0), a + 1 < line, right)
        piece(a + s < line, jnp.minimum(a + s, line - 1), a > 0, left)

    def gather_tasks(l):
        if line <= 8:
            return [
                functools.partial(gather_step, l, s, g)
                for s in range(1, line)
                for g in range(pieces)
            ]

        def everything():
            def go(s):
                for g in range(pieces):
                    gather_step(l, s, g)

            steps(1, line, go)

        return [everything]

    def gather_finish(l):
        shards_of(l, line, 1).wait_recv()

    def gather_drain(l):
        shards_of(l, line, 1).wait_send()
        inner = jnp.logical_and(a > 0, a + 1 < line)
        pl.when(inner)(lambda: shards_of(l, line + 1, 0).wait_send())
        pl.when(jnp.logical_not(inner))(lambda: shards_of(l, 1, 0).wait_send())

    def stat_send(e):
        def go(d):
            peer = lax.rem(m + d, maps)
            view = stat.at[e, m]
            remote(view, view, st_s.at[e], st_r.at[e], (peer, c)).start()

        steps(1, maps, go)

    def stat_all(e):
        view = stat.at[e, pl.ds(0, maps - 1)]
        return remote(view, view, st_s.at[e], st_r.at[e], beside)

    def stat_wait(e):
        stat_all(e).wait_recv()

    def stat_drain(e):
        stat_all(e).wait_send()

    lane_own = pl.ds(pl.multiple_of(c * LANES, LANES), LANES)

    def lanes_of(owner):
        return pl.ds(pl.multiple_of(owner * LANES, LANES), LANES)

    def act_copy(l, n, owner, dev, place):
        rows = pl.ds(n * map_rows, map_rows)
        view = act.at[0, rows, lanes_of(owner)] if l == 0 else raw.at[l - 1, owner, rows]
        return remote(view, view, ag_s.at[l], ag_r.at[l, place], dev)

    def act_blocks(l, count, place):
        view = act.at[0, :, pl.ds(0, count * LANES)] if l == 0 else raw.at[l - 1, pl.ds(0, count)]
        return remote(view, view, ag_s.at[l], ag_r.at[l, place], (m, core))

    def act_send(l, n):
        act_copy(l, n, c, (m, far), n).start()
        act_copy(l, n, c, (m, core), nm).start()

    def act_forward(l, n):
        act_copy(l, n, far, (m, far), n).wait_recv()
        act_copy(l, n, far, (m, core), nm + 1).start()

    def act_near(l):
        act_blocks(l, 1, nm).wait_recv()

    def act_across(l):
        act_blocks(l, 1, nm + 1).wait_recv()

    def act_drain(l):
        act_blocks(l, 3, 0).wait_send()

    def scale_copy(l, owner, dev, ssem):
        view = scale_ref.at[l, owner]
        return remote(view, view, ssem, sc_r.at[l, owner], dev)

    def scale_send(l):
        for other in (core, far, across):
            scale_copy(l, c, (m, other), sc_s.at[l]).start()

    def scale_wait(l, owner):
        scale_copy(l, owner, (m, core), sc_s.at[l]).wait_recv()

    def scale_drain(l):
        view = scale_ref.at[l, pl.ds(0, 3)]
        remote(view, view, sc_s.at[l], sc_r.at[l, core], (m, core)).wait_send()

    gather_own(0)

    loads[2].wait()
    col_of = lax.broadcasted_iota(jnp.int32, (width, width), 0)
    diagonal = col_of == lax.broadcasted_iota(jnp.int32, (width, width), 1)
    for n in range(nm):

        @pl.loop(0, height)
        def _(h):
            line_n = jnp.broadcast_to(mask_in[h, n : n + 1, :].astype(F32), (width, width))
            r = pl.ds(pl.multiple_of(n * map_rows + h * width, 8), width)
            conv[r, 0:width] = jnp.where(diagonal, line_n, 0.0)

    mask_ref[...] = jnp.dot(
        conv[:, 0:width].astype(BF16), jnp.ones((width, LANES), BF16), preferred_element_type=F32
    )
    loads[1].wait()

    @pl.loop(0, chunks)
    def _(i):
        r = rows_of(i)
        act[0, r, lane_own] = (x_in[r, :].astype(F32) * mask_ref[r, :]).astype(BF16)

    for n in range(nm):
        act_send(0, n)

    for n in range(nm):
        for i in range(3):
            for j in range(3):
                prod[i, j, n, 0:PAD, :] = jnp.zeros((PAD, LANES), F32)
                prod[i, j, n, PAD + map_rows :, :] = jnp.zeros((PAD, LANES), F32)
        zpad[n, 0:PAD, :] = jnp.zeros((PAD, LANES), F32)
        zpad[n, PAD + map_rows :, :] = jnp.zeros((PAD, LANES), F32)

    col_chunk = lax.broadcasted_iota(jnp.int32, (6, width, LANES), 1).reshape(chunk, LANES)
    has_left = jnp.where(col_chunk > 0, 1.0, 0.0)
    has_right = jnp.where(col_chunk < width - 1, 1.0, 0.0)

    loads[3].wait()
    loads[4].wait()
    half_h, half_w = height // 2, width // 2

    @pl.loop(0, half_h)
    def _(h):
        pool32[...] = grad_in[h].astype(F32)
        for n in range(nm):
            pick = pl.ds(n, half_w, stride=nm)
            kept = index_in[h, pick, :]
            value = pool32[pick, :]
            base = n * map_rows + 2 * h * width
            for r in range(2):
                for s in range(2):
                    spread[pl.ds(base + r * width + s, half_w, stride=2), :] = jnp.where(
                        kept == 2 * r + s, value, 0.0
                    )

    tasks = gather_tasks(0)
    with scope("gather0"):
        run(tasks)
    for n in range(nm):
        act_forward(0, n)
    with scope("gather0_end"):
        gather_finish(0)
    act_near(0)
    act_across(0)
    for cp in loads[5:]:
        cp.wait()

    for l in range(layers):
        tasks = []
        if l + 1 < layers:
            gather_own(l + 1)
            tasks = gather_tasks(l + 1)

        @pl.loop(0, 3)
        def _(i):
            cols = pl.ds(pl.multiple_of(i * (3 * LANES), LANES), 3 * LANES)
            w = wcat[l * maps : (l + 1) * maps, :, cols].reshape(maps * rows_w, 3 * LANES)
            for n in range(nm):
                out = jnp.dot(
                    act[l, pl.ds(n * map_rows, map_rows), :], w, preferred_element_type=F32
                )
                for j in range(3):
                    prod[i, j, n, PAD : PAD + map_rows, :] = out[:, j * LANES : (j + 1) * LANES]

        def conv_chunk(i, carry):
            total, count = carry
            r = rows_of(i)
            value = None
            for j in range(3):
                side = None
                for k in range(3):
                    n, pr = padded_rows(i, width * (k - 1) + (j - 1))
                    term = prod[k, j, n, pr, :]
                    side = term if side is None else side + term
                if j == 0:
                    side = side * has_left
                if j == 2:
                    side = side * has_right
                value = side if value is None else value + side
            conv[r, :] = value
            valid = mask_ref[r, :]
            return total + tile8(value * valid), count + tile8(valid)

        zero8 = jnp.zeros((8, LANES), F32)
        total, count = lax.fori_loop(0, chunks, conv_chunk, (zero8, zero8))
        total = jnp.sum(total, axis=0, keepdims=True)
        count = jnp.sum(count, axis=0, keepdims=True)
        mean = total / jnp.maximum(count, 1.0)

        def dev_chunk(i, carry):
            r = rows_of(i)
            delta = conv[r, :] - mean
            if l + 1 < layers:
                raw[l, c, r, :] = delta.astype(BF16)
            return carry + tile8(delta * delta * mask_ref[r, :])

        spread_sum = zero8
        for n in range(nm):
            spread_sum = lax.fori_loop(n * per_map, (n + 1) * per_map, dev_chunk, spread_sum)
            if l + 1 < layers:
                act_send(l + 1, n)
        spread_sum = jnp.sum(spread_sum, axis=0, keepdims=True)
        stat[l, m] = jnp.concatenate(
            [total, spread_sum, count, mean, jnp.zeros((4, LANES), F32)], axis=0
        )
        stat_send(l)
        with scope("gather_a"):
            run(tasks, pieces)
        with scope("stat_wait"):
            stat_wait(l)

        def add_totals(s, carry):
            block = stat[l, s]
            return carry[0] + block[0:1, :], carry[1] + block[2:3, :]

        zero1 = jnp.zeros((1, LANES), F32)
        total, count = lax.fori_loop(0, maps, add_totals, (zero1, zero1))
        center = total / count

        def add_spread(s, carry):
            block = stat[l, s]
            delta = block[3:4, :] - center
            return carry + block[1:2, :] + block[2:3, :] * delta * delta

        variance = lax.fori_loop(0, maps, add_spread, zero1) / count
        inv_std = lax.rsqrt(variance + norm_epsilon)
        gain = gain_in[l : l + 1, :]
        bias = bias_in[l : l + 1, :]
        if l == 0:
            count_all = count
            scales = []
        scales.append(gain * inv_std)

        if l + 1 < layers:
            factor = gain * inv_std
            scale_ref[l, c] = jnp.concatenate(
                [factor, bias + factor * (mean - center), jnp.zeros((6, LANES), F32)], axis=0
            )
            scale_send(l)

        @pl.loop(0, chunks)
        def _(i):
            r = rows_of(i)
            unit = (conv[r, :] - center) * inv_std
            pre = gain * unit + bias
            sigma = 1.0 / (1.0 + jnp.exp(-pre))
            valid = mask_ref[r, :]
            result = pre * sigma * valid
            normed[l, r, :] = unit
            slope[l, r, :] = sigma * (1.0 + pre * (1.0 - sigma)) * valid
            if l + 1 < layers:
                act[l + 1, r, lane_own] = result.astype(BF16)
            else:
                result_ref[r, :] = result

        def activate(owner, first, last):
            pair = scale_ref[l, owner]
            factor, offset = pair[0:1, :], pair[1:2, :]
            lanes = lanes_of(owner)

            @pl.loop(first * per_map, last * per_map)
            def _(i):
                r = rows_of(i)
                pre = factor * raw[l, owner, r, :].astype(F32) + offset
                result = pre / (1.0 + jnp.exp(-pre)) * mask_ref[r, :]
                act[l + 1, r, lanes] = result.astype(BF16)

        if l + 1 < layers:
            with scope("act_near"):
                act_near(l + 1)
                scale_wait(l, core)
                activate(core, 0, nm)
            with scope("gather_b"):
                run(tasks, 1)
            with scope("act_far"):
                for n in range(nm):
                    act_forward(l + 1, n)
                    if n == 0:
                        scale_wait(l, far)
                    activate(far, n, n + 1)
            with scope("gather_c"):
                run(tasks, 2)
            with scope("act_across"):
                act_across(l + 1)
                scale_wait(l, across)
                activate(across, 0, nm)
            with scope("gather_d"):
                run(tasks)
            with scope("gather_end"):
                gather_finish(l + 1)

    def pool():
        @pl.loop(0, half_h)
        def _(h):
            for n in range(nm):
                pick = pl.ds(n, half_w, stride=nm)
                kept = index_in[h, pick, :]
                base = n * map_rows + 2 * h * width
                total = jnp.zeros((half_w, LANES), F32)
                for r in range(2):
                    for s in range(2):
                        total = total + jnp.where(
                            kept == 2 * r + s,
                            result_ref[pl.ds(base + r * width + s, half_w, stride=2), :],
                            0.0,
                        )
                pool32[pick, :] = total
            pooled_ref[h] = pool32[...].astype(BF16)

    def far_first(body):
        def go(e):
            d = line - e

            @pl.when(a + d < line)
            def _():
                body(jnp.minimum(a + d, line - 1))

            @pl.when(a >= d)
            def _():
                body(jnp.maximum(a - d, 0))

        steps(1, line, go)
        body(a)

    def part_of(g):
        return pl.ds(g * piece_rows, piece_rows)

    def gx_copy(l, z, g):
        return remote(
            gx_out.at[l, z, part_of(g)], gx_in.at[l, z, part_of(g)],
            gx_s.at[l], gx_r.at[l, z, g], beside,
        )

    def gz_copy(l, z, g, slot, dev):
        return remote(
            gz_out.at[l, z, part_of(g)], gz_in.at[l, slot, part_of(g)],
            gz_s.at[l], gz_r.at[l, slot, g], dev,
        )

    def shard(l, slot, g):
        first = pl.multiple_of(slot * rows_w, 8) + g * piece_rows
        return grad_w[l, pl.ds(first, piece_rows), :]

    tile = 2 * rows_w
    fine = tile % LANES == 0

    def kernel_grad(l, first, amount):
        rows = pl.ds(pl.multiple_of(first, LANES), amount)
        grad_w[l, rows, :] = lax.dot_general(
            act[l, :, rows], dcat[...], (((0,), (0,)), ((), ())), preferred_element_type=F32
        )

    def kernel_grads(l, send):
        if not fine:
            coarse = (maps * rows_w) // 4
            pl.loop(0, 4)(lambda i: kernel_grad(l, i * coarse, coarse))

        def go(z):
            if fine:
                kernel_grad(l, z * tile, tile)
            for g in range(pieces):
                gx_out[l, z, part_of(g)] = shard(l, z * 2 + 1 - b, g).astype(BF16)
                if send:
                    gx_copy(l, z, g).start()

        far_first(go)

    def scatter_x(l):
        def go(z):
            for g in range(pieces):
                gx_copy(l, z, g).start()

        far_first(go)

    def pair_sum(l, z, g):
        gx_copy(l, z, g).wait_recv()
        return shard(l, z * 2 + b, g) + gx_in[l, z, part_of(g)].astype(F32)

    def onward(l, z, g, has_more, dev, slot):
        @pl.when(has_more)
        def _():
            gz_copy(l, z, g, z, dev).wait_recv()
            gz_out[l, z, part_of(g)] = (
                pair_sum(l, z, g) + gz_in[l, z, part_of(g)].astype(F32)
            ).astype(BF16)

        @pl.when(jnp.logical_not(has_more))
        def _():
            gz_out[l, z, part_of(g)] = pair_sum(l, z, g).astype(BF16)

        gz_copy(l, z, g, slot, dev).start()

    def scatter_step(l, d, g):
        @pl.when(a + d < line)
        def _():
            z = jnp.minimum(a + d, line - 1)
            onward(l, z, g, a > 0, right, z)

        @pl.when(a >= d)
        def _():
            z = jnp.maximum(a - d, 0)
            onward(l, z, g, a + 1 < line, left, jnp.where(z == a - 1, line, z))

    def scatter_own(l, g):
        r = part_of(g)
        total_w[r, :] = pair_sum(l, a, g)

        @pl.when(a > 0)
        def _():
            gz_copy(l, a, g, a, left).wait_recv()
            total_w[r, :] += gz_in[l, a, r].astype(F32)

        @pl.when(a + 1 < line)
        def _():
            gz_copy(l, a, g, line, right).wait_recv()
            total_w[r, :] += gz_in[l, line, r].astype(F32)

        for t in range(taps):
            gradient = total_w[r, t * LANES : (t + 1) * LANES]
            new, first, second = adamw_update(
                weight_in[l, t, r], gradient, first_in[l, t, r], second_in[l, t, r], rate_conv
            )
            wgrad_ref[l, t, r] = gradient
            wfirst_ref[l, t, r] = first
            wsecond_ref[l, t, r] = second
            wnew_ref[l, t, r] = new
            wcopy_ref[l, t, r] = new.astype(BF16)

    def scatter_tasks(l):
        owns = [functools.partial(scatter_own, l, g) for g in range(pieces)]
        if line <= 8:
            return [
                functools.partial(scatter_step, l, line - e, g)
                for e in range(1, line)
                for g in range(pieces)
            ], owns

        def everything():
            def go(e):
                for g in range(pieces):
                    scatter_step(l, line - e, g)

            steps(1, line, go)

        return [everything], owns

    def scatter_drain(l):
        remote(gx_out.at[l], gx_in.at[l], gx_s.at[l], gx_r.at[l, 0, 0], beside).wait_send()
        view = pl.ds(0, line - 1)
        remote(
            gz_out.at[l, view], gz_in.at[l, view], gz_s.at[l], gz_r.at[l, 0, 0], beside
        ).wait_send()

    def layer_drain(l):
        stat_drain(layers + l)
        remote(pair_out.at[l], pair_in.at[l], pr_s.at[l], pr_r.at[l, 0], (m, core)).wait_send()
        remote(far_out.at[l], far_in.at[l], fr_s.at[l], fr_r.at[l, 0], (m, far)).wait_send()

    half = 2 * LANES
    own_half = (c // 2) * half
    other_half = half - own_half
    lane_in_half = pl.ds(pl.multiple_of((c % 2) * LANES, LANES), LANES)
    lane_out_half = pl.ds(pl.multiple_of((1 - c % 2) * LANES, LANES), LANES)

    def pair_copy(l, h, n):
        return remote(
            pair_out.at[l, h, pl.ds(n * map_rows, map_rows), :],
            pair_in.at[l, h, pl.ds(n * map_rows, map_rows), :],
            pr_s.at[l], pr_r.at[l, n if h == 0 else nm], (m, core),
        )

    def far_copy(l, n):
        return remote(
            far_out.at[l, pl.ds(n * map_rows, map_rows), :],
            far_in.at[l, pl.ds(n * map_rows, map_rows), :],
            fr_s.at[l], fr_r.at[l, n], (m, far),
        )

    todo, owns = {}, {}
    for l in reversed(range(layers)):
        e = layers + l
        source = spread if l == layers - 1 else back

        def slope_chunk(i, carry):
            r = rows_of(i)
            value = source[r, :] * slope[l, r, :]
            conv[r, :] = value
            return carry[0] + tile8(value * normed[l, r, :]), carry[1] + tile8(value)

        zero8 = jnp.zeros((8, LANES), F32)
        gain_sum, bias_sum = lax.fori_loop(0, chunks, slope_chunk, (zero8, zero8))
        stat[e, m] = jnp.concatenate(
            [
                jnp.sum(gain_sum, axis=0, keepdims=True),
                jnp.sum(bias_sum, axis=0, keepdims=True),
                jnp.zeros((6, LANES), F32),
            ],
            axis=0,
        )
        stat_send(e)
        if l + 1 < layers:
            scatter_x(l + 1)
        else:
            pool()
        if l + 1 < layers:
            todo[l + 1], owns[l + 1] = scatter_tasks(l + 1)
        if l + 2 < layers:
            with scope("scatter_last"):
                run(todo[l + 2])
        with scope("stat_wait_back"):
            stat_wait(e)

        def add_sums(s, carry):
            return carry + stat[e, s]

        sums = lax.fori_loop(0, maps, add_sums, jnp.zeros((8, LANES), F32))
        ngrad_ref[l] = sums[0:2, :]
        gain_grad = sums[0:1, :]
        bias_grad = sums[1:2, :]
        scale = scales[l]

        def conv_grad(n):
            @pl.loop(n * per_map, (n + 1) * per_map)
            def _(i):
                r = rows_of(i)
                value = (
                    mask_ref[r, :]
                    * scale
                    * (conv[r, :] - (bias_grad + normed[l, r, :] * gain_grad) / count_all)
                )
                pr = pl.ds(pl.multiple_of((i - n * per_map) * chunk, 16) + PAD, chunk)
                zpad[n, pr, :] = value

            @pl.loop(n * per_map, (n + 1) * per_map)
            def _(i):
                r = rows_of(i)
                for k in range(3):
                    for j in range(3):
                        shift = PAD - (width * (k - 1) + (j - 1))
                        pr = pl.ds(pl.multiple_of((i - n * per_map) * chunk, 16) + shift, chunk)
                        term = zpad[n, pr, :]
                        if j == 0:
                            term = term * has_right
                        if j == 2:
                            term = term * has_left
                        t = 3 * k + j
                        dcat[r, t * LANES : (t + 1) * LANES] = term.astype(BF16)

        def input_grad(h, n):
            start = other_half if h == 0 else own_half
            slots = maps // 2
            w = wcat[pl.ds(l * maps + (start // half) * slots, slots), :, :].reshape(half, wide)
            r = pl.ds(n * map_rows, map_rows)
            part[h, r, :] = lax.dot_general(
                dcat[r, :], w, (((1,), (1,)), ((), ())), preferred_element_type=F32
            )
            pair_out[l, h, r, :] = part[h, r, lane_out_half].astype(BF16)
            pair_copy(l, h, n).start()

        def to_far(n):
            r = pl.ds(n * map_rows, map_rows)
            pair_copy(l, 0, n).wait_recv()
            far_out[l, r, :] = (
                part[0, r, lane_in_half] + pair_in[l, 0, r, :].astype(F32)
            ).astype(BF16)
            far_copy(l, n).start()

        if l > 0:
            for n in range(nm):
                with scope("conv_grad"):
                    conv_grad(n)
                with scope("input_grad"):
                    input_grad(0, n)
                if n > 0:
                    with scope("to_far"):
                        to_far(n - 1)
            for n in range(nm):
                with scope("input_grad"):
                    input_grad(1, n)
                if n == 0:
                    with scope("to_far"):
                        to_far(nm - 1)
                    if l + 1 < layers:
                        with scope("scatter_step"):
                            run(todo[l + 1], pieces)
            with scope("kernel_grad"):
                kernel_grads(l, False)
            if l + 1 < layers:
                with scope("scatter_step"):
                    run(todo[l + 1], pieces)
            with scope("drain"):
                if l + 1 == layers:
                    for k in range(layers):
                        gather_drain(k)
                        act_drain(k)
                        stat_drain(k)
                        if k + 1 < layers:
                            scale_drain(k)
                else:
                    layer_drain(l + 1)
        else:
            for n in range(nm):
                with scope("conv_grad"):
                    conv_grad(n)
            with scope("scatter_1a"):
                run(todo[1], pieces)
            with scope("kernel_grad"):
                kernel_grads(0, True)
            todo[0], owns[0] = scatter_tasks(0)
            with scope("scatter_1b"):
                run(todo[1], pieces)
            for n in range(nm):
                with scope("input_grad"):
                    input_grad(0, n)
            with scope("scatter_1c"):
                run(todo[1])
            with scope("to_far"):
                for n in range(nm):
                    to_far(n)
            with scope("scatter_0a"):
                run(todo[0], pieces)
            for n in range(nm):
                with scope("input_grad"):
                    input_grad(1, n)
            with scope("owns"):
                for k in range(layers - 1, 0, -1):
                    run(owns[k])
            with scope("scatter_0b"):
                run(todo[0], pieces)
            with scope("drain"):
                for k in range(1, layers):
                    scatter_drain(k)
                layer_drain(1)

        for n in range(nm):
            r = pl.ds(n * map_rows, map_rows)
            with scope("far_wait"):
                if n == 0:
                    remote(
                        pair_out.at[l, 1], pair_in.at[l, 1], pr_s.at[l], pr_r.at[l, nm], (m, core)
                    ).wait_recv()
                far_copy(l, n).wait_recv()

            @pl.loop(n * per_map, (n + 1) * per_map)
            def _(i):
                r = rows_of(i)
                value = (
                    part[1, r, lane_in_half]
                    + pair_in[l, 1, r, :].astype(F32)
                    + far_in[l, r, :].astype(F32)
                )
                if l == 0:
                    value = value * mask_ref[r, :]
                back[r, :] = value

    with scope("norms"):
        for values, place in ((gain_in, 0), (bias_in, 1)):
            new, first, second = adamw_update(
                values[...], ngrad_ref[:, place, :], norm_first_in[:, place, :],
                norm_second_in[:, place, :], rate_norm,
            )
            nfirst_ref[:, place, :] = first
            nsecond_ref[:, place, :] = second
            nnew_ref[:, place, :] = new
    with scope("scatter_end"):
        run(todo[0])
    with scope("owns"):
        run(owns[0])

    with scope("drain_end"):
        layer_drain(0)
        scatter_drain(0)


def store_kernel(count, *refs):
    copies = [
        pltpu.make_async_copy(refs[i], refs[count + i], refs[2 * count].at[i]) for i in range(count)
    ]
    for cp in copies:
        cp.start()
    for cp in copies:
        cp.wait()


def store_results(results):
    any_spec = pl.BlockSpec(memory_space=pl.ANY)
    count = len(results)
    return pl.pallas_call(
        functools.partial(store_kernel, count),
        out_shape=tuple(jax.ShapeDtypeStruct(r.shape, r.dtype) for r in results),
        in_specs=[any_spec] * count,
        out_specs=(any_spec,) * count,
        scratch_shapes=[pltpu.SemaphoreType.DMA((count,))],
        compiler_params=pltpu.CompilerParams(vmem_limit_bytes=1 << 20),
    )(*results)


def block_call(maps, chans, x, mask, index, grad, weights, gain, bias, *moments):
    nm, height, width, lanes = x.shape
    layers, taps, rows_w, _ = weights.shape
    pixels = nm * height * width
    line = maps // 2
    wide = taps * LANES
    channels = chans * LANES
    map_rows = height * width
    sizes = (maps, chans, layers, taps, nm, height, width)
    pieces = 2 if rows_w % 32 == 0 else 1
    vm = pltpu.VMEM
    dma = pltpu.SemaphoreType.DMA
    hbm = pl.BlockSpec(memory_space=pltpu.HBM)
    scratch = [
        vm((pixels, LANES), BF16), vm(mask.shape, jnp.int32), vm(index.shape, jnp.int32),
        vm(grad.shape, BF16), vm(weights.shape, F32), vm(gain.shape, F32), vm(bias.shape, F32),
        *(vm(v.shape, F32) for v in moments),
        vm((pixels, LANES), F32),
        vm((layers * maps, rows_w, wide), BF16),
        vm((layers, pixels, channels), BF16),
        vm((layers - 1, chans, pixels, LANES), BF16),
        vm((layers - 1, chans, 8, LANES), F32),
        vm((3, 3, nm, map_rows + 2 * PAD, LANES), F32),
        vm((pixels, LANES), F32),
        vm((layers, pixels, LANES), F32),
        vm((layers, pixels, LANES), F32),
        vm((pixels, LANES), F32),
        vm((pixels, LANES), F32),
        vm((nm * (width // 2), LANES), F32),
        vm((nm, map_rows + 2 * PAD, LANES), F32),
        vm((pixels, wide), BF16),
        vm((layers, channels, wide), F32),
        vm((2, pixels, 2 * LANES), F32),
        vm((2 * layers, maps, 8, LANES), F32),
        vm((layers, 2, pixels, LANES), BF16), vm((layers, 2, pixels, LANES), BF16),
        vm((layers, pixels, LANES), BF16), vm((layers, pixels, LANES), BF16),
        vm((layers, line, rows_w, wide), BF16), vm((layers, line, rows_w, wide), BF16),
        vm((layers, line, rows_w, wide), BF16), vm((layers, line + 1, rows_w, wide), BF16),
        vm((rows_w, wide), F32),
        dma((11,)),
        dma((layers, 2)), dma((layers, line, pieces)), dma((layers,)),
        dma((2 * layers,)), dma((2 * layers,)),
        dma((layers,)), dma((layers, nm + 2)),
        dma((layers - 1,)), dma((layers - 1, chans)),
        dma((layers,)), dma((layers, nm + 1)),
        dma((layers,)), dma((layers, nm)),
        dma((layers,)), dma((layers, line, pieces)),
        dma((layers,)), dma((layers, line + 1, pieces)),
    ]
    arrays = (
        [(index.shape, BF16), ((pixels, LANES), F32)]
        + [(weights.shape, F32)] * 4
        + [(weights.shape, BF16)]
        + [((layers, 2, LANES), F32)] * 4
    )
    return pl.pallas_call(
        functools.partial(block_kernel, sizes),
        out_shape=tuple(jax.ShapeDtypeStruct(*kind) for kind in arrays),
        in_specs=[hbm] * 11,
        out_specs=(pl.BlockSpec(memory_space=pltpu.VMEM),) * len(arrays),
        scratch_shapes=scratch,
        compiler_params=pltpu.CompilerParams(
            collective_id=0, has_side_effects=True, vmem_limit_bytes=48 << 20
        ),
    )(*(
        pltpu.with_memory_space_constraint(v, pltpu.HBM)
        for v in (x.reshape(pixels, LANES), mask, index, grad, weights, gain, bias, *moments)
    ))


def local(
    maps, chans,
    input_maps, valid_mask, pool_index, out_grad, conv_weights, weight_first, weight_second,
    norm_gain, norm_bias, norm_first, norm_second,
):
    nm, half_h, half_w, lanes = pool_index.shape
    by_row = (half_h, half_w * nm, lanes)
    pooled, image, *updates = store_results(
        block_call(
            maps, chans, input_maps, valid_mask.transpose(1, 0, 2),
            pool_index.transpose(1, 2, 0, 3).reshape(by_row),
            out_grad.transpose(1, 2, 0, 3).reshape(by_row),
            conv_weights, norm_gain, norm_bias, weight_first, weight_second, norm_first, norm_second,
        )
    )
    pooled = pooled.reshape(half_h, half_w, nm, lanes).transpose(2, 0, 1, 3)
    return (pooled, image.reshape(input_maps.shape), *updates)


def solution(mesh):
    return jax.shard_map(
        functools.partial(local, mesh.shape["maps"], mesh.shape["chan"]),
        mesh=mesh,
        in_specs=(
            P("maps", None, None, "chan"),
            P("maps", None, None),
            P("maps", None, None, "chan"),
            P("maps", None, None, "chan"),
            P(None, None, "maps", "chan"),
            P(None, None, "maps", "chan"),
            P(None, None, "maps", "chan"),
            P(None, "chan"),
            P(None, "chan"),
            P(None, None, "chan"),
            P(None, None, "chan"),
        ),
        out_specs=(
            P("maps", None, None, "chan"),
            P("maps", None, None, "chan"),
            P(None, None, "maps", "chan"),
            P(None, None, "maps", "chan"),
            P(None, None, "maps", "chan"),
            P(None, None, "maps", "chan"),
            P(None, None, "maps", "chan"),
            P(None, None, "chan"),
            P(None, None, "chan"),
            P(None, None, "chan"),
            P(None, None, "chan"),
        ),
        check_vma=False,
    )
```

```python
import functools

import jax
import jax.numpy as jnp
from jax import lax
from jax.experimental import pallas as pl
from jax.experimental.pallas import tpu as pltpu
from jax.sharding import PartitionSpec as P

beta_first = 0.5
beta_second = 0.5
rate_conv = 0.01
rate_norm = 0.2
decay_rate = 0.01
adam_epsilon = 1e-08
norm_epsilon = 1e-05
step_count = 5.0
first_scale = 1.0 / (1.0 - beta_first**step_count)
second_scale = 1.0 / (1.0 - beta_second**step_count)

MESH = pl.DeviceIdType.MESH
F32 = jnp.float32
BF16 = jnp.bfloat16
LANES = 128
PAD = 32


def adamw_update(parameter, gradient, first_moment, second_moment, step_rate):
    first_new = beta_first * first_moment + (1.0 - beta_first) * gradient
    second_new = beta_second * second_moment + (1.0 - beta_second) * gradient * gradient
    step = first_new * first_scale / (jnp.sqrt(second_new * second_scale) + adam_epsilon)
    return (parameter - step_rate * (step + decay_rate * parameter), first_new, second_new)


def steps(low, high, body):
    if high - low <= 8:
        for index in range(low, high):
            body(index)
    else:
        pl.loop(low, high)(body)


scope = jax.named_scope


def run(tasks, amount=None):
    for _ in range(len(tasks) if amount is None else min(amount, len(tasks))):
        tasks.pop(0)()


def tile8(values):
    rows = values.shape[0]
    return jnp.sum(values.reshape(rows // 8, 8, LANES), axis=0)


def block_kernel(
    sizes,
    x_hbm, mask_hbm, index_hbm, grad_hbm, weight_hbm, gain_hbm, bias_hbm,
    first_hbm, second_hbm, norm_first_hbm, norm_second_hbm,
    pooled_ref, back, wgrad_ref, wfirst_ref, wsecond_ref, wnew_ref, wcopy_ref,
    ngrad_ref, nfirst_ref, nsecond_ref, nnew_ref,
    x_in, mask_in, index_in, grad_in, weight_in, gain_in, bias_in,
    first_in, second_in, norm_first_in, norm_second_in,
    mask_ref, wcat, act, raw, scale_ref, prod, conv, normed, slope, result_ref, spread, pool32, zpad, dcat,
    grad_w, part, stat, pair_out, pair_in, far_out, far_in,
    gx_out, gx_in, gz_out, gz_in, total_w,
    in_sem,
    w_s, wz_r, wx_r, st_s, st_r, ag_s, ag_r, sc_s, sc_r, pr_s, pr_r, fr_s, fr_r,
    gx_s, gx_r, gz_s, gz_r,
):
    maps, chans, layers, taps, nm, height, width = sizes
    line = maps // 2
    m = lax.axis_index("maps")
    c = lax.axis_index("chan")
    a = m // 2
    b = m % 2
    core = c + 1 - 2 * (c % 2)
    far = lax.rem(c + 2, 4)
    across = core + 2 - 4 * (core // 2)
    map_rows = height * width
    pixels = nm * map_rows
    rows_w = wcat.shape[1]
    wide = taps * LANES
    chunk = 6 * width
    chunks = pixels // chunk
    per_map = map_rows // chunk

    def rows_of(i):
        return pl.ds(pl.multiple_of(i * chunk, 16), chunk)

    def padded_rows(i, shift):
        n = i // per_map
        return n, pl.ds(pl.multiple_of((i - n * per_map) * chunk, 8) + (PAD + shift), chunk)

    def remote(src, dst, ssem, rsem, dev):
        return pltpu.make_async_remote_copy(
            src_ref=src, dst_ref=dst, send_sem=ssem, recv_sem=rsem,
            device_id=dev, device_id_type=MESH,
        )

    loads = []
    for i, (src, dst) in enumerate(
        (
            (weight_hbm, weight_in), (x_hbm, x_in), (mask_hbm, mask_in),
            (index_hbm, index_in), (grad_hbm, grad_in), (gain_hbm, gain_in), (bias_hbm, bias_in),
            (first_hbm, first_in), (second_hbm, second_in),
            (norm_first_hbm, norm_first_in), (norm_second_hbm, norm_second_in),
        )
    ):
        cp = pltpu.make_async_copy(src, dst, in_sem.at[i])
        cp.start()
        loads.append(cp)

    barrier = pltpu.get_barrier_semaphore()

    def greet(d):
        peer = lax.rem(m + d, maps)
        pl.semaphore_signal(barrier, inc=1, device_id=(peer, c), device_id_type=MESH)

    steps(1, maps, greet)
    for other in (core, far, across):
        pl.semaphore_signal(barrier, inc=1, device_id=(m, other), device_id_type=MESH)

    with scope("load"):
        loads[0].wait()
    for l in range(layers):
        for t in range(taps):
            wcat[l * maps + m, :, t * LANES : (t + 1) * LANES] = weight_in[l, t].astype(BF16)

    with scope("barrier"):
        pl.semaphore_wait(barrier, maps + 2)

    pieces = wz_r.shape[2]
    piece_rows = rows_w // pieces
    right = (jnp.minimum(m + 2, maps - 1), c)
    left = (jnp.maximum(m - 2, 0), c)
    beside = (m + 1 - 2 * b, c)

    def weight_view(l, slot, g):
        return wcat.at[l * maps + slot, pl.ds(g * piece_rows, piece_rows)]

    def along(l, z, g, dev):
        view = weight_view(l, z * 2 + b, g)
        return remote(view, view, w_s.at[l, 0], wz_r.at[l, z, g], dev)

    def aside(l, z, g):
        view = weight_view(l, z * 2 + b, g)
        return remote(view, view, w_s.at[l, 1], wx_r.at[l], beside)

    def shards_of(l, count, place):
        view = wcat.at[pl.ds(0, count)]
        return remote(view, view, w_s.at[l, place], wx_r.at[l], beside)

    def own_along(l):
        for g in range(pieces):
            pl.when(a + 1 < line)(lambda: along(l, a, g, right).start())
            pl.when(a > 0)(lambda: along(l, a, g, left).start())

    def own_aside(l):
        for g in range(pieces):
            aside(l, a, g).start()

    def own_aside_late(l, late):
        pl.when(c % 2 == late)(lambda: own_aside(l))

    def step_along(l, s, g):
        def piece(cond, z, onward_cond, onward):
            @pl.when(cond)
            def _():
                along(l, z, g, onward).wait_recv()
                pl.when(onward_cond)(lambda: along(l, z, g, onward).start())

        piece(a >= s, jnp.maximum(a - s, 0), a + 1 < line, right)
        piece(a + s < line, jnp.minimum(a + s, line - 1), a > 0, left)

    def step_aside(l, s, g):
        pl.when(a >= s)(lambda: aside(l, jnp.maximum(a - s, 0), g).start())
        pl.when(a + s < line)(lambda: aside(l, jnp.minimum(a + s, line - 1), g).start())

    def step_both(l, s, g):
        step_along(l, s, g)
        step_aside(l, s, g)

    def gather_tasks(step, l):
        if line <= 8:
            return [
                functools.partial(step, l, s, g) for s in range(1, line) for g in range(pieces)
            ]

        def everything():
            def go(s):
                for g in range(pieces):
                    step(l, s, g)

            steps(1, line, go)

        return [everything]

    def gather_finish(l):
        shards_of(l, line, 1).wait_recv()

    def gather_drain(l):
        shards_of(l, line, 1).wait_send()
        inner = jnp.logical_and(a > 0, a + 1 < line)
        pl.when(inner)(lambda: shards_of(l, line + 1, 0).wait_send())
        pl.when(jnp.logical_not(inner))(lambda: shards_of(l, 1, 0).wait_send())

    def stat_send(e):
        def go(d):
            peer = lax.rem(m + d, maps)
            view = stat.at[e, m]
            remote(view, view, st_s.at[e], st_r.at[e], (peer, c)).start()

        steps(1, maps, go)

    def stat_all(e):
        view = stat.at[e, pl.ds(0, maps - 1)]
        return remote(view, view, st_s.at[e], st_r.at[e], beside)

    def stat_wait(e):
        stat_all(e).wait_recv()

    def stat_drain(e):
        stat_all(e).wait_send()

    lane_own = pl.ds(pl.multiple_of(c * LANES, LANES), LANES)

    def lanes_of(owner):
        return pl.ds(pl.multiple_of(owner * LANES, LANES), LANES)

    def act_copy(l, n, owner, dev, place):
        rows = pl.ds(n * map_rows, map_rows)
        view = act.at[0, rows, lanes_of(owner)] if l == 0 else raw.at[l - 1, owner, rows]
        return remote(view, view, ag_s.at[l], ag_r.at[l, place], dev)

    def act_blocks(l, count, place):
        view = act.at[0, :, pl.ds(0, count * LANES)] if l == 0 else raw.at[l - 1, pl.ds(0, count)]
        return remote(view, view, ag_s.at[l], ag_r.at[l, place], (m, core))

    def act_send(l, n):
        act_copy(l, n, c, (m, far), n).start()
        act_copy(l, n, c, (m, core), nm).start()

    def act_forward(l, n):
        act_copy(l, n, far, (m, far), n).wait_recv()
        act_copy(l, n, far, (m, core), nm + 1).start()

    def act_near(l):
        act_blocks(l, 1, nm).wait_recv()

    def act_across(l):
        act_blocks(l, 1, nm + 1).wait_recv()

    def act_drain(l):
        act_blocks(l, 3, 0).wait_send()

    def scale_copy(l, owner, dev, ssem):
        view = scale_ref.at[l, owner]
        return remote(view, view, ssem, sc_r.at[l, owner], dev)

    def scale_send(l):
        for other in (core, far, across):
            scale_copy(l, c, (m, other), sc_s.at[l]).start()

    def scale_wait(l, owner):
        scale_copy(l, owner, (m, core), sc_s.at[l]).wait_recv()

    def scale_drain(l):
        view = scale_ref.at[l, pl.ds(0, 3)]
        remote(view, view, sc_s.at[l], sc_r.at[l, core], (m, core)).wait_send()

    own_along(0)
    own_aside(0)

    loads[2].wait()
    col_of = lax.broadcasted_iota(jnp.int32, (width, width), 0)
    diagonal = col_of == lax.broadcasted_iota(jnp.int32, (width, width), 1)
    for n in range(nm):

        @pl.loop(0, height)
        def _(h):
            line_n = jnp.broadcast_to(mask_in[h, n : n + 1, :].astype(F32), (width, width))
            r = pl.ds(pl.multiple_of(n * map_rows + h * width, 8), width)
            conv[r, 0:width] = jnp.where(diagonal, line_n, 0.0)

    mask_ref[...] = jnp.dot(
        conv[:, 0:width].astype(BF16), jnp.ones((width, LANES), BF16), preferred_element_type=F32
    )
    loads[1].wait()

    @pl.loop(0, chunks)
    def _(i):
        r = rows_of(i)
        act[0, r, lane_own] = (x_in[r, :].astype(F32) * mask_ref[r, :]).astype(BF16)

    for n in range(nm):
        act_send(0, n)

    for n in range(nm):
        for i in range(3):
            for j in range(3):
                prod[i, j, n, 0:PAD, :] = jnp.zeros((PAD, LANES), F32)
                prod[i, j, n, PAD + map_rows :, :] = jnp.zeros((PAD, LANES), F32)
        zpad[n, 0:PAD, :] = jnp.zeros((PAD, LANES), F32)
        zpad[n, PAD + map_rows :, :] = jnp.zeros((PAD, LANES), F32)

    col_chunk = lax.broadcasted_iota(jnp.int32, (6, width, LANES), 1).reshape(chunk, LANES)
    has_left = jnp.where(col_chunk > 0, 1.0, 0.0)
    has_right = jnp.where(col_chunk < width - 1, 1.0, 0.0)

    loads[3].wait()
    loads[4].wait()
    half_h, half_w = height // 2, width // 2

    @pl.loop(0, half_h)
    def _(h):
        pool32[...] = grad_in[h].astype(F32)
        for n in range(nm):
            pick = pl.ds(n, half_w, stride=nm)
            kept = index_in[h, pick, :]
            value = pool32[pick, :]
            base = n * map_rows + 2 * h * width
            for r in range(2):
                for s in range(2):
                    spread[pl.ds(base + r * width + s, half_w, stride=2), :] = jnp.where(
                        kept == 2 * r + s, value, 0.0
                    )

    tasks = gather_tasks(step_both, 0)
    z_tasks = {l: gather_tasks(step_along, l) for l in range(1, layers)}
    x_tasks = {l: gather_tasks(step_aside, l) for l in range(1, layers)}
    with scope("gather0"):
        run(tasks, 2 * pieces)
        if layers > 1:
            own_along(1)
        run(tasks)
    if layers > 1:
        own_aside_late(1, 0)
    for n in range(nm):
        act_forward(0, n)
    if layers > 1:
        with scope("along_1"):
            run(z_tasks[1], pieces)
    with scope("gather0_end"):
        gather_finish(0)
    if layers > 1:
        own_aside_late(1, 1)
    act_near(0)
    act_across(0)
    for cp in loads[5:]:
        cp.wait()

    for l in range(layers):
        z_near, x_near = z_tasks.get(l + 1, []), x_tasks.get(l + 1, [])
        z_next = z_tasks.get(l + 2, [])

        @pl.loop(0, 3)
        def _(i):
            cols = pl.ds(pl.multiple_of(i * (3 * LANES), LANES), 3 * LANES)
            w = wcat[l * maps : (l + 1) * maps, :, cols].reshape(maps * rows_w, 3 * LANES)
            for n in range(nm):
                out = jnp.dot(
                    act[l, pl.ds(n * map_rows, map_rows), :], w, preferred_element_type=F32
                )
                for j in range(3):
                    prod[i, j, n, PAD : PAD + map_rows, :] = out[:, j * LANES : (j + 1) * LANES]

        def conv_chunk(i, carry):
            total, count = carry
            r = rows_of(i)
            value = None
            for j in range(3):
                side = None
                for k in range(3):
                    n, pr = padded_rows(i, width * (k - 1) + (j - 1))
                    term = prod[k, j, n, pr, :]
                    side = term if side is None else side + term
                if j == 0:
                    side = side * has_left
                if j == 2:
                    side = side * has_right
                value = side if value is None else value + side
            conv[r, :] = value
            valid = mask_ref[r, :]
            return total + tile8(value * valid), count + tile8(valid)

        zero8 = jnp.zeros((8, LANES), F32)
        total, count = lax.fori_loop(0, chunks, conv_chunk, (zero8, zero8))
        total = jnp.sum(total, axis=0, keepdims=True)
        count = jnp.sum(count, axis=0, keepdims=True)
        mean = total / jnp.maximum(count, 1.0)

        def dev_chunk(i, carry):
            r = rows_of(i)
            delta = conv[r, :] - mean
            if l + 1 < layers:
                raw[l, c, r, :] = delta.astype(BF16)
            return carry + tile8(delta * delta * mask_ref[r, :])

        spread_sum = zero8
        for n in range(nm):
            spread_sum = lax.fori_loop(n * per_map, (n + 1) * per_map, dev_chunk, spread_sum)
            if l + 1 < layers:
                act_send(l + 1, n)
        spread_sum = jnp.sum(spread_sum, axis=0, keepdims=True)
        stat[l, m] = jnp.concatenate(
            [total, spread_sum, count, mean, jnp.zeros((4, LANES), F32)], axis=0
        )
        stat_send(l)
        with scope("gather_a"):
            done = len(x_near) - len(z_near)
            run(x_near, done)
            if l + 2 < layers:
                own_along(l + 2)
            if len(z_near) > pieces:
                run(z_near, pieces)
                run(x_near, pieces)
        with scope("stat_wait"):
            stat_wait(l)

        def add_totals(s, carry):
            block = stat[l, s]
            return carry[0] + block[0:1, :], carry[1] + block[2:3, :]

        zero1 = jnp.zeros((1, LANES), F32)
        total, count = lax.fori_loop(0, maps, add_totals, (zero1, zero1))
        center = total / count

        def add_spread(s, carry):
            block = stat[l, s]
            delta = block[3:4, :] - center
            return carry + block[1:2, :] + block[2:3, :] * delta * delta

        variance = lax.fori_loop(0, maps, add_spread, zero1) / count
        inv_std = lax.rsqrt(variance + norm_epsilon)
        gain = gain_in[l : l + 1, :]
        bias = bias_in[l : l + 1, :]
        if l == 0:
            count_all = count
            scales = []
        scales.append(gain * inv_std)

        if l + 1 < layers:
            factor = gain * inv_std
            scale_ref[l, c] = jnp.concatenate(
                [factor, bias + factor * (mean - center), jnp.zeros((6, LANES), F32)], axis=0
            )
            scale_send(l)

        @pl.loop(0, chunks)
        def _(i):
            r = rows_of(i)
            unit = (conv[r, :] - center) * inv_std
            pre = gain * unit + bias
            sigma = 1.0 / (1.0 + jnp.exp(-pre))
            valid = mask_ref[r, :]
            result = pre * sigma * valid
            normed[l, r, :] = unit
            slope[l, r, :] = sigma * (1.0 + pre * (1.0 - sigma)) * valid
            if l + 1 < layers:
                act[l + 1, r, lane_own] = result.astype(BF16)
            else:
                result_ref[r, :] = result

        def activate(owner, first, last):
            pair = scale_ref[l, owner]
            factor, offset = pair[0:1, :], pair[1:2, :]
            lanes = lanes_of(owner)

            @pl.loop(first * per_map, last * per_map)
            def _(i):
                r = rows_of(i)
                pre = factor * raw[l, owner, r, :].astype(F32) + offset
                result = pre / (1.0 + jnp.exp(-pre)) * mask_ref[r, :]
                act[l + 1, r, lanes] = result.astype(BF16)

        if l + 1 < layers:
            with scope("act_near"):
                act_near(l + 1)
                scale_wait(l, core)
                activate(core, 0, nm)
            with scope("gather_b"):
                run(z_near)
                run(x_near)
            with scope("act_far"):
                for n in range(nm):
                    act_forward(l + 1, n)
                    if n == 0:
                        scale_wait(l, far)
                    activate(far, n, n + 1)
            with scope("gather_c"):
                run(z_next, pieces)
            with scope("act_across"):
                act_across(l + 1)
                scale_wait(l, across)
                activate(across, 0, nm)
            if l + 2 < layers:
                own_aside_late(l + 2, 0)
            with scope("gather_end"):
                gather_finish(l + 1)
            if l + 2 < layers:
                own_aside_late(l + 2, 1)

    def pool():
        @pl.loop(0, half_h)
        def _(h):
            for n in range(nm):
                pick = pl.ds(n, half_w, stride=nm)
                kept = index_in[h, pick, :]
                base = n * map_rows + 2 * h * width
                total = jnp.zeros((half_w, LANES), F32)
                for r in range(2):
                    for s in range(2):
                        total = total + jnp.where(
                            kept == 2 * r + s,
                            result_ref[pl.ds(base + r * width + s, half_w, stride=2), :],
                            0.0,
                        )
                pool32[pick, :] = total
            pooled_ref[h] = pool32[...].astype(BF16)

    def far_first(body):
        def go(e):
            d = line - e

            @pl.when(a + d < line)
            def _():
                body(jnp.minimum(a + d, line - 1))

            @pl.when(a >= d)
            def _():
                body(jnp.maximum(a - d, 0))

        steps(1, line, go)
        body(a)

    def part_of(g):
        return pl.ds(g * piece_rows, piece_rows)

    def gx_copy(l, z, g):
        return remote(
            gx_out.at[l, z, part_of(g)], gx_in.at[l, z, part_of(g)],
            gx_s.at[l], gx_r.at[l, z, g], beside,
        )

    def gz_copy(l, z, g, slot, dev):
        return remote(
            gz_out.at[l, z, part_of(g)], gz_in.at[l, slot, part_of(g)],
            gz_s.at[l], gz_r.at[l, slot, g], dev,
        )

    def shard(l, slot, g):
        first = pl.multiple_of(slot * rows_w, 8) + g * piece_rows
        return grad_w[l, pl.ds(first, piece_rows), :]

    tile = 2 * rows_w
    fine = tile % LANES == 0

    def kernel_grad(l, first, amount):
        rows = pl.ds(pl.multiple_of(first, LANES), amount)
        grad_w[l, rows, :] = lax.dot_general(
            act[l, :, rows], dcat[...], (((0,), (0,)), ((), ())), preferred_element_type=F32
        )

    def kernel_grads(l, send):
        if not fine:
            coarse = (maps * rows_w) // 4
            pl.loop(0, 4)(lambda i: kernel_grad(l, i * coarse, coarse))

        def go(z):
            if fine:
                kernel_grad(l, z * tile, tile)
            for g in range(pieces):
                gx_out[l, z, part_of(g)] = shard(l, z * 2 + 1 - b, g).astype(BF16)
            if send:
                for g in range(pieces):
                    gx_copy(l, z, g).start()
            else:

                @pl.when(z == farthest)
                def _():
                    for g in range(pieces):
                        gx_copy(l, z, g).start()

        far_first(go)

    farthest = jnp.where(a < line // 2, line - 1, 0)

    def scatter_x(l):
        def go(z):
            @pl.when(z != farthest)
            def _():
                for g in range(pieces):
                    gx_copy(l, z, g).start()

        far_first(go)

    def pair_sum(l, z, g):
        gx_copy(l, z, g).wait_recv()
        return shard(l, z * 2 + b, g) + gx_in[l, z, part_of(g)].astype(F32)

    def onward(l, z, g, has_more, dev, slot):
        @pl.when(has_more)
        def _():
            gz_copy(l, z, g, z, dev).wait_recv()
            gz_out[l, z, part_of(g)] = (
                pair_sum(l, z, g) + gz_in[l, z, part_of(g)].astype(F32)
            ).astype(BF16)

        @pl.when(jnp.logical_not(has_more))
        def _():
            gz_out[l, z, part_of(g)] = pair_sum(l, z, g).astype(BF16)

        gz_copy(l, z, g, slot, dev).start()

    def scatter_step(l, d, g):
        @pl.when(a + d < line)
        def _():
            z = jnp.minimum(a + d, line - 1)
            onward(l, z, g, a > 0, right, z)

        @pl.when(a >= d)
        def _():
            z = jnp.maximum(a - d, 0)
            onward(l, z, g, a + 1 < line, left, jnp.where(z == a - 1, line, z))

    def scatter_own(l, g):
        r = part_of(g)
        total_w[r, :] = pair_sum(l, a, g)

        @pl.when(a > 0)
        def _():
            gz_copy(l, a, g, a, left).wait_recv()
            total_w[r, :] += gz_in[l, a, r].astype(F32)

        @pl.when(a + 1 < line)
        def _():
            gz_copy(l, a, g, line, right).wait_recv()
            total_w[r, :] += gz_in[l, line, r].astype(F32)

        for t in range(taps):
            gradient = total_w[r, t * LANES : (t + 1) * LANES]
            new, first, second = adamw_update(
                weight_in[l, t, r], gradient, first_in[l, t, r], second_in[l, t, r], rate_conv
            )
            wgrad_ref[l, t, r] = gradient
            wfirst_ref[l, t, r] = first
            wsecond_ref[l, t, r] = second
            wnew_ref[l, t, r] = new
            wcopy_ref[l, t, r] = new.astype(BF16)

    def scatter_tasks(l):
        owns = [functools.partial(scatter_own, l, g) for g in range(pieces)]
        if line <= 8:
            return [
                functools.partial(scatter_step, l, line - e, g)
                for e in range(1, line)
                for g in range(pieces)
            ], owns

        def everything():
            def go(e):
                for g in range(pieces):
                    scatter_step(l, line - e, g)

            steps(1, line, go)

        return [everything], owns

    def scatter_drain(l):
        remote(gx_out.at[l], gx_in.at[l], gx_s.at[l], gx_r.at[l, 0, 0], beside).wait_send()
        view = pl.ds(0, line - 1)
        remote(
            gz_out.at[l, view], gz_in.at[l, view], gz_s.at[l], gz_r.at[l, 0, 0], beside
        ).wait_send()

    def layer_drain(l):
        stat_drain(layers + l)
        remote(pair_out.at[l], pair_in.at[l], pr_s.at[l], pr_r.at[l, 0], (m, core)).wait_send()
        remote(far_out.at[l], far_in.at[l], fr_s.at[l], fr_r.at[l, 0], (m, far)).wait_send()

    half = 2 * LANES
    own_half = (c // 2) * half
    other_half = half - own_half
    lane_in_half = pl.ds(pl.multiple_of((c % 2) * LANES, LANES), LANES)
    lane_out_half = pl.ds(pl.multiple_of((1 - c % 2) * LANES, LANES), LANES)

    def pair_copy(l, h, n):
        return remote(
            pair_out.at[l, h, pl.ds(n * map_rows, map_rows), :],
            pair_in.at[l, h, pl.ds(n * map_rows, map_rows), :],
            pr_s.at[l], pr_r.at[l, n if h == 0 else nm], (m, core),
        )

    def far_copy(l, n):
        return remote(
            far_out.at[l, pl.ds(n * map_rows, map_rows), :],
            far_in.at[l, pl.ds(n * map_rows, map_rows), :],
            fr_s.at[l], fr_r.at[l, n], (m, far),
        )

    todo, owns = {}, {}
    for l in reversed(range(layers)):
        e = layers + l
        source = spread if l == layers - 1 else back

        def slope_chunk(i, carry):
            r = rows_of(i)
            value = source[r, :] * slope[l, r, :]
            conv[r, :] = value
            return carry[0] + tile8(value * normed[l, r, :]), carry[1] + tile8(value)

        zero8 = jnp.zeros((8, LANES), F32)
        gain_sum, bias_sum = lax.fori_loop(0, chunks, slope_chunk, (zero8, zero8))
        stat[e, m] = jnp.concatenate(
            [
                jnp.sum(gain_sum, axis=0, keepdims=True),
                jnp.sum(bias_sum, axis=0, keepdims=True),
                jnp.zeros((6, LANES), F32),
            ],
            axis=0,
        )
        stat_send(e)
        if l + 1 < layers:
            scatter_x(l + 1)
        else:
            pool()
        if l + 1 < layers:
            todo[l + 1], owns[l + 1] = scatter_tasks(l + 1)
        if l + 2 < layers:
            with scope("scatter_last"):
                run(todo[l + 2])
        with scope("stat_wait_back"):
            stat_wait(e)

        def add_sums(s, carry):
            return carry + stat[e, s]

        sums = lax.fori_loop(0, maps, add_sums, jnp.zeros((8, LANES), F32))
        ngrad_ref[l] = sums[0:2, :]
        gain_grad = sums[0:1, :]
        bias_grad = sums[1:2, :]
        scale = scales[l]

        def conv_grad(n):
            @pl.loop(n * per_map, (n + 1) * per_map)
            def _(i):
                r = rows_of(i)
                value = (
                    mask_ref[r, :]
                    * scale
                    * (conv[r, :] - (bias_grad + normed[l, r, :] * gain_grad) / count_all)
                )
                pr = pl.ds(pl.multiple_of((i - n * per_map) * chunk, 16) + PAD, chunk)
                zpad[n, pr, :] = value

            @pl.loop(n * per_map, (n + 1) * per_map)
            def _(i):
                r = rows_of(i)
                for k in range(3):
                    for j in range(3):
                        shift = PAD - (width * (k - 1) + (j - 1))
                        pr = pl.ds(pl.multiple_of((i - n * per_map) * chunk, 16) + shift, chunk)
                        term = zpad[n, pr, :]
                        if j == 0:
                            term = term * has_right
                        if j == 2:
                            term = term * has_left
                        t = 3 * k + j
                        dcat[r, t * LANES : (t + 1) * LANES] = term.astype(BF16)

        def input_grad(h, n):
            start = other_half if h == 0 else own_half
            slots = maps // 2
            w = wcat[pl.ds(l * maps + (start // half) * slots, slots), :, :].reshape(half, wide)
            r = pl.ds(n * map_rows, map_rows)
            part[h, r, :] = lax.dot_general(
                dcat[r, :], w, (((1,), (1,)), ((), ())), preferred_element_type=F32
            )
            pair_out[l, h, r, :] = part[h, r, lane_out_half].astype(BF16)
            pair_copy(l, h, n).start()

        def to_far(n):
            r = pl.ds(n * map_rows, map_rows)
            pair_copy(l, 0, n).wait_recv()
            far_out[l, r, :] = (
                part[0, r, lane_in_half] + pair_in[l, 0, r, :].astype(F32)
            ).astype(BF16)
            far_copy(l, n).start()

        if l > 0:
            for n in range(nm):
                with scope("conv_grad"):
                    conv_grad(n)
                with scope("input_grad"):
                    input_grad(0, n)
                if n > 0:
                    with scope("to_far"):
                        to_far(n - 1)
            for n in range(nm):
                with scope("input_grad"):
                    input_grad(1, n)
                if n == 0:
                    with scope("to_far"):
                        to_far(nm - 1)
                    if l + 1 < layers:
                        with scope("scatter_step"):
                            run(todo[l + 1], pieces)
            with scope("kernel_grad"):
                kernel_grads(l, False)
            if l + 1 < layers:
                with scope("scatter_step"):
                    run(todo[l + 1], pieces)
            with scope("drain"):
                if l + 1 == layers:
                    for k in range(layers):
                        gather_drain(k)
                        act_drain(k)
                        stat_drain(k)
                        if k + 1 < layers:
                            scale_drain(k)
                else:
                    layer_drain(l + 1)
        else:
            for n in range(nm):
                with scope("conv_grad"):
                    conv_grad(n)
            with scope("scatter_1a"):
                run(todo[1], pieces)
            with scope("kernel_grad"):
                kernel_grads(0, True)
            todo[0], owns[0] = scatter_tasks(0)
            with scope("scatter_1b"):
                run(todo[1], pieces)
            for n in range(nm):
                with scope("input_grad"):
                    input_grad(0, n)
            with scope("scatter_1c"):
                run(todo[1])
            with scope("to_far"):
                for n in range(nm):
                    to_far(n)
            with scope("scatter_0a"):
                run(todo[0], pieces)
            for n in range(nm):
                with scope("input_grad"):
                    input_grad(1, n)
            with scope("owns"):
                for k in range(layers - 1, 0, -1):
                    run(owns[k])
            with scope("scatter_0b"):
                run(todo[0], pieces)
            with scope("drain"):
                for k in range(1, layers):
                    scatter_drain(k)
                layer_drain(1)

        for n in range(nm):
            r = pl.ds(n * map_rows, map_rows)
            with scope("far_wait"):
                if n == 0:
                    remote(
                        pair_out.at[l, 1], pair_in.at[l, 1], pr_s.at[l], pr_r.at[l, nm], (m, core)
                    ).wait_recv()
                far_copy(l, n).wait_recv()

            @pl.loop(n * per_map, (n + 1) * per_map)
            def _(i):
                r = rows_of(i)
                value = (
                    part[1, r, lane_in_half]
                    + pair_in[l, 1, r, :].astype(F32)
                    + far_in[l, r, :].astype(F32)
                )
                if l == 0:
                    value = value * mask_ref[r, :]
                back[r, :] = value

    with scope("norms"):
        for values, place in ((gain_in, 0), (bias_in, 1)):
            new, first, second = adamw_update(
                values[...], ngrad_ref[:, place, :], norm_first_in[:, place, :],
                norm_second_in[:, place, :], rate_norm,
            )
            nfirst_ref[:, place, :] = first
            nsecond_ref[:, place, :] = second
            nnew_ref[:, place, :] = new
    with scope("scatter_end"):
        run(todo[0])
    with scope("owns"):
        run(owns[0])

    with scope("drain_end"):
        layer_drain(0)
        scatter_drain(0)


def store_kernel(count, *refs):
    copies = [
        pltpu.make_async_copy(refs[i], refs[count + i], refs[2 * count].at[i]) for i in range(count)
    ]
    for cp in copies:
        cp.start()
    for cp in copies:
        cp.wait()


def store_results(results):
    any_spec = pl.BlockSpec(memory_space=pl.ANY)
    count = len(results)
    return pl.pallas_call(
        functools.partial(store_kernel, count),
        out_shape=tuple(jax.ShapeDtypeStruct(r.shape, r.dtype) for r in results),
        in_specs=[any_spec] * count,
        out_specs=(any_spec,) * count,
        scratch_shapes=[pltpu.SemaphoreType.DMA((count,))],
        compiler_params=pltpu.CompilerParams(vmem_limit_bytes=1 << 20),
    )(*results)


def block_call(maps, chans, x, mask, index, grad, weights, gain, bias, *moments):
    nm, height, width, lanes = x.shape
    layers, taps, rows_w, _ = weights.shape
    pixels = nm * height * width
    line = maps // 2
    wide = taps * LANES
    channels = chans * LANES
    map_rows = height * width
    sizes = (maps, chans, layers, taps, nm, height, width)
    pieces = 2 if rows_w % 32 == 0 else 1
    vm = pltpu.VMEM
    dma = pltpu.SemaphoreType.DMA
    hbm = pl.BlockSpec(memory_space=pltpu.HBM)
    scratch = [
        vm((pixels, LANES), BF16), vm(mask.shape, jnp.int32), vm(index.shape, jnp.int32),
        vm(grad.shape, BF16), vm(weights.shape, F32), vm(gain.shape, F32), vm(bias.shape, F32),
        *(vm(v.shape, F32) for v in moments),
        vm((pixels, LANES), F32),
        vm((layers * maps, rows_w, wide), BF16),
        vm((layers, pixels, channels), BF16),
        vm((layers - 1, chans, pixels, LANES), BF16),
        vm((layers - 1, chans, 8, LANES), F32),
        vm((3, 3, nm, map_rows + 2 * PAD, LANES), F32),
        vm((pixels, LANES), F32),
        vm((layers, pixels, LANES), F32),
        vm((layers, pixels, LANES), F32),
        vm((pixels, LANES), F32),
        vm((pixels, LANES), F32),
        vm((nm * (width // 2), LANES), F32),
        vm((nm, map_rows + 2 * PAD, LANES), F32),
        vm((pixels, wide), BF16),
        vm((layers, channels, wide), F32),
        vm((2, pixels, 2 * LANES), F32),
        vm((2 * layers, maps, 8, LANES), F32),
        vm((layers, 2, pixels, LANES), BF16), vm((layers, 2, pixels, LANES), BF16),
        vm((layers, pixels, LANES), BF16), vm((layers, pixels, LANES), BF16),
        vm((layers, line, rows_w, wide), BF16), vm((layers, line, rows_w, wide), BF16),
        vm((layers, line, rows_w, wide), BF16), vm((layers, line + 1, rows_w, wide), BF16),
        vm((rows_w, wide), F32),
        dma((11,)),
        dma((layers, 2)), dma((layers, line, pieces)), dma((layers,)),
        dma((2 * layers,)), dma((2 * layers,)),
        dma((layers,)), dma((layers, nm + 2)),
        dma((layers - 1,)), dma((layers - 1, chans)),
        dma((layers,)), dma((layers, nm + 1)),
        dma((layers,)), dma((layers, nm)),
        dma((layers,)), dma((layers, line, pieces)),
        dma((layers,)), dma((layers, line + 1, pieces)),
    ]
    arrays = (
        [(index.shape, BF16), ((pixels, LANES), F32)]
        + [(weights.shape, F32)] * 4
        + [(weights.shape, BF16)]
        + [((layers, 2, LANES), F32)] * 4
    )
    return pl.pallas_call(
        functools.partial(block_kernel, sizes),
        out_shape=tuple(jax.ShapeDtypeStruct(*kind) for kind in arrays),
        in_specs=[hbm] * 11,
        out_specs=(pl.BlockSpec(memory_space=pltpu.VMEM),) * len(arrays),
        scratch_shapes=scratch,
        compiler_params=pltpu.CompilerParams(
            collective_id=0, has_side_effects=True, vmem_limit_bytes=48 << 20
        ),
    )(*(
        pltpu.with_memory_space_constraint(v, pltpu.HBM)
        for v in (x.reshape(pixels, LANES), mask, index, grad, weights, gain, bias, *moments)
    ))


def local(
    maps, chans,
    input_maps, valid_mask, pool_index, out_grad, conv_weights, weight_first, weight_second,
    norm_gain, norm_bias, norm_first, norm_second,
):
    nm, half_h, half_w, lanes = pool_index.shape
    by_row = (half_h, half_w * nm, lanes)
    pooled, image, *updates = store_results(
        block_call(
            maps, chans, input_maps, valid_mask.transpose(1, 0, 2),
            pool_index.transpose(1, 2, 0, 3).reshape(by_row),
            out_grad.transpose(1, 2, 0, 3).reshape(by_row),
            conv_weights, norm_gain, norm_bias, weight_first, weight_second, norm_first, norm_second,
        )
    )
    pooled = pooled.reshape(half_h, half_w, nm, lanes).transpose(2, 0, 1, 3)
    return (pooled, image.reshape(input_maps.shape), *updates)


def solution(mesh):
    return jax.shard_map(
        functools.partial(local, mesh.shape["maps"], mesh.shape["chan"]),
        mesh=mesh,
        in_specs=(
            P("maps", None, None, "chan"),
            P("maps", None, None),
            P("maps", None, None, "chan"),
            P("maps", None, None, "chan"),
            P(None, None, "maps", "chan"),
            P(None, None, "maps", "chan"),
            P(None, None, "maps", "chan"),
            P(None, "chan"),
            P(None, "chan"),
            P(None, None, "chan"),
            P(None, None, "chan"),
        ),
        out_specs=(
            P("maps", None, None, "chan"),
            P("maps", None, None, "chan"),
            P(None, None, "maps", "chan"),
            P(None, None, "maps", "chan"),
            P(None, None, "maps", "chan"),
            P(None, None, "maps", "chan"),
            P(None, None, "maps", "chan"),
            P(None, None, "chan"),
            P(None, None, "chan"),
            P(None, None, "chan"),
            P(None, None, "chan"),
        ),
        check_vma=False,
    )
```

```python
import functools

import jax
import jax.numpy as jnp
from jax import lax
from jax.experimental import pallas as pl
from jax.experimental.pallas import tpu as pltpu
from jax.sharding import PartitionSpec as P

beta_first = 0.5
beta_second = 0.5
rate_conv = 0.01
rate_norm = 0.2
decay_rate = 0.01
adam_epsilon = 1e-08
norm_epsilon = 1e-05
step_count = 5.0
first_scale = 1.0 / (1.0 - beta_first**step_count)
second_scale = 1.0 / (1.0 - beta_second**step_count)

MESH = pl.DeviceIdType.MESH
F32 = jnp.float32
BF16 = jnp.bfloat16
LANES = 128
PAD = 32


def adamw_update(parameter, gradient, first_moment, second_moment, step_rate):
    first_new = beta_first * first_moment + (1.0 - beta_first) * gradient
    second_new = beta_second * second_moment + (1.0 - beta_second) * gradient * gradient
    step = first_new * first_scale / (jnp.sqrt(second_new * second_scale) + adam_epsilon)
    return (parameter - step_rate * (step + decay_rate * parameter), first_new, second_new)


def steps(low, high, body):
    if high - low <= 8:
        for index in range(low, high):
            body(index)
    else:
        pl.loop(low, high)(body)


scope = jax.named_scope


def run(tasks, amount=None):
    for _ in range(len(tasks) if amount is None else min(amount, len(tasks))):
        tasks.pop(0)()


def tile8(values):
    rows = values.shape[0]
    return jnp.sum(values.reshape(rows // 8, 8, LANES), axis=0)


def block_kernel(
    sizes,
    x_hbm, mask_hbm, index_hbm, grad_hbm, weight_hbm, gain_hbm, bias_hbm,
    first_hbm, second_hbm, norm_first_hbm, norm_second_hbm,
    pooled_ref, back, wgrad_ref, wfirst_ref, wsecond_ref, wnew_ref, wcopy_ref,
    ngrad_ref, nfirst_ref, nsecond_ref, nnew_ref,
    x_in, mask_in, index_in, grad_in, weight_in, gain_in, bias_in,
    first_in, second_in, norm_first_in, norm_second_in,
    mask_ref, wcat, turned, act, raw, scale_ref, prod, conv, normed, slope, result_ref, spread, pool32, zpad, dcat,
    grad_w, part, stat, pair_out, pair_in, far_out, far_in,
    gx_out, gx_in, gz_out, gz_in, total_w,
    in_sem,
    w_s, wz_r, wx_r, st_s, st_r, ag_s, ag_r, sc_s, sc_r, pr_s, pr_r, fr_s, fr_r,
    gx_s, gx_r, gz_s, gz_r,
):
    maps, chans, layers, taps, nm, height, width = sizes
    line = maps // 2
    m = lax.axis_index("maps")
    c = lax.axis_index("chan")
    a = m // 2
    b = m % 2
    core = c + 1 - 2 * (c % 2)
    far = lax.rem(c + 2, 4)
    across = core + 2 - 4 * (core // 2)
    map_rows = height * width
    pixels = nm * map_rows
    rows_w = wcat.shape[1]
    wide = taps * LANES
    chunk = 6 * width
    chunks = pixels // chunk
    per_map = map_rows // chunk

    def rows_of(i):
        return pl.ds(pl.multiple_of(i * chunk, 16), chunk)

    def padded_rows(i, shift):
        n = i // per_map
        return n, pl.ds(pl.multiple_of((i - n * per_map) * chunk, 8) + (PAD + shift), chunk)

    def remote(src, dst, ssem, rsem, dev):
        return pltpu.make_async_remote_copy(
            src_ref=src, dst_ref=dst, send_sem=ssem, recv_sem=rsem,
            device_id=dev, device_id_type=MESH,
        )

    loads = []
    for i, (src, dst) in enumerate(
        (
            (weight_hbm, weight_in), (x_hbm, x_in), (mask_hbm, mask_in),
            (index_hbm, index_in), (grad_hbm, grad_in), (gain_hbm, gain_in), (bias_hbm, bias_in),
            (first_hbm, first_in), (second_hbm, second_in),
            (norm_first_hbm, norm_first_in), (norm_second_hbm, norm_second_in),
        )
    ):
        cp = pltpu.make_async_copy(src, dst, in_sem.at[i])
        cp.start()
        loads.append(cp)

    barrier = pltpu.get_barrier_semaphore()

    def greet(d):
        peer = lax.rem(m + d, maps)
        pl.semaphore_signal(barrier, inc=1, device_id=(peer, c), device_id_type=MESH)

    steps(1, maps, greet)
    for other in (core, far, across):
        pl.semaphore_signal(barrier, inc=1, device_id=(m, other), device_id_type=MESH)

    with scope("load"):
        loads[0].wait()
    for l in range(layers):
        for t in range(taps):
            wcat[l * maps + m, :, t * LANES : (t + 1) * LANES] = weight_in[l, t].astype(BF16)

    with scope("barrier"):
        pl.semaphore_wait(barrier, maps + 2)

    pieces = wz_r.shape[2]
    piece_rows = rows_w // pieces
    right = (jnp.minimum(m + 2, maps - 1), c)
    left = (jnp.maximum(m - 2, 0), c)
    beside = (m + 1 - 2 * b, c)

    def weight_view(l, slot, g):
        return wcat.at[l * maps + slot, pl.ds(g * piece_rows, piece_rows)]

    def along(l, z, g, dev):
        view = weight_view(l, z * 2 + b, g)
        return remote(view, view, w_s.at[l, 0], wz_r.at[l, z, g], dev)

    def aside(l, z, g):
        view = weight_view(l, z * 2 + b, g)
        return remote(view, view, w_s.at[l, 1], wx_r.at[l], beside)

    def shards_of(l, count, place):
        view = wcat.at[pl.ds(0, count)]
        return remote(view, view, w_s.at[l, place], wx_r.at[l], beside)

    def own_along(l):
        for g in range(pieces):
            pl.when(a + 1 < line)(lambda: along(l, a, g, right).start())
            pl.when(a > 0)(lambda: along(l, a, g, left).start())

    def own_aside(l):
        for g in range(pieces):
            aside(l, a, g).start()

    def own_aside_late(l, late):
        pl.when(c % 2 == late)(lambda: own_aside(l))

    def step_along(l, s, g):
        def piece(cond, z, onward_cond, onward):
            @pl.when(cond)
            def _():
                along(l, z, g, onward).wait_recv()
                pl.when(onward_cond)(lambda: along(l, z, g, onward).start())

        piece(a >= s, jnp.maximum(a - s, 0), a + 1 < line, right)
        piece(a + s < line, jnp.minimum(a + s, line - 1), a > 0, left)

    def step_aside(l, s, g):
        pl.when(a >= s)(lambda: aside(l, jnp.maximum(a - s, 0), g).start())
        pl.when(a + s < line)(lambda: aside(l, jnp.minimum(a + s, line - 1), g).start())

    def step_both(l, s, g):
        step_along(l, s, g)
        step_aside(l, s, g)

    def gather_tasks(step, l):
        if line <= 8:
            return [
                functools.partial(step, l, s, g) for s in range(1, line) for g in range(pieces)
            ]

        def everything():
            def go(s):
                for g in range(pieces):
                    step(l, s, g)

            steps(1, line, go)

        return [everything]

    def gather_finish(l):
        shards_of(l, line, 1).wait_recv()

    def gather_drain(l):
        shards_of(l, line, 1).wait_send()
        inner = jnp.logical_and(a > 0, a + 1 < line)
        pl.when(inner)(lambda: shards_of(l, line + 1, 0).wait_send())
        pl.when(jnp.logical_not(inner))(lambda: shards_of(l, 1, 0).wait_send())

    def stat_send(e):
        view = stat.at[e, m]

        def send(peer):
            remote(view, view, st_s.at[e], st_r.at[e], (peer, c)).start()

        def go(d):
            @pl.when(a + line - d < line)
            def _():
                first = jnp.minimum(a + line - d, line - 1) * 2
                send(first + 1 - b)
                send(first + b)

            @pl.when(a >= line - d)
            def _():
                first = jnp.maximum(a - line + d, 0) * 2
                send(first + 1 - b)
                send(first + b)

        steps(1, line, go)
        send(m + 1 - 2 * b)

    def stat_all(e):
        view = stat.at[e, pl.ds(0, maps - 1)]
        return remote(view, view, st_s.at[e], st_r.at[e], beside)

    def stat_wait(e):
        stat_all(e).wait_recv()

    def stat_drain(e):
        stat_all(e).wait_send()

    lane_own = pl.ds(pl.multiple_of(c * LANES, LANES), LANES)

    def lanes_of(owner):
        return pl.ds(pl.multiple_of(owner * LANES, LANES), LANES)

    def act_copy(l, n, owner, dev, place):
        rows = pl.ds(n * map_rows, map_rows)
        view = act.at[0, rows, lanes_of(owner)] if l == 0 else raw.at[l - 1, owner, rows]
        return remote(view, view, ag_s.at[l], ag_r.at[l, place], dev)

    def act_blocks(l, count, place):
        view = act.at[0, :, pl.ds(0, count * LANES)] if l == 0 else raw.at[l - 1, pl.ds(0, count)]
        return remote(view, view, ag_s.at[l], ag_r.at[l, place], (m, core))

    def act_send(l, n):
        act_copy(l, n, c, (m, far), n).start()
        act_copy(l, n, c, (m, core), nm).start()

    def act_forward(l, n):
        act_copy(l, n, far, (m, far), n).wait_recv()
        act_copy(l, n, far, (m, core), nm + 1).start()

    def act_near(l):
        act_blocks(l, 1, nm).wait_recv()

    def act_across(l):
        act_blocks(l, 1, nm + 1).wait_recv()

    def act_drain(l):
        act_blocks(l, 3, 0).wait_send()

    def scale_copy(l, owner, dev, ssem):
        view = scale_ref.at[l, owner]
        return remote(view, view, ssem, sc_r.at[l, owner], dev)

    def scale_send(l):
        for other in (core, far, across):
            scale_copy(l, c, (m, other), sc_s.at[l]).start()

    def scale_wait(l, owner):
        scale_copy(l, owner, (m, core), sc_s.at[l]).wait_recv()

    def scale_drain(l):
        view = scale_ref.at[l, pl.ds(0, 3)]
        remote(view, view, sc_s.at[l], sc_r.at[l, core], (m, core)).wait_send()

    own_along(0)
    own_aside(0)

    loads[2].wait()
    col_of = lax.broadcasted_iota(jnp.int32, (width, width), 0)
    diagonal = col_of == lax.broadcasted_iota(jnp.int32, (width, width), 1)
    for n in range(nm):

        @pl.loop(0, height)
        def _(h):
            line_n = jnp.broadcast_to(mask_in[h, n : n + 1, :].astype(F32), (width, width))
            r = pl.ds(pl.multiple_of(n * map_rows + h * width, 8), width)
            conv[r, 0:width] = jnp.where(diagonal, line_n, 0.0)

    mask_ref[...] = jnp.dot(
        conv[:, 0:width].astype(BF16), jnp.ones((width, LANES), BF16), preferred_element_type=F32
    )
    loads[1].wait()

    @pl.loop(0, chunks)
    def _(i):
        r = rows_of(i)
        act[0, r, lane_own] = (x_in[r, :].astype(F32) * mask_ref[r, :]).astype(BF16)

    for n in range(nm):
        act_send(0, n)

    for n in range(nm):
        for i in range(3):
            for j in range(3):
                prod[i, j, n, 0:PAD, :] = jnp.zeros((PAD, LANES), F32)
                prod[i, j, n, PAD + map_rows :, :] = jnp.zeros((PAD, LANES), F32)
        zpad[n, 0:PAD, :] = jnp.zeros((PAD, LANES), F32)
        zpad[n, PAD + map_rows :, :] = jnp.zeros((PAD, LANES), F32)

    col_chunk = lax.broadcasted_iota(jnp.int32, (6, width, LANES), 1).reshape(chunk, LANES)
    has_left = jnp.where(col_chunk > 0, 1.0, 0.0)
    has_right = jnp.where(col_chunk < width - 1, 1.0, 0.0)

    loads[3].wait()
    loads[4].wait()
    half_h, half_w = height // 2, width // 2

    @pl.loop(0, half_h)
    def _(h):
        pool32[...] = grad_in[h].astype(F32)
        for n in range(nm):
            pick = pl.ds(n, half_w, stride=nm)
            kept = index_in[h, pick, :]
            value = pool32[pick, :]
            base = n * map_rows + 2 * h * width
            for r in range(2):
                for s in range(2):
                    spread[pl.ds(base + r * width + s, half_w, stride=2), :] = jnp.where(
                        kept == 2 * r + s, value, 0.0
                    )

    tasks = gather_tasks(step_both, 0)
    z_tasks = {l: gather_tasks(step_along, l) for l in range(1, layers)}
    x_tasks = {l: gather_tasks(step_aside, l) for l in range(1, layers)}
    with scope("gather0"):
        run(tasks, 2 * pieces)
        if layers > 1:
            own_along(1)
        run(tasks)
    if layers > 1:
        own_aside_late(1, 0)
    for n in range(nm):
        act_forward(0, n)
    if layers > 1:
        with scope("along_1"):
            run(z_tasks[1], pieces)
    with scope("gather0_end"):
        gather_finish(0)
    if layers > 1:
        own_aside_late(1, 1)
    act_near(0)
    act_across(0)
    for cp in loads[5:]:
        cp.wait()

    for l in range(layers):
        z_near, x_near = z_tasks.get(l + 1, []), x_tasks.get(l + 1, [])
        z_next = z_tasks.get(l + 2, [])

        kernel = wcat[l * maps : (l + 1) * maps, :, :].reshape(maps * rows_w, wide)
        for n in range(nm):
            out = jnp.dot(
                act[l, pl.ds(n * map_rows, map_rows), :], kernel, preferred_element_type=F32
            )
            for i in range(3):
                for j in range(3):
                    t = 3 * i + j
                    prod[i, j, n, PAD : PAD + map_rows, :] = out[:, t * LANES : (t + 1) * LANES]

        def conv_chunk(i, carry):
            total, count = carry
            r = rows_of(i)
            value = None
            for j in range(3):
                side = None
                for k in range(3):
                    n, pr = padded_rows(i, width * (k - 1) + (j - 1))
                    term = prod[k, j, n, pr, :]
                    side = term if side is None else side + term
                if j == 0:
                    side = side * has_left
                if j == 2:
                    side = side * has_right
                value = side if value is None else value + side
            conv[r, :] = value
            valid = mask_ref[r, :]
            return total + tile8(value * valid), count + tile8(valid)

        zero8 = jnp.zeros((8, LANES), F32)
        total, count = lax.fori_loop(0, chunks, conv_chunk, (zero8, zero8))
        total = jnp.sum(total, axis=0, keepdims=True)
        count = jnp.sum(count, axis=0, keepdims=True)
        mean = total / jnp.maximum(count, 1.0)

        def dev_chunk(i, carry):
            r = rows_of(i)
            delta = conv[r, :] - mean
            if l + 1 < layers:
                raw[l, c, r, :] = delta.astype(BF16)
            return carry + tile8(delta * delta * mask_ref[r, :])

        spread_sum = zero8
        for n in range(nm):
            spread_sum = lax.fori_loop(n * per_map, (n + 1) * per_map, dev_chunk, spread_sum)
            if l + 1 < layers:
                act_send(l + 1, n)
        spread_sum = jnp.sum(spread_sum, axis=0, keepdims=True)
        stat[l, m] = jnp.concatenate(
            [total, spread_sum, count, mean, jnp.zeros((4, LANES), F32)], axis=0
        )
        stat_send(l)
        with scope("gather_a"):
            done = len(x_near) - len(z_near)
            run(x_near, done)
            if l + 2 < layers:
                own_along(l + 2)
            if len(z_near) > pieces:
                run(z_near, pieces)
                run(x_near, pieces)
        with scope("turn"):
            slots = LANES // rows_w
            for i in range(maps // slots):
                turned[l, :, i * LANES : (i + 1) * LANES] = (
                    wcat[l * maps + i * slots : l * maps + (i + 1) * slots, :, :].reshape(LANES, wide).T
                )
        with scope("stat_wait"):
            stat_wait(l)

        def add_totals(s, carry):
            block = stat[l, s]
            return carry[0] + block[0:1, :], carry[1] + block[2:3, :]

        zero1 = jnp.zeros((1, LANES), F32)
        total, count = lax.fori_loop(0, maps, add_totals, (zero1, zero1))
        center = total / count

        def add_spread(s, carry):
            block = stat[l, s]
            delta = block[3:4, :] - center
            return carry + block[1:2, :] + block[2:3, :] * delta * delta

        variance = lax.fori_loop(0, maps, add_spread, zero1) / count
        inv_std = lax.rsqrt(variance + norm_epsilon)
        gain = gain_in[l : l + 1, :]
        bias = bias_in[l : l + 1, :]
        if l == 0:
            count_all = count
            scales = []
        scales.append(gain * inv_std)

        if l + 1 < layers:
            factor = gain * inv_std
            scale_ref[l, c] = jnp.concatenate(
                [factor, bias + factor * (mean - center), jnp.zeros((6, LANES), F32)], axis=0
            )
            scale_send(l)

        @pl.loop(0, chunks)
        def _(i):
            r = rows_of(i)
            unit = (conv[r, :] - center) * inv_std
            pre = gain * unit + bias
            sigma = 1.0 / (1.0 + jnp.exp(-pre))
            valid = mask_ref[r, :]
            result = pre * sigma * valid
            normed[l, r, :] = unit
            slope[l, r, :] = sigma * (1.0 + pre * (1.0 - sigma)) * valid
            if l + 1 < layers:
                act[l + 1, r, lane_own] = result.astype(BF16)
            else:
                result_ref[r, :] = result

        def activate(owner, first, last):
            pair = scale_ref[l, owner]
            factor, offset = pair[0:1, :], pair[1:2, :]
            lanes = lanes_of(owner)

            @pl.loop(first * per_map, last * per_map)
            def _(i):
                r = rows_of(i)
                pre = factor * raw[l, owner, r, :].astype(F32) + offset
                result = pre / (1.0 + jnp.exp(-pre)) * mask_ref[r, :]
                act[l + 1, r, lanes] = result.astype(BF16)

        if l + 1 < layers:
            with scope("act_near"):
                act_near(l + 1)
                scale_wait(l, core)
                activate(core, 0, nm)
            with scope("gather_b"):
                run(z_near)
                run(x_near)
            with scope("act_far"):
                for n in range(nm):
                    act_forward(l + 1, n)
                    if n == 0:
                        scale_wait(l, far)
                    activate(far, n, n + 1)
            with scope("gather_c"):
                run(z_next, pieces)
            with scope("act_across"):
                act_across(l + 1)
                scale_wait(l, across)
                activate(across, 0, nm)
            if l + 2 < layers:
                own_aside_late(l + 2, 0)
            with scope("gather_end"):
                gather_finish(l + 1)
            if l + 2 < layers:
                own_aside_late(l + 2, 1)

    def pool():
        @pl.loop(0, half_h)
        def _(h):
            for n in range(nm):
                pick = pl.ds(n, half_w, stride=nm)
                kept = index_in[h, pick, :]
                base = n * map_rows + 2 * h * width
                total = jnp.zeros((half_w, LANES), F32)
                for r in range(2):
                    for s in range(2):
                        total = total + jnp.where(
                            kept == 2 * r + s,
                            result_ref[pl.ds(base + r * width + s, half_w, stride=2), :],
                            0.0,
                        )
                pool32[pick, :] = total
            pooled_ref[h] = pool32[...].astype(BF16)

    def kth_place(k):
        before, after = a, line - 1 - a
        spare = jnp.maximum(before, after) - jnp.minimum(before, after)
        q = jnp.maximum(k - spare, 0)
        near, side = q // 2, q % 2
        low = jnp.where(before > after, spare, 0) + near
        high = line - 1 - jnp.where(before < after, spare, 0) - near
        outer = jnp.where(before > after, k, line - 1 - k)
        return jnp.where(k < spare, outer, jnp.where(side == 0, high, low))

    def part_of(g):
        return pl.ds(g * piece_rows, piece_rows)

    def gx_copy(l, z, g):
        return remote(
            gx_out.at[l, z, part_of(g)], gx_in.at[l, z, part_of(g)],
            gx_s.at[l], gx_r.at[l, z, g], beside,
        )

    def gz_copy(l, z, g, slot, dev):
        return remote(
            gz_out.at[l, z, part_of(g)], gz_in.at[l, slot, part_of(g)],
            gz_s.at[l], gz_r.at[l, slot, g], dev,
        )

    def shard(l, slot, g):
        first = pl.multiple_of(slot * rows_w, 8) + g * piece_rows
        return grad_w[l, pl.ds(first, piece_rows), :]

    tile = 2 * rows_w
    fine = tile % LANES == 0

    def kernel_grad(l, first, amount):
        rows = pl.ds(pl.multiple_of(first, LANES), amount)
        grad_w[l, rows, :] = lax.dot_general(
            act[l, :, rows], dcat[...], (((0,), (0,)), ((), ())), preferred_element_type=F32
        )

    def kernel_grads(l, low=0, high=None):
        high = line if high is None else high
        if not fine and low == 0:
            coarse = (maps * rows_w) // 4
            pl.loop(0, 4)(lambda i: kernel_grad(l, i * coarse, coarse))

        def go(k):
            z = kth_place(k)
            if fine:
                kernel_grad(l, z * tile, tile)
            for g in range(pieces):
                gx_out[l, z, part_of(g)] = shard(l, z * 2 + 1 - b, g).astype(BF16)
            for g in range(pieces):
                if line > 8 or is_early(l, k, g):
                    gx_copy(l, z, g).start()

        steps(low, high, go)

    def is_early(l, k, g):
        return l == 0 or k < 2

    def scatter_x(l):
        if line <= 8:
            for k in range(line):
                for g in range(pieces):
                    if not is_early(l, k, g):
                        gx_copy(l, kth_place(k), g).start()

    def pair_sum(l, z, g):
        gx_copy(l, z, g).wait_recv()
        return shard(l, z * 2 + b, g) + gx_in[l, z, part_of(g)].astype(F32)

    def onward(l, z, g, fed, dev, slot):
        value = pair_sum(l, z, g)
        if fed:
            gz_copy(l, z, g, z, dev).wait_recv()
            value = value + gz_in[l, z, part_of(g)].astype(F32)
        gz_out[l, z, part_of(g)] = value.astype(BF16)
        gz_copy(l, z, g, slot, dev).start()

    def straight(l):
        return l == 0 and 2 < line <= 8

    def scatter_step(l, d, g, fed):
        ends = straight(l) and d == line - 1
        zr, zl = jnp.minimum(a + d, line - 1), jnp.maximum(a - d, 0)
        more_r, more_l = a > 0, a + 1 < line
        if straight(l):
            more_r = jnp.where(zr == line - 1, a > 1, more_r)
            more_l = jnp.where(zl == 0, a + 2 < line, more_l)
        for there, z, more, dev, slot in (
            (a + d < line, zr, more_r, right, zr),
            (a >= d, zl, more_l, left, jnp.where(zl == a - 1, line, zl)),
        ):
            if ends:
                dev, slot = (z * 2 + b, c), line + 1
            now = jnp.logical_and(there, more if fed else jnp.logical_not(more))
            pl.when(now)(functools.partial(onward, l, z, g, fed, dev, slot))

    def scatter_own(l, g):
        r = part_of(g)
        total_w[r, :] = pair_sum(l, a, g)

        def add(slot):
            gz_copy(l, a, g, slot, left).wait_recv()
            total_w[r, :] += gz_in[l, slot, r].astype(F32)

        pl.when(a > 0)(lambda: add(a))
        pl.when(a + 1 < line)(lambda: add(line))
        if straight(l):
            pl.when(jnp.logical_or(a == 0, a + 1 == line))(lambda: add(line + 1))
        for t in range(taps):
            gradient = total_w[r, t * LANES : (t + 1) * LANES]
            new, first, second = adamw_update(
                weight_in[l, t, r], gradient, first_in[l, t, r], second_in[l, t, r], rate_conv
            )
            wgrad_ref[l, t, r] = gradient
            wfirst_ref[l, t, r] = first
            wsecond_ref[l, t, r] = second
            wnew_ref[l, t, r] = new
            wcopy_ref[l, t, r] = new.astype(BF16)

    def scatter_tasks(l):
        owns = [functools.partial(scatter_own, l, g) for g in range(pieces)]
        if line <= 8:
            first, fed = (
                [
                    functools.partial(scatter_step, l, line - e, g, kind)
                    for e in range(1 + kind, line)
                    for g in range(pieces)
                ]
                for kind in (False, True)
            )
            return first, fed, owns

        def everything():
            def go(e):
                for g in range(pieces):
                    scatter_step(l, line - e, g, False)
                    scatter_step(l, line - e, g, True)

            steps(1, line, go)

        return [everything], [], owns

    def scatter_drain(l):
        remote(gx_out.at[l], gx_in.at[l], gx_s.at[l], gx_r.at[l, 0, 0], beside).wait_send()
        view = pl.ds(0, line - 1)
        remote(
            gz_out.at[l, view], gz_in.at[l, view], gz_s.at[l], gz_r.at[l, 0, 0], beside
        ).wait_send()

    def layer_drain(l):
        stat_drain(layers + l)
        remote(pair_out.at[l], pair_in.at[l], pr_s.at[l], pr_r.at[l, 0], (m, core)).wait_send()
        remote(far_out.at[l], far_in.at[l], fr_s.at[l], fr_r.at[l, 0], (m, far)).wait_send()

    half = 2 * LANES
    own_half = (c // 2) * half
    other_half = half - own_half
    lane_in_half = pl.ds(pl.multiple_of((c % 2) * LANES, LANES), LANES)
    lane_out_half = pl.ds(pl.multiple_of((1 - c % 2) * LANES, LANES), LANES)

    def pair_copy(l, h, n):
        return remote(
            pair_out.at[l, h, pl.ds(n * map_rows, map_rows), :],
            pair_in.at[l, h, pl.ds(n * map_rows, map_rows), :],
            pr_s.at[l], pr_r.at[l, n if h == 0 else nm], (m, core),
        )

    def far_copy(l, n):
        return remote(
            far_out.at[l, pl.ds(n * map_rows, map_rows), :],
            far_in.at[l, pl.ds(n * map_rows, map_rows), :],
            fr_s.at[l], fr_r.at[l, n], (m, far),
        )

    todo, fed, owns = {}, {}, {}
    for l in reversed(range(layers)):
        e = layers + l
        source = spread if l == layers - 1 else back

        def slope_chunk(i, carry):
            r = rows_of(i)
            value = source[r, :] * slope[l, r, :]
            conv[r, :] = value
            return carry[0] + tile8(value * normed[l, r, :]), carry[1] + tile8(value)

        zero8 = jnp.zeros((8, LANES), F32)
        gain_sum, bias_sum = lax.fori_loop(0, chunks, slope_chunk, (zero8, zero8))
        stat[e, m] = jnp.concatenate(
            [
                jnp.sum(gain_sum, axis=0, keepdims=True),
                jnp.sum(bias_sum, axis=0, keepdims=True),
                jnp.zeros((6, LANES), F32),
            ],
            axis=0,
        )
        stat_send(e)
        if l + 1 < layers:
            scatter_x(l + 1)
        else:
            pool()
        if l + 1 < layers:
            todo[l + 1], fed[l + 1], owns[l + 1] = scatter_tasks(l + 1)
        if l + 2 < layers:
            run(todo[l + 2])
            run(fed[l + 2])
        if l + 1 < layers:
            with scope("scatter_a"):
                run(todo[l + 1], pieces)
        with scope("stat_wait_back"):
            stat_wait(e)

        def add_sums(s, carry):
            return carry + stat[e, s]

        sums = lax.fori_loop(0, maps, add_sums, jnp.zeros((8, LANES), F32))
        ngrad_ref[l] = sums[0:2, :]
        gain_grad = sums[0:1, :]
        bias_grad = sums[1:2, :]
        scale = scales[l]

        def conv_grad(n):
            @pl.loop(n * per_map, (n + 1) * per_map)
            def _(i):
                r = rows_of(i)
                value = (
                    mask_ref[r, :]
                    * scale
                    * (conv[r, :] - (bias_grad + normed[l, r, :] * gain_grad) / count_all)
                )
                pr = pl.ds(pl.multiple_of((i - n * per_map) * chunk, 16) + PAD, chunk)
                zpad[n, pr, :] = value

            @pl.loop(n * per_map, (n + 1) * per_map)
            def _(i):
                r = rows_of(i)
                for k in range(3):
                    for j in range(3):
                        shift = PAD - (width * (k - 1) + (j - 1))
                        pr = pl.ds(pl.multiple_of((i - n * per_map) * chunk, 16) + shift, chunk)
                        term = zpad[n, pr, :]
                        if j == 0:
                            term = term * has_right
                        if j == 2:
                            term = term * has_left
                        t = 3 * k + j
                        dcat[r, t * LANES : (t + 1) * LANES] = term.astype(BF16)

        def input_grad(h, n):
            start = other_half if h == 0 else own_half
            r = pl.ds(n * map_rows, map_rows)
            part[h, r, :] = jnp.dot(
                dcat[r, :], turned[l, :, pl.ds(pl.multiple_of(start, half), half)],
                preferred_element_type=F32,
            )
            pair_out[l, h, r, :] = part[h, r, lane_out_half].astype(BF16)
            pair_copy(l, h, n).start()

        def to_far(n):
            r = pl.ds(n * map_rows, map_rows)
            pair_copy(l, 0, n).wait_recv()
            far_out[l, r, :] = (
                part[0, r, lane_in_half] + pair_in[l, 0, r, :].astype(F32)
            ).astype(BF16)
            far_copy(l, n).start()

        if l > 0:
            for n in range(nm):
                with scope("conv_grad"):
                    conv_grad(n)
                with scope("input_grad"):
                    input_grad(0, n)
                if n > 0:
                    with scope("to_far"):
                        to_far(n - 1)
            if l + 1 < layers:
                with scope("scatter_b"):
                    run(todo[l + 1], pieces)
                    run(fed[l + 1], pieces)
            with scope("kernel_grad"):
                kernel_grads(l, 0, line // 2)
            with scope("to_far"):
                to_far(nm - 1)
            if l + 1 < layers:
                with scope("scatter_c"):
                    run(todo[l + 1])
            with scope("kernel_grad"):
                kernel_grads(l, line // 2)
            for n in range(nm):
                with scope("input_grad"):
                    input_grad(1, n)
            with scope("drain"):
                if l + 1 == layers:
                    for k in range(layers):
                        gather_drain(k)
                        act_drain(k)
                        stat_drain(k)
                        if k + 1 < layers:
                            scale_drain(k)
                else:
                    layer_drain(l + 1)
        else:
            for n in range(nm):
                with scope("conv_grad"):
                    conv_grad(n)
            with scope("scatter_1b"):
                run(todo[1], pieces)
            with scope("kernel_grad"):
                kernel_grads(0)
            todo[0], fed[0], owns[0] = scatter_tasks(0)
            with scope("scatter_1c"):
                run(todo[1])
                run(fed[1], pieces)
            for n in range(nm):
                with scope("input_grad"):
                    input_grad(0, n)
            with scope("to_far"):
                for n in range(nm):
                    to_far(n)
            with scope("input_grad"):
                input_grad(1, 0)
            with scope("scatter_0a"):
                run(todo[0], pieces)
            with scope("scatter_1d"):
                run(fed[1])
            with scope("input_grad"):
                for n in range(1, nm):
                    input_grad(1, n)
            with scope("scatter_0b"):
                run(todo[0], pieces)
                run(fed[0], pieces)
            with scope("owns_2"):
                for k in range(layers - 1, 1, -1):
                    run(owns[k])

        for n in range(nm):
            r = pl.ds(n * map_rows, map_rows)
            with scope("far_wait"):
                if n == 0:
                    remote(
                        pair_out.at[l, 1], pair_in.at[l, 1], pr_s.at[l], pr_r.at[l, nm], (m, core)
                    ).wait_recv()
                far_copy(l, n).wait_recv()
            if n == 0 and l > 0 and l + 1 < layers:
                with scope("scatter_d"):
                    run(fed[l + 1])

            @pl.loop(n * per_map, (n + 1) * per_map)
            def _(i):
                r = rows_of(i)
                value = (
                    part[1, r, lane_in_half]
                    + pair_in[l, 1, r, :].astype(F32)
                    + far_in[l, r, :].astype(F32)
                )
                if l == 0:
                    value = value * mask_ref[r, :]
                back[r, :] = value

    with scope("norms"):
        for values, place in ((gain_in, 0), (bias_in, 1)):
            new, first, second = adamw_update(
                values[...], ngrad_ref[:, place, :], norm_first_in[:, place, :],
                norm_second_in[:, place, :], rate_norm,
            )
            nfirst_ref[:, place, :] = first
            nsecond_ref[:, place, :] = second
            nnew_ref[:, place, :] = new
    with scope("scatter_end"):
        run(todo[0])
        run(fed[0])
    with scope("owns_1"):
        for k in range(1, min(2, layers)):
            run(owns[k])
    with scope("drain"):
        for k in range(1, layers):
            scatter_drain(k)
        layer_drain(1)
    with scope("owns"):
        run(owns[0])

    with scope("drain_end"):
        layer_drain(0)
        scatter_drain(0)


def store_kernel(count, *refs):
    copies = [
        pltpu.make_async_copy(refs[i], refs[count + i], refs[2 * count].at[i]) for i in range(count)
    ]
    for cp in copies:
        cp.start()
    for cp in copies:
        cp.wait()


def store_results(results):
    any_spec = pl.BlockSpec(memory_space=pl.ANY)
    count = len(results)
    return pl.pallas_call(
        functools.partial(store_kernel, count),
        out_shape=tuple(jax.ShapeDtypeStruct(r.shape, r.dtype) for r in results),
        in_specs=[any_spec] * count,
        out_specs=(any_spec,) * count,
        scratch_shapes=[pltpu.SemaphoreType.DMA((count,))],
        compiler_params=pltpu.CompilerParams(vmem_limit_bytes=1 << 20),
    )(*results)


def block_call(maps, chans, x, mask, index, grad, weights, gain, bias, *moments):
    nm, height, width, lanes = x.shape
    layers, taps, rows_w, _ = weights.shape
    pixels = nm * height * width
    line = maps // 2
    wide = taps * LANES
    channels = chans * LANES
    map_rows = height * width
    sizes = (maps, chans, layers, taps, nm, height, width)
    pieces = 2 if rows_w % 32 == 0 else 1
    vm = pltpu.VMEM
    dma = pltpu.SemaphoreType.DMA
    hbm = pl.BlockSpec(memory_space=pltpu.HBM)
    scratch = [
        vm((pixels, LANES), BF16), vm(mask.shape, jnp.int32), vm(index.shape, jnp.int32),
        vm(grad.shape, BF16), vm(weights.shape, F32), vm(gain.shape, F32), vm(bias.shape, F32),
        *(vm(v.shape, F32) for v in moments),
        vm((pixels, LANES), F32),
        vm((layers * maps, rows_w, wide), BF16),
        vm((layers, wide, channels), BF16),
        vm((layers, pixels, channels), BF16),
        vm((layers - 1, chans, pixels, LANES), BF16),
        vm((layers - 1, chans, 8, LANES), F32),
        vm((3, 3, nm, map_rows + 2 * PAD, LANES), F32),
        vm((pixels, LANES), F32),
        vm((layers, pixels, LANES), F32),
        vm((layers, pixels, LANES), F32),
        vm((pixels, LANES), F32),
        vm((pixels, LANES), F32),
        vm((nm * (width // 2), LANES), F32),
        vm((nm, map_rows + 2 * PAD, LANES), F32),
        vm((pixels, wide), BF16),
        vm((layers, channels, wide), F32),
        vm((2, pixels, 2 * LANES), F32),
        vm((2 * layers, maps, 8, LANES), F32),
        vm((layers, 2, pixels, LANES), BF16), vm((layers, 2, pixels, LANES), BF16),
        vm((layers, pixels, LANES), BF16), vm((layers, pixels, LANES), BF16),
        vm((layers, line, rows_w, wide), BF16), vm((layers, line, rows_w, wide), BF16),
        vm((layers, line, rows_w, wide), BF16), vm((layers, line + 2, rows_w, wide), BF16),
        vm((rows_w, wide), F32),
        dma((11,)),
        dma((layers, 2)), dma((layers, line, pieces)), dma((layers,)),
        dma((2 * layers,)), dma((2 * layers,)),
        dma((layers,)), dma((layers, nm + 2)),
        dma((layers - 1,)), dma((layers - 1, chans)),
        dma((layers,)), dma((layers, nm + 1)),
        dma((layers,)), dma((layers, nm)),
        dma((layers,)), dma((layers, line, pieces)),
        dma((layers,)), dma((layers, line + 2, pieces)),
    ]
    arrays = (
        [(index.shape, BF16), ((pixels, LANES), F32)]
        + [(weights.shape, F32)] * 4
        + [(weights.shape, BF16)]
        + [((layers, 2, LANES), F32)] * 4
    )
    return pl.pallas_call(
        functools.partial(block_kernel, sizes),
        out_shape=tuple(jax.ShapeDtypeStruct(*kind) for kind in arrays),
        in_specs=[hbm] * 11,
        out_specs=(pl.BlockSpec(memory_space=pltpu.VMEM),) * len(arrays),
        scratch_shapes=scratch,
        compiler_params=pltpu.CompilerParams(
            collective_id=0, has_side_effects=True, vmem_limit_bytes=48 << 20
        ),
    )(*(
        pltpu.with_memory_space_constraint(v, pltpu.HBM)
        for v in (x.reshape(pixels, LANES), mask, index, grad, weights, gain, bias, *moments)
    ))


def local(
    maps, chans,
    input_maps, valid_mask, pool_index, out_grad, conv_weights, weight_first, weight_second,
    norm_gain, norm_bias, norm_first, norm_second,
):
    nm, half_h, half_w, lanes = pool_index.shape
    by_row = (half_h, half_w * nm, lanes)
    pooled, image, *updates = store_results(
        block_call(
            maps, chans, input_maps, valid_mask.transpose(1, 0, 2),
            pool_index.transpose(1, 2, 0, 3).reshape(by_row),
            out_grad.transpose(1, 2, 0, 3).reshape(by_row),
            conv_weights, norm_gain, norm_bias, weight_first, weight_second, norm_first, norm_second,
        )
    )
    pooled = pooled.reshape(half_h, half_w, nm, lanes).transpose(2, 0, 1, 3)
    return (pooled, image.reshape(input_maps.shape), *updates)


def solution(mesh):
    return jax.shard_map(
        functools.partial(local, mesh.shape["maps"], mesh.shape["chan"]),
        mesh=mesh,
        in_specs=(
            P("maps", None, None, "chan"),
            P("maps", None, None),
            P("maps", None, None, "chan"),
            P("maps", None, None, "chan"),
            P(None, None, "maps", "chan"),
            P(None, None, "maps", "chan"),
            P(None, None, "maps", "chan"),
            P(None, "chan"),
            P(None, "chan"),
            P(None, None, "chan"),
            P(None, None, "chan"),
        ),
        out_specs=(
            P("maps", None, None, "chan"),
            P("maps", None, None, "chan"),
            P(None, None, "maps", "chan"),
            P(None, None, "maps", "chan"),
            P(None, None, "maps", "chan"),
            P(None, None, "maps", "chan"),
            P(None, None, "maps", "chan"),
            P(None, None, "chan"),
            P(None, None, "chan"),
            P(None, None, "chan"),
            P(None, None, "chan"),
        ),
        check_vma=False,
    )
```

```python
import functools

import jax
import jax.numpy as jnp
from jax import lax
from jax.experimental import pallas as pl
from jax.experimental.pallas import tpu as pltpu
from jax.sharding import PartitionSpec as P

beta_first = 0.5
beta_second = 0.5
rate_conv = 0.01
rate_norm = 0.2
decay_rate = 0.01
adam_epsilon = 1e-08
norm_epsilon = 1e-05
step_count = 5.0
first_scale = 1.0 / (1.0 - beta_first**step_count)
second_scale = 1.0 / (1.0 - beta_second**step_count)

MESH = pl.DeviceIdType.MESH
F32 = jnp.float32
BF16 = jnp.bfloat16
LANES = 128
PAD = 32


def adamw_update(parameter, gradient, first_moment, second_moment, step_rate):
    first_new = beta_first * first_moment + (1.0 - beta_first) * gradient
    second_new = beta_second * second_moment + (1.0 - beta_second) * gradient * gradient
    step = first_new * first_scale / (jnp.sqrt(second_new * second_scale) + adam_epsilon)
    return (parameter - step_rate * (step + decay_rate * parameter), first_new, second_new)


def steps(low, high, body):
    if high - low <= 8:
        for index in range(low, high):
            body(index)
    else:
        pl.loop(low, high)(body)


scope = jax.named_scope


def run(tasks, amount=None):
    for _ in range(len(tasks) if amount is None else min(amount, len(tasks))):
        tasks.pop(0)()


def tile8(values):
    rows = values.shape[0]
    return jnp.sum(values.reshape(rows // 8, 8, LANES), axis=0)


def block_kernel(
    sizes,
    x_hbm, mask_hbm, index_hbm, grad_hbm, weight_hbm, gain_hbm, bias_hbm,
    first_hbm, second_hbm, norm_first_hbm, norm_second_hbm,
    pooled_ref, back, wgrad_ref, wfirst_ref, wsecond_ref, wnew_ref, wcopy_ref,
    ngrad_ref, nfirst_ref, nsecond_ref, nnew_ref,
    x_in, mask_in, index_in, grad_in, weight_in, gain_in, bias_in,
    first_in, second_in, norm_first_in, norm_second_in,
    mask_ref, wcat, turned, act, raw, scale_ref, prod, conv, normed, slope, result_ref, spread, pool32, zpad, dcat,
    grad_w, part, stat, pair_out, pair_in, far_out, far_in,
    gx_out, gx_in, gz_out, gz_in, total_w,
    in_sem,
    w_s, wz_r, wx_r, wc_r, st_s, st_r, ag_s, ag_r, sc_s, sc_r, pr_s, pr_r, fr_s, fr_r,
    gx_s, gx_r, gz_s, gz_r,
):
    maps, chans, layers, taps, nm, height, width = sizes
    line = maps // 2
    m = lax.axis_index("maps")
    c = lax.axis_index("chan")
    a = m // 2
    b = m % 2
    core = c + 1 - 2 * (c % 2)
    far = lax.rem(c + 2, 4)
    across = core + 2 - 4 * (core // 2)
    map_rows = height * width
    pixels = nm * map_rows
    rows_w = wcat.shape[1]
    wide = taps * LANES
    chunk = 6 * width
    chunks = pixels // chunk
    per_map = map_rows // chunk

    def rows_of(i):
        return pl.ds(pl.multiple_of(i * chunk, 16), chunk)

    def padded_rows(i, shift):
        n = i // per_map
        return n, pl.ds(pl.multiple_of((i - n * per_map) * chunk, 8) + (PAD + shift), chunk)

    def remote(src, dst, ssem, rsem, dev):
        return pltpu.make_async_remote_copy(
            src_ref=src, dst_ref=dst, send_sem=ssem, recv_sem=rsem,
            device_id=dev, device_id_type=MESH,
        )

    loads = []
    for i, (src, dst) in enumerate(
        (
            (weight_hbm, weight_in), (x_hbm, x_in), (mask_hbm, mask_in),
            (index_hbm, index_in), (grad_hbm, grad_in), (gain_hbm, gain_in), (bias_hbm, bias_in),
            (first_hbm, first_in), (second_hbm, second_in),
            (norm_first_hbm, norm_first_in), (norm_second_hbm, norm_second_in),
        )
    ):
        cp = pltpu.make_async_copy(src, dst, in_sem.at[i])
        cp.start()
        loads.append(cp)

    barrier = pltpu.get_barrier_semaphore()

    def greet(d):
        peer = lax.rem(m + d, maps)
        pl.semaphore_signal(barrier, inc=1, device_id=(peer, c), device_id_type=MESH)

    steps(1, maps, greet)
    for other in (core, far, across):
        pl.semaphore_signal(barrier, inc=1, device_id=(m, other), device_id_type=MESH)

    with scope("load"):
        loads[0].wait()
    for l in range(layers):
        for t in range(taps):
            wcat[l * maps + m, :, t * LANES : (t + 1) * LANES] = weight_in[l, t].astype(BF16)

    with scope("barrier"):
        pl.semaphore_wait(barrier, maps + 2)

    pieces = wz_r.shape[2]
    piece_rows = rows_w // pieces
    right = (jnp.minimum(m + 2, maps - 1), c)
    left = (jnp.maximum(m - 2, 0), c)
    beside = (m + 1 - 2 * b, c)
    opposite = ((line - 1 - a) * 2 + b, c)
    straight_cross = line == 4

    def crossing(l):
        return (1 if l == 0 else 2) * LANES

    def along(l, z, g, dev):
        view = wcat.at[l * maps + z * 2 + b, pl.ds(g * piece_rows, piece_rows)]
        return remote(view, view, w_s.at[l, 0], wz_r.at[l, z, g], dev)

    def aside(l, z, g):
        lanes = pl.ds(crossing(l), wide - crossing(l))
        view = wcat.at[l * maps + z * 2 + b, pl.ds(g * piece_rows, piece_rows), lanes]
        return remote(view, view, w_s.at[l, 1], wx_r.at[l, 0], beside)

    def aside_own(l, slot):
        view = wcat.at[l * maps + slot]
        return remote(view, view, w_s.at[l, 2], wx_r.at[l, 1], beside)

    def across_line(l, z, dev):
        view = wcat.at[l * maps + z * 2 + 1 - b, :, pl.ds(0, crossing(l))]
        return remote(view, view, w_s.at[l, 3], wc_r.at[l, z], dev)

    def own_along(l):
        for g in range(pieces):
            pl.when(a + 1 < line)(lambda: along(l, a, g, right).start())
            pl.when(a > 0)(lambda: along(l, a, g, left).start())

    def own_aside(l):
        aside_own(l, m).start()

    def own_aside_late(l, late):
        pl.when(c % 2 == late)(lambda: own_aside(l))

    def flows(s, body):
        body(a >= s, jnp.maximum(a - s, 0), a + 1 < line, right)
        body(a + s < line, jnp.minimum(a + s, line - 1), a > 0, left)

    def step_along(l, s, g, both=False):
        def piece(there, z, on, dev):
            @pl.when(there)
            def _():
                along(l, z, g, dev).wait_recv()
                pl.when(on)(lambda: along(l, z, g, dev).start())
                if both:
                    aside(l, z, g).start()

        flows(s, piece)

    def step_aside(l, s, g):
        flows(s, lambda there, z, on, dev: pl.when(there)(lambda: aside(l, z, g).start()))

    def step_both(l, s, g):
        step_along(l, s, g, True)

    def own_cross(l):
        aside_own(l, m + 1 - 2 * b).wait_recv()
        pl.when(a + 1 < line)(lambda: across_line(l, a, right).start())
        pl.when(a > 0)(lambda: across_line(l, a, left).start())
        if straight_cross:
            pl.when(jnp.logical_or(a == 0, a + 1 == line))(
                lambda: across_line(l, a, opposite).start()
            )

    def step_cross(l, s):
        def piece(there, z, on, dev):
            if straight_cross:
                far_end = jnp.logical_or(
                    jnp.logical_and(z == 0, a + 2 == line), jnp.logical_and(z + 1 == line, a == 1)
                )
                on = jnp.logical_and(on, jnp.logical_not(far_end))

            @pl.when(there)
            def _():
                across_line(l, z, dev).wait_recv()
                pl.when(on)(lambda: across_line(l, z, dev).start())

        flows(s, piece)

    def gather_tasks(step, l):
        if line <= 8:
            return [
                functools.partial(step, l, s, g) for s in range(1, line) for g in range(pieces)
            ]

        def everything():
            def go(s):
                for g in range(pieces):
                    step(l, s, g)

            steps(1, line, go)

        return [everything]

    def cross_tasks(l):
        if line <= 8:
            return [functools.partial(own_cross, l)] + [
                functools.partial(step_cross, l, s) for s in range(1, line)
            ]
        return [
            functools.partial(own_cross, l),
            lambda: steps(1, line, lambda s: step_cross(l, s)),
        ]

    def rest_of(l):
        lanes = pl.ds(crossing(l), wide - crossing(l))
        view = wcat.at[pl.ds(0, line - 1), :, lanes]
        return remote(view, view, w_s.at[l, 1], wx_r.at[l, 0], beside)

    def gather_finish(l):
        rest_of(l).wait_recv()

    def gather_drain(l):
        rest_of(l).wait_send()
        aside_own(l, m).wait_send()
        inner = jnp.logical_and(a > 0, a + 1 < line)

        def lines(count):
            view = wcat.at[pl.ds(0, count)]
            remote(view, view, w_s.at[l, 0], wx_r.at[l, 0], beside).wait_send()

        def crossed(count):
            view = wcat.at[pl.ds(0, count), :, pl.ds(0, crossing(l))]
            remote(view, view, w_s.at[l, 3], wx_r.at[l, 0], beside).wait_send()

        for at, count in ((inner, line + 1), (jnp.logical_not(inner), 1)):
            pl.when(at)(functools.partial(lines, count))
        counts = (line, 2) if straight_cross else (line + 1, 1)
        for at, count in zip((inner, jnp.logical_not(inner)), counts):
            pl.when(at)(functools.partial(crossed, count))

    def stat_send(e):
        view = stat.at[e, m]

        def send(peer):
            remote(view, view, st_s.at[e], st_r.at[e], (peer, c)).start()

        def go(d):
            @pl.when(a + line - d < line)
            def _():
                first = jnp.minimum(a + line - d, line - 1) * 2
                send(first + 1 - b)
                send(first + b)

            @pl.when(a >= line - d)
            def _():
                first = jnp.maximum(a - line + d, 0) * 2
                send(first + 1 - b)
                send(first + b)

        steps(1, line, go)
        send(m + 1 - 2 * b)

    def stat_all(e):
        view = stat.at[e, pl.ds(0, maps - 1)]
        return remote(view, view, st_s.at[e], st_r.at[e], beside)

    def stat_wait(e):
        stat_all(e).wait_recv()

    def stat_drain(e):
        stat_all(e).wait_send()

    lane_own = pl.ds(pl.multiple_of(c * LANES, LANES), LANES)

    def lanes_of(owner):
        return pl.ds(pl.multiple_of(owner * LANES, LANES), LANES)

    def act_copy(l, n, owner, dev, place):
        rows = pl.ds(n * map_rows, map_rows)
        view = act.at[0, rows, lanes_of(owner)] if l == 0 else raw.at[l - 1, owner, rows]
        return remote(view, view, ag_s.at[l], ag_r.at[l, place], dev)

    def act_blocks(l, count, place):
        view = act.at[0, :, pl.ds(0, count * LANES)] if l == 0 else raw.at[l - 1, pl.ds(0, count)]
        return remote(view, view, ag_s.at[l], ag_r.at[l, place], (m, core))

    def act_send(l, n):
        act_copy(l, n, c, (m, far), n).start()
        act_copy(l, n, c, (m, core), nm).start()

    def act_forward(l, n):
        act_copy(l, n, far, (m, far), n).wait_recv()
        act_copy(l, n, far, (m, core), nm + 1).start()

    def act_near(l):
        act_blocks(l, 1, nm).wait_recv()

    def act_across(l):
        act_blocks(l, 1, nm + 1).wait_recv()

    def act_drain(l):
        act_blocks(l, 3, 0).wait_send()

    def scale_copy(l, owner, dev, ssem):
        view = scale_ref.at[l, owner]
        return remote(view, view, ssem, sc_r.at[l, owner], dev)

    def scale_send(l):
        for other in (core, far, across):
            scale_copy(l, c, (m, other), sc_s.at[l]).start()

    def scale_wait(l, owner):
        scale_copy(l, owner, (m, core), sc_s.at[l]).wait_recv()

    def scale_drain(l):
        view = scale_ref.at[l, pl.ds(0, 3)]
        remote(view, view, sc_s.at[l], sc_r.at[l, core], (m, core)).wait_send()

    own_along(0)
    own_aside(0)

    loads[2].wait()
    col_of = lax.broadcasted_iota(jnp.int32, (width, width), 0)
    diagonal = col_of == lax.broadcasted_iota(jnp.int32, (width, width), 1)
    for n in range(nm):

        @pl.loop(0, height)
        def _(h):
            line_n = jnp.broadcast_to(mask_in[h, n : n + 1, :].astype(F32), (width, width))
            r = pl.ds(pl.multiple_of(n * map_rows + h * width, 8), width)
            conv[r, 0:width] = jnp.where(diagonal, line_n, 0.0)

    mask_ref[...] = jnp.dot(
        conv[:, 0:width].astype(BF16), jnp.ones((width, LANES), BF16), preferred_element_type=F32
    )
    loads[1].wait()

    @pl.loop(0, chunks)
    def _(i):
        r = rows_of(i)
        act[0, r, lane_own] = (x_in[r, :].astype(F32) * mask_ref[r, :]).astype(BF16)

    for n in range(nm):
        act_send(0, n)

    for n in range(nm):
        for i in range(3):
            for j in range(3):
                prod[i, j, n, 0:PAD, :] = jnp.zeros((PAD, LANES), F32)
                prod[i, j, n, PAD + map_rows :, :] = jnp.zeros((PAD, LANES), F32)
        zpad[n, 0:PAD, :] = jnp.zeros((PAD, LANES), F32)
        zpad[n, PAD + map_rows :, :] = jnp.zeros((PAD, LANES), F32)

    col_chunk = lax.broadcasted_iota(jnp.int32, (6, width, LANES), 1).reshape(chunk, LANES)
    has_left = jnp.where(col_chunk > 0, 1.0, 0.0)
    has_right = jnp.where(col_chunk < width - 1, 1.0, 0.0)

    loads[3].wait()
    loads[4].wait()
    half_h, half_w = height // 2, width // 2

    @pl.loop(0, half_h)
    def _(h):
        pool32[...] = grad_in[h].astype(F32)
        for n in range(nm):
            pick = pl.ds(n, half_w, stride=nm)
            kept = index_in[h, pick, :]
            value = pool32[pick, :]
            base = n * map_rows + 2 * h * width
            for r in range(2):
                for s in range(2):
                    spread[pl.ds(base + r * width + s, half_w, stride=2), :] = jnp.where(
                        kept == 2 * r + s, value, 0.0
                    )

    tasks = gather_tasks(step_both, 0)
    z_tasks = {l: gather_tasks(step_along, l) for l in range(1, layers)}
    x_tasks = {l: gather_tasks(step_aside, l) for l in range(1, layers)}
    c_tasks = {l: cross_tasks(l) for l in range(layers)}
    with scope("gather0"):
        run(tasks, pieces)
        run(c_tasks[0], 1)
        run(tasks, pieces)
        if layers > 1:
            own_along(1)
        run(c_tasks[0], 1)
        run(tasks)
    if layers > 1:
        own_aside_late(1, 0)
    for n in range(nm):
        act_forward(0, n)
    if layers > 1:
        with scope("along_1"):
            run(z_tasks[1], pieces)
    with scope("gather0_cross"):
        run(c_tasks[0])
    with scope("gather0_end"):
        gather_finish(0)
    if layers > 1:
        own_aside_late(1, 1)
    act_near(0)
    act_across(0)
    for cp in loads[5:]:
        cp.wait()

    for l in range(layers):
        z_near, x_near = z_tasks.get(l + 1, []), x_tasks.get(l + 1, [])
        z_next = z_tasks.get(l + 2, [])

        kernel = wcat[l * maps : (l + 1) * maps, :, :].reshape(maps * rows_w, wide)
        for n in range(nm):
            out = jnp.dot(
                act[l, pl.ds(n * map_rows, map_rows), :], kernel, preferred_element_type=F32
            )
            for i in range(3):
                for j in range(3):
                    t = 3 * i + j
                    prod[i, j, n, PAD : PAD + map_rows, :] = out[:, t * LANES : (t + 1) * LANES]

        def conv_chunk(i, carry):
            total, count = carry
            r = rows_of(i)
            value = None
            for j in range(3):
                side = None
                for k in range(3):
                    n, pr = padded_rows(i, width * (k - 1) + (j - 1))
                    term = prod[k, j, n, pr, :]
                    side = term if side is None else side + term
                if j == 0:
                    side = side * has_left
                if j == 2:
                    side = side * has_right
                value = side if value is None else value + side
            conv[r, :] = value
            valid = mask_ref[r, :]
            return total + tile8(value * valid), count + tile8(valid)

        zero8 = jnp.zeros((8, LANES), F32)
        total, count = lax.fori_loop(0, chunks, conv_chunk, (zero8, zero8))
        total = jnp.sum(total, axis=0, keepdims=True)
        count = jnp.sum(count, axis=0, keepdims=True)
        mean = total / jnp.maximum(count, 1.0)

        def dev_chunk(i, carry):
            r = rows_of(i)
            delta = conv[r, :] - mean
            if l + 1 < layers:
                raw[l, c, r, :] = delta.astype(BF16)
            return carry + tile8(delta * delta * mask_ref[r, :])

        spread_sum = zero8
        for n in range(nm):
            spread_sum = lax.fori_loop(n * per_map, (n + 1) * per_map, dev_chunk, spread_sum)
            if l + 1 < layers:
                act_send(l + 1, n)
        spread_sum = jnp.sum(spread_sum, axis=0, keepdims=True)
        stat[l, m] = jnp.concatenate(
            [total, spread_sum, count, mean, jnp.zeros((4, LANES), F32)], axis=0
        )
        stat_send(l)
        with scope("gather_a"):
            run(x_near, len(x_near) - len(z_near))
            if len(z_near) > pieces:
                run(z_near, pieces)
                run(x_near, pieces)
        with scope("turn"):
            slots = LANES // rows_w
            for i in range(maps // slots):
                turned[l, :, i * LANES : (i + 1) * LANES] = (
                    wcat[l * maps + i * slots : l * maps + (i + 1) * slots, :, :].reshape(LANES, wide).T
                )
        if l + 1 < layers:
            with scope("gather_own_cross"):
                run(c_tasks[l + 1], 1)
                if l + 2 < layers:
                    own_along(l + 2)
        with scope("stat_wait"):
            stat_wait(l)

        def add_totals(s, carry):
            block = stat[l, s]
            return carry[0] + block[0:1, :], carry[1] + block[2:3, :]

        zero1 = jnp.zeros((1, LANES), F32)
        total, count = lax.fori_loop(0, maps, add_totals, (zero1, zero1))
        center = total / count

        def add_spread(s, carry):
            block = stat[l, s]
            delta = block[3:4, :] - center
            return carry + block[1:2, :] + block[2:3, :] * delta * delta

        variance = lax.fori_loop(0, maps, add_spread, zero1) / count
        inv_std = lax.rsqrt(variance + norm_epsilon)
        gain = gain_in[l : l + 1, :]
        bias = bias_in[l : l + 1, :]
        if l == 0:
            count_all = count
            scales = []
        scales.append(gain * inv_std)

        if l + 1 < layers:
            factor = gain * inv_std
            scale_ref[l, c] = jnp.concatenate(
                [factor, bias + factor * (mean - center), jnp.zeros((6, LANES), F32)], axis=0
            )
            scale_send(l)

        @pl.loop(0, chunks)
        def _(i):
            r = rows_of(i)
            unit = (conv[r, :] - center) * inv_std
            pre = gain * unit + bias
            sigma = 1.0 / (1.0 + jnp.exp(-pre))
            valid = mask_ref[r, :]
            result = pre * sigma * valid
            normed[l, r, :] = unit
            slope[l, r, :] = sigma * (1.0 + pre * (1.0 - sigma)) * valid
            if l + 1 < layers:
                act[l + 1, r, lane_own] = result.astype(BF16)
            else:
                result_ref[r, :] = result

        def activate(owner, first, last):
            pair = scale_ref[l, owner]
            factor, offset = pair[0:1, :], pair[1:2, :]
            lanes = lanes_of(owner)

            @pl.loop(first * per_map, last * per_map)
            def _(i):
                r = rows_of(i)
                pre = factor * raw[l, owner, r, :].astype(F32) + offset
                result = pre / (1.0 + jnp.exp(-pre)) * mask_ref[r, :]
                act[l + 1, r, lanes] = result.astype(BF16)

        if l + 1 < layers:
            with scope("act_near"):
                act_near(l + 1)
                scale_wait(l, core)
                activate(core, 0, nm)
            with scope("gather_b"):
                run(z_near)
                run(x_near)
                run(c_tasks[l + 1], 1)
            with scope("act_far"):
                for n in range(nm):
                    act_forward(l + 1, n)
                    if n == 0:
                        scale_wait(l, far)
                    activate(far, n, n + 1)
            with scope("gather_c"):
                run(c_tasks[l + 1], 1)
                if l + 2 < layers:
                    own_aside(l + 2)
                run(z_next, pieces)
            with scope("act_across"):
                act_across(l + 1)
                scale_wait(l, across)
                activate(across, 0, nm)
            with scope("gather_cross"):
                run(c_tasks[l + 1])
            with scope("gather_end"):
                gather_finish(l + 1)

    def pool():
        @pl.loop(0, half_h)
        def _(h):
            for n in range(nm):
                pick = pl.ds(n, half_w, stride=nm)
                kept = index_in[h, pick, :]
                base = n * map_rows + 2 * h * width
                total = jnp.zeros((half_w, LANES), F32)
                for r in range(2):
                    for s in range(2):
                        total = total + jnp.where(
                            kept == 2 * r + s,
                            result_ref[pl.ds(base + r * width + s, half_w, stride=2), :],
                            0.0,
                        )
                pool32[pick, :] = total
            pooled_ref[h] = pool32[...].astype(BF16)

    def place_of(k):
        before, after = a, line - 1 - a
        spare = jnp.maximum(before, after) - jnp.minimum(before, after)
        q = jnp.maximum(k - spare, 0)
        near, side = q // 2, q % 2
        low = jnp.where(before > after, spare, 0) + near
        high = line - 1 - jnp.where(before < after, spare, 0) - near
        outer = jnp.where(before > after, k, line - 1 - k)
        return jnp.where(k < spare, outer, jnp.where(side == 0, high, low))

    places = {False: [place_of(k) for k in range(line)] if line <= 8 else []}
    places[True] = list(places[False])
    if 2 < line <= 8:
        ends = jnp.logical_or(a == 0, a + 1 == line)
        places[True][0] = jnp.where(ends, places[False][1], places[False][0])
        places[True][1] = jnp.where(ends, places[False][0], places[False][1])

    def kth_place(k, l):
        return places[straight(l)][k] if line <= 8 else place_of(k)

    def part_of(g):
        return pl.ds(g * piece_rows, piece_rows)

    def gx_copy(l, z, g):
        return remote(
            gx_out.at[l, z, part_of(g)], gx_in.at[l, z, part_of(g)],
            gx_s.at[l], gx_r.at[l, z, g], beside,
        )

    def gz_copy(l, z, g, slot, dev):
        return remote(
            gz_out.at[l, z, part_of(g)], gz_in.at[l, slot, part_of(g)],
            gz_s.at[l], gz_r.at[l, slot, g], dev,
        )

    def shard(l, slot, g):
        first = pl.multiple_of(slot * rows_w, 8) + g * piece_rows
        return grad_w[l, pl.ds(first, piece_rows), :]

    tile = 2 * rows_w
    fine = tile % LANES == 0

    def kernel_grad(l, first, amount):
        rows = pl.ds(pl.multiple_of(first, LANES), amount)
        grad_w[l, rows, :] = lax.dot_general(
            act[l, :, rows], dcat[...], (((0,), (0,)), ((), ())), preferred_element_type=F32
        )

    def kernel_grads(l, low=0, high=None):
        high = line if high is None else high
        if not fine and low == 0:
            coarse = (maps * rows_w) // 4
            pl.loop(0, 4)(lambda i: kernel_grad(l, i * coarse, coarse))

        def go(k):
            z = kth_place(k, l)
            if fine:
                kernel_grad(l, z * tile, tile)
            for g in range(pieces):
                gx_out[l, z, part_of(g)] = shard(l, z * 2 + 1 - b, g).astype(BF16)
            for g in range(pieces):
                if line > 8 or is_early(l, k, g):
                    gx_copy(l, z, g).start()

        steps(low, high, go)

    def is_early(l, k, g):
        return l == 0 or k < 2

    def scatter_x(l):
        if line <= 8:
            for k in range(line):
                for g in range(pieces):
                    if not is_early(l, k, g):
                        gx_copy(l, kth_place(k, l), g).start()

    def pair_sum(l, z, g):
        gx_copy(l, z, g).wait_recv()
        return shard(l, z * 2 + b, g) + gx_in[l, z, part_of(g)].astype(F32)

    def onward(l, z, g, fed, dev, slot):
        value = pair_sum(l, z, g)
        if fed:
            gz_copy(l, z, g, z, dev).wait_recv()
            value = value + gz_in[l, z, part_of(g)].astype(F32)
        gz_out[l, z, part_of(g)] = value.astype(BF16)
        gz_copy(l, z, g, slot, dev).start()

    def straight(l):
        return l == 0 and 2 < line <= 8

    def scatter_step(l, d, g, fed):
        ends = straight(l) and d == line - 1
        zr, zl = jnp.minimum(a + d, line - 1), jnp.maximum(a - d, 0)
        more_r, more_l = a > 0, a + 1 < line
        if straight(l):
            more_r = jnp.where(zr == line - 1, a > 1, more_r)
            more_l = jnp.where(zl == 0, a + 2 < line, more_l)
        for there, z, more, dev, slot in (
            (a + d < line, zr, more_r, right, zr),
            (a >= d, zl, more_l, left, jnp.where(zl == a - 1, line, zl)),
        ):
            if ends:
                dev, slot = (z * 2 + b, c), line + 1
            now = jnp.logical_and(there, more if fed else jnp.logical_not(more))
            pl.when(now)(functools.partial(onward, l, z, g, fed, dev, slot))

    def scatter_own(l, g):
        r = part_of(g)
        total_w[r, :] = pair_sum(l, a, g)

        def add(slot):
            gz_copy(l, a, g, slot, left).wait_recv()
            total_w[r, :] += gz_in[l, slot, r].astype(F32)

        pl.when(a > 0)(lambda: add(a))
        pl.when(a + 1 < line)(lambda: add(line))
        if straight(l):
            pl.when(jnp.logical_or(a == 0, a + 1 == line))(lambda: add(line + 1))
        for t in range(taps):
            gradient = total_w[r, t * LANES : (t + 1) * LANES]
            new, first, second = adamw_update(
                weight_in[l, t, r], gradient, first_in[l, t, r], second_in[l, t, r], rate_conv
            )
            wgrad_ref[l, t, r] = gradient
            wfirst_ref[l, t, r] = first
            wsecond_ref[l, t, r] = second
            wnew_ref[l, t, r] = new
            wcopy_ref[l, t, r] = new.astype(BF16)

    def scatter_tasks(l):
        owns = [functools.partial(scatter_own, l, g) for g in range(pieces)]
        if line <= 8:
            first, fed = (
                [
                    functools.partial(scatter_step, l, line - e, g, kind)
                    for e in ((2, 1, *range(3, line)) if straight(l) else range(1, line))
                    if e > kind + (kind and straight(l))
                    for g in range(pieces)
                ]
                for kind in (False, True)
            )
            return first, fed, owns

        def everything():
            def go(e):
                for g in range(pieces):
                    scatter_step(l, line - e, g, False)
                    scatter_step(l, line - e, g, True)

            steps(1, line, go)

        return [everything], [], owns

    def scatter_drain(l):
        remote(gx_out.at[l], gx_in.at[l], gx_s.at[l], gx_r.at[l, 0, 0], beside).wait_send()
        view = pl.ds(0, line - 1)
        remote(
            gz_out.at[l, view], gz_in.at[l, view], gz_s.at[l], gz_r.at[l, 0, 0], beside
        ).wait_send()

    def layer_drain(l):
        stat_drain(layers + l)
        remote(pair_out.at[l], pair_in.at[l], pr_s.at[l], pr_r.at[l, 0], (m, core)).wait_send()
        remote(far_out.at[l], far_in.at[l], fr_s.at[l], fr_r.at[l, 0], (m, far)).wait_send()

    half = 2 * LANES
    own_half = (c // 2) * half
    other_half = half - own_half
    lane_in_half = pl.ds(pl.multiple_of((c % 2) * LANES, LANES), LANES)
    lane_out_half = pl.ds(pl.multiple_of((1 - c % 2) * LANES, LANES), LANES)

    def pair_copy(l, h, n):
        return remote(
            pair_out.at[l, h, pl.ds(n * map_rows, map_rows), :],
            pair_in.at[l, h, pl.ds(n * map_rows, map_rows), :],
            pr_s.at[l], pr_r.at[l, n if h == 0 else nm], (m, core),
        )

    def far_copy(l, n):
        return remote(
            far_out.at[l, pl.ds(n * map_rows, map_rows), :],
            far_in.at[l, pl.ds(n * map_rows, map_rows), :],
            fr_s.at[l], fr_r.at[l, n], (m, far),
        )

    todo, fed, owns = {}, {}, {}
    for l in reversed(range(layers)):
        e = layers + l
        source = spread if l == layers - 1 else back

        def slope_chunk(i, carry):
            r = rows_of(i)
            value = source[r, :] * slope[l, r, :]
            conv[r, :] = value
            return carry[0] + tile8(value * normed[l, r, :]), carry[1] + tile8(value)

        zero8 = jnp.zeros((8, LANES), F32)
        gain_sum, bias_sum = lax.fori_loop(0, chunks, slope_chunk, (zero8, zero8))
        stat[e, m] = jnp.concatenate(
            [
                jnp.sum(gain_sum, axis=0, keepdims=True),
                jnp.sum(bias_sum, axis=0, keepdims=True),
                jnp.zeros((6, LANES), F32),
            ],
            axis=0,
        )
        stat_send(e)
        if l + 1 < layers:
            scatter_x(l + 1)
        else:
            pool()
        if l + 1 < layers:
            todo[l + 1], fed[l + 1], owns[l + 1] = scatter_tasks(l + 1)
        if l + 2 < layers:
            run(todo[l + 2])
            run(fed[l + 2])
        if l + 1 < layers:
            with scope("scatter_a"):
                run(todo[l + 1], pieces if l > 0 else 2 * pieces)
        with scope("stat_wait_back"):
            stat_wait(e)

        def add_sums(s, carry):
            return carry + stat[e, s]

        sums = lax.fori_loop(0, maps, add_sums, jnp.zeros((8, LANES), F32))
        ngrad_ref[l] = sums[0:2, :]
        gain_grad = sums[0:1, :]
        bias_grad = sums[1:2, :]
        scale = scales[l]

        def conv_grad(n):
            @pl.loop(n * per_map, (n + 1) * per_map)
            def _(i):
                r = rows_of(i)
                value = (
                    mask_ref[r, :]
                    * scale
                    * (conv[r, :] - (bias_grad + normed[l, r, :] * gain_grad) / count_all)
                )
                pr = pl.ds(pl.multiple_of((i - n * per_map) * chunk, 16) + PAD, chunk)
                zpad[n, pr, :] = value

            @pl.loop(n * per_map, (n + 1) * per_map)
            def _(i):
                r = rows_of(i)
                for k in range(3):
                    for j in range(3):
                        shift = PAD - (width * (k - 1) + (j - 1))
                        pr = pl.ds(pl.multiple_of((i - n * per_map) * chunk, 16) + shift, chunk)
                        term = zpad[n, pr, :]
                        if j == 0:
                            term = term * has_right
                        if j == 2:
                            term = term * has_left
                        t = 3 * k + j
                        dcat[r, t * LANES : (t + 1) * LANES] = term.astype(BF16)

        def input_grad(h, first, last):
            start = other_half if h == 0 else own_half
            r = pl.ds(first * map_rows, (last - first) * map_rows)
            part[h, r, :] = jnp.dot(
                dcat[r, :], turned[l, :, pl.ds(pl.multiple_of(start, half), half)],
                preferred_element_type=F32,
            )
            pair_out[l, h, r, :] = part[h, r, lane_out_half].astype(BF16)
            for n in range(first, last):
                pair_copy(l, h, n).start()

        def to_far(n):
            r = pl.ds(n * map_rows, map_rows)
            pair_copy(l, 0, n).wait_recv()
            far_out[l, r, :] = (
                part[0, r, lane_in_half] + pair_in[l, 0, r, :].astype(F32)
            ).astype(BF16)
            far_copy(l, n).start()

        if l > 0:
            for n in range(nm):
                with scope("conv_grad"):
                    conv_grad(n)
                with scope("input_grad"):
                    input_grad(0, n, n + 1)
                if n > 0:
                    with scope("to_far"):
                        to_far(n - 1)
            if l + 1 < layers:
                with scope("scatter_b"):
                    run(todo[l + 1], pieces)
                    run(fed[l + 1], pieces)
            with scope("kernel_grad"):
                kernel_grads(l, 0, line // 2)
            with scope("to_far"):
                to_far(nm - 1)
            if l + 1 < layers:
                with scope("scatter_c"):
                    run(todo[l + 1])
            with scope("kernel_grad"):
                kernel_grads(l, line // 2)
            with scope("input_grad"):
                input_grad(1, 0, nm)
            with scope("drain"):
                if l + 1 == layers:
                    for k in range(layers):
                        gather_drain(k)
                        act_drain(k)
                        stat_drain(k)
                        if k + 1 < layers:
                            scale_drain(k)
                else:
                    layer_drain(l + 1)
        else:
            for n in range(nm):
                with scope("conv_grad"):
                    conv_grad(n)
            with scope("kernel_grad"):
                kernel_grads(0)
            todo[0], fed[0], owns[0] = scatter_tasks(0)
            with scope("scatter_1c"):
                run(todo[1])
                run(fed[1], pieces)
            with scope("input_grad"):
                input_grad(0, 0, nm)
            with scope("to_far"):
                for n in range(nm):
                    to_far(n)
            with scope("scatter_0a"):
                run(todo[0], pieces)
            with scope("scatter_1d"):
                run(fed[1])
            with scope("input_grad"):
                input_grad(1, 0, nm)
            with scope("scatter_0b"):
                run(todo[0], pieces)
            with scope("owns_2"):
                for k in range(layers - 1, 1, -1):
                    run(owns[k])

        for n in range(nm):
            r = pl.ds(n * map_rows, map_rows)
            with scope("far_wait"):
                if n == 0:
                    remote(
                        pair_out.at[l, 1], pair_in.at[l, 1], pr_s.at[l], pr_r.at[l, nm], (m, core)
                    ).wait_recv()
                far_copy(l, n).wait_recv()
            if n == 0 and l > 0 and l + 1 < layers:
                with scope("scatter_d"):
                    run(fed[l + 1])

            @pl.loop(n * per_map, (n + 1) * per_map)
            def _(i):
                r = rows_of(i)
                value = (
                    part[1, r, lane_in_half]
                    + pair_in[l, 1, r, :].astype(F32)
                    + far_in[l, r, :].astype(F32)
                )
                if l == 0:
                    value = value * mask_ref[r, :]
                back[r, :] = value

    with scope("norms"):
        for values, place in ((gain_in, 0), (bias_in, 1)):
            new, first, second = adamw_update(
                values[...], ngrad_ref[:, place, :], norm_first_in[:, place, :],
                norm_second_in[:, place, :], rate_norm,
            )
            nfirst_ref[:, place, :] = first
            nsecond_ref[:, place, :] = second
            nnew_ref[:, place, :] = new
    with scope("scatter_end"):
        run(todo[0])
        run(fed[0])
    with scope("owns_1"):
        for k in range(1, min(2, layers)):
            run(owns[k])
    with scope("drain"):
        for k in range(1, layers):
            scatter_drain(k)
        layer_drain(1)
    with scope("owns"):
        run(owns[0])

    with scope("drain_end"):
        layer_drain(0)
        scatter_drain(0)


def store_kernel(count, *refs):
    copies = [
        pltpu.make_async_copy(refs[i], refs[count + i], refs[2 * count].at[i]) for i in range(count)
    ]
    for cp in copies:
        cp.start()
    for cp in copies:
        cp.wait()


def store_results(results):
    any_spec = pl.BlockSpec(memory_space=pl.ANY)
    count = len(results)
    return pl.pallas_call(
        functools.partial(store_kernel, count),
        out_shape=tuple(jax.ShapeDtypeStruct(r.shape, r.dtype) for r in results),
        in_specs=[any_spec] * count,
        out_specs=(any_spec,) * count,
        scratch_shapes=[pltpu.SemaphoreType.DMA((count,))],
        compiler_params=pltpu.CompilerParams(vmem_limit_bytes=1 << 20),
    )(*results)


def block_call(maps, chans, x, mask, index, grad, weights, gain, bias, *moments):
    nm, height, width, lanes = x.shape
    layers, taps, rows_w, _ = weights.shape
    pixels = nm * height * width
    line = maps // 2
    wide = taps * LANES
    channels = chans * LANES
    map_rows = height * width
    sizes = (maps, chans, layers, taps, nm, height, width)
    pieces = 2 if rows_w % 32 == 0 else 1
    vm = pltpu.VMEM
    dma = pltpu.SemaphoreType.DMA
    hbm = pl.BlockSpec(memory_space=pltpu.HBM)
    scratch = [
        vm((pixels, LANES), BF16), vm(mask.shape, jnp.int32), vm(index.shape, jnp.int32),
        vm(grad.shape, BF16), vm(weights.shape, F32), vm(gain.shape, F32), vm(bias.shape, F32),
        *(vm(v.shape, F32) for v in moments),
        vm((pixels, LANES), F32),
        vm((layers * maps, rows_w, wide), BF16),
        vm((layers, wide, channels), BF16),
        vm((layers, pixels, channels), BF16),
        vm((layers - 1, chans, pixels, LANES), BF16),
        vm((layers - 1, chans, 8, LANES), F32),
        vm((3, 3, nm, map_rows + 2 * PAD, LANES), F32),
        vm((pixels, LANES), F32),
        vm((layers, pixels, LANES), F32),
        vm((layers, pixels, LANES), F32),
        vm((pixels, LANES), F32),
        vm((pixels, LANES), F32),
        vm((nm * (width // 2), LANES), F32),
        vm((nm, map_rows + 2 * PAD, LANES), F32),
        vm((pixels, wide), BF16),
        vm((layers, channels, wide), F32),
        vm((2, pixels, 2 * LANES), F32),
        vm((2 * layers, maps, 8, LANES), F32),
        vm((layers, 2, pixels, LANES), BF16), vm((layers, 2, pixels, LANES), BF16),
        vm((layers, pixels, LANES), BF16), vm((layers, pixels, LANES), BF16),
        vm((layers, line, rows_w, wide), BF16), vm((layers, line, rows_w, wide), BF16),
        vm((layers, line, rows_w, wide), BF16), vm((layers, line + 2, rows_w, wide), BF16),
        vm((rows_w, wide), F32),
        dma((11,)),
        dma((layers, 4)), dma((layers, line, pieces)), dma((layers, 2)), dma((layers, line)),
        dma((2 * layers,)), dma((2 * layers,)),
        dma((layers,)), dma((layers, nm + 2)),
        dma((layers - 1,)), dma((layers - 1, chans)),
        dma((layers,)), dma((layers, nm + 1)),
        dma((layers,)), dma((layers, nm)),
        dma((layers,)), dma((layers, line, pieces)),
        dma((layers,)), dma((layers, line + 2, pieces)),
    ]
    arrays = (
        [(index.shape, BF16), ((pixels, LANES), F32)]
        + [(weights.shape, F32)] * 4
        + [(weights.shape, BF16)]
        + [((layers, 2, LANES), F32)] * 4
    )
    return pl.pallas_call(
        functools.partial(block_kernel, sizes),
        out_shape=tuple(jax.ShapeDtypeStruct(*kind) for kind in arrays),
        in_specs=[hbm] * 11,
        out_specs=(pl.BlockSpec(memory_space=pltpu.VMEM),) * len(arrays),
        scratch_shapes=scratch,
        compiler_params=pltpu.CompilerParams(
            collective_id=0, has_side_effects=True, vmem_limit_bytes=48 << 20
        ),
    )(*(
        pltpu.with_memory_space_constraint(v, pltpu.HBM)
        for v in (x.reshape(pixels, LANES), mask, index, grad, weights, gain, bias, *moments)
    ))


def local(
    maps, chans,
    input_maps, valid_mask, pool_index, out_grad, conv_weights, weight_first, weight_second,
    norm_gain, norm_bias, norm_first, norm_second,
):
    nm, half_h, half_w, lanes = pool_index.shape
    by_row = (half_h, half_w * nm, lanes)
    pooled, image, *updates = store_results(
        block_call(
            maps, chans, input_maps, valid_mask.transpose(1, 0, 2),
            pool_index.transpose(1, 2, 0, 3).reshape(by_row),
            out_grad.transpose(1, 2, 0, 3).reshape(by_row),
            conv_weights, norm_gain, norm_bias, weight_first, weight_second, norm_first, norm_second,
        )
    )
    pooled = pooled.reshape(half_h, half_w, nm, lanes).transpose(2, 0, 1, 3)
    return (pooled, image.reshape(input_maps.shape), *updates)


def solution(mesh):
    return jax.shard_map(
        functools.partial(local, mesh.shape["maps"], mesh.shape["chan"]),
        mesh=mesh,
        in_specs=(
            P("maps", None, None, "chan"),
            P("maps", None, None),
            P("maps", None, None, "chan"),
            P("maps", None, None, "chan"),
            P(None, None, "maps", "chan"),
            P(None, None, "maps", "chan"),
            P(None, None, "maps", "chan"),
            P(None, "chan"),
            P(None, "chan"),
            P(None, None, "chan"),
            P(None, None, "chan"),
        ),
        out_specs=(
            P("maps", None, None, "chan"),
            P("maps", None, None, "chan"),
            P(None, None, "maps", "chan"),
            P(None, None, "maps", "chan"),
            P(None, None, "maps", "chan"),
            P(None, None, "maps", "chan"),
            P(None, None, "maps", "chan"),
            P(None, None, "chan"),
            P(None, None, "chan"),
            P(None, None, "chan"),
            P(None, None, "chan"),
        ),
        check_vma=False,
    )
```

```python
import functools

import jax
import jax.numpy as jnp
from jax import lax
from jax.experimental import pallas as pl
from jax.experimental.pallas import tpu as pltpu
from jax.sharding import PartitionSpec as P

beta_first = 0.5
beta_second = 0.5
rate_conv = 0.01
rate_norm = 0.2
decay_rate = 0.01
adam_epsilon = 1e-08
norm_epsilon = 1e-05
step_count = 5.0
first_scale = 1.0 / (1.0 - beta_first**step_count)
second_scale = 1.0 / (1.0 - beta_second**step_count)

MESH = pl.DeviceIdType.MESH
F32 = jnp.float32
BF16 = jnp.bfloat16
LANES = 128
PAD = 32


def adamw_update(parameter, gradient, first_moment, second_moment, step_rate):
    first_new = beta_first * first_moment + (1.0 - beta_first) * gradient
    second_new = beta_second * second_moment + (1.0 - beta_second) * gradient * gradient
    step = first_new * first_scale / (jnp.sqrt(second_new * second_scale) + adam_epsilon)
    return (parameter - step_rate * (step + decay_rate * parameter), first_new, second_new)


def steps(low, high, body):
    if high - low <= 8:
        for index in range(low, high):
            body(index)
    else:
        pl.loop(low, high)(body)


class scope:
    def __init__(self, name): pass
    def __enter__(self): return self
    def __exit__(self, *a): return False


def run(tasks, amount=None):
    for _ in range(len(tasks) if amount is None else min(amount, len(tasks))):
        tasks.pop(0)()


def grad_parts(layers, rows_w):
    pieces = 2 if rows_w % 32 == 0 else 1
    return [4 if l == 0 and rows_w % 64 == 0 else pieces for l in range(layers)]


def tile8(values):
    rows = values.shape[0]
    return jnp.sum(values.reshape(rows // 8, 8, LANES), axis=0)


def block_kernel(
    sizes,
    x_hbm, mask_hbm, index_hbm, grad_hbm, weight_hbm, gain_hbm, bias_hbm,
    first_hbm, second_hbm, norm_first_hbm, norm_second_hbm,
    pooled_ref, back, wgrad_ref, wfirst_ref, wsecond_ref, wnew_ref, wcopy_ref,
    ngrad_ref, nfirst_ref, nsecond_ref, nnew_ref,
    x_in, mask_in, index_in, grad_in, weight_in, gain_in, bias_in,
    first_in, second_in, norm_first_in, norm_second_in,
    mask_ref, wcat, turned, act, raw, scale_ref, prod, conv, normed, slope, result_ref, spread, pool32, zpad, dcat,
    grad_w, part, stat, pair_out, pair_in, far_out, far_in,
    gx_out, gx_in, gz_out, gz_in, total_w,
    in_sem,
    w_s, wz_r, wx_r, wc_r, st_s, st_r, ag_s, ag_r, sc_s, sc_r, pr_s, pr_r, fr_s, fr_r,
    gx_s, gx_r, gz_s, gz_r,
):
    maps, chans, layers, taps, nm, height, width = sizes
    line = maps // 2
    m = lax.axis_index("maps")
    c = lax.axis_index("chan")
    a = m // 2
    b = m % 2
    core = c + 1 - 2 * (c % 2)
    far = lax.rem(c + 2, 4)
    across = core + 2 - 4 * (core // 2)
    map_rows = height * width
    pixels = nm * map_rows
    rows_w = wcat.shape[1]
    wide = taps * LANES
    chunk = 6 * width
    chunks = pixels // chunk
    per_map = map_rows // chunk

    def rows_of(i):
        return pl.ds(pl.multiple_of(i * chunk, 16), chunk)

    def padded_rows(i, shift):
        n = i // per_map
        return n, pl.ds(pl.multiple_of((i - n * per_map) * chunk, 8) + (PAD + shift), chunk)

    def remote(src, dst, ssem, rsem, dev):
        return pltpu.make_async_remote_copy(
            src_ref=src, dst_ref=dst, send_sem=ssem, recv_sem=rsem,
            device_id=dev, device_id_type=MESH,
        )

    loads = []
    for i, (src, dst) in enumerate(
        (
            (weight_hbm, weight_in), (x_hbm, x_in), (mask_hbm, mask_in),
            (index_hbm, index_in), (grad_hbm, grad_in), (gain_hbm, gain_in), (bias_hbm, bias_in),
            (first_hbm, first_in), (second_hbm, second_in),
            (norm_first_hbm, norm_first_in), (norm_second_hbm, norm_second_in),
        )
    ):
        cp = pltpu.make_async_copy(src, dst, in_sem.at[i])
        cp.start()
        loads.append(cp)

    barrier = pltpu.get_barrier_semaphore()

    def greet(d):
        peer = lax.rem(m + d, maps)
        pl.semaphore_signal(barrier, inc=1, device_id=(peer, c), device_id_type=MESH)

    steps(1, maps, greet)
    for other in (core, far, across):
        pl.semaphore_signal(barrier, inc=1, device_id=(m, other), device_id_type=MESH)

    with scope("load"):
        loads[0].wait()
    for l in range(layers):
        for t in range(taps):
            wcat[l * maps + m, :, t * LANES : (t + 1) * LANES] = weight_in[l, t].astype(BF16)

    with scope("barrier"):
        pl.semaphore_wait(barrier, maps + 2)

    pieces = wz_r.shape[2]
    piece_rows = rows_w // pieces
    right = (jnp.minimum(m + 2, maps - 1), c)
    left = (jnp.maximum(m - 2, 0), c)
    beside = (m + 1 - 2 * b, c)
    opposite = ((line - 1 - a) * 2 + b, c)
    straight_cross = line == 4

    def crossing(l):
        return (1 if l == 0 else 2) * LANES

    def along(l, z, g, dev):
        view = wcat.at[l * maps + z * 2 + b, pl.ds(g * piece_rows, piece_rows)]
        return remote(view, view, w_s.at[l, 0], wz_r.at[l, z, g], dev)

    def aside(l, z, g):
        lanes = pl.ds(crossing(l), wide - crossing(l))
        view = wcat.at[l * maps + z * 2 + b, pl.ds(g * piece_rows, piece_rows), lanes]
        return remote(view, view, w_s.at[l, 1], wx_r.at[l, 0], beside)

    def aside_own(l, slot):
        view = wcat.at[l * maps + slot]
        return remote(view, view, w_s.at[l, 2], wx_r.at[l, 1], beside)

    def across_line(l, z, dev):
        view = wcat.at[l * maps + z * 2 + 1 - b, :, pl.ds(0, crossing(l))]
        return remote(view, view, w_s.at[l, 3], wc_r.at[l, z], dev)

    def own_along(l):
        for g in range(pieces):
            pl.when(a + 1 < line)(lambda: along(l, a, g, right).start())
            pl.when(a > 0)(lambda: along(l, a, g, left).start())

    def own_aside(l):
        aside_own(l, m).start()

    def own_aside_late(l, late):
        pl.when(c % 2 == late)(lambda: own_aside(l))

    def flows(s, body):
        body(a >= s, jnp.maximum(a - s, 0), a + 1 < line, right)
        body(a + s < line, jnp.minimum(a + s, line - 1), a > 0, left)

    def step_along(l, s, g, both=False):
        def piece(there, z, on, dev):
            @pl.when(there)
            def _():
                along(l, z, g, dev).wait_recv()
                pl.when(on)(lambda: along(l, z, g, dev).start())
                if both:
                    aside(l, z, g).start()

        flows(s, piece)

    def step_aside(l, s, g):
        flows(s, lambda there, z, on, dev: pl.when(there)(lambda: aside(l, z, g).start()))

    def step_both(l, s, g):
        step_along(l, s, g, True)

    def own_cross(l):
        aside_own(l, m + 1 - 2 * b).wait_recv()
        pl.when(a + 1 < line)(lambda: across_line(l, a, right).start())
        pl.when(a > 0)(lambda: across_line(l, a, left).start())
        if straight_cross:
            pl.when(jnp.logical_or(a == 0, a + 1 == line))(
                lambda: across_line(l, a, opposite).start()
            )

    def step_cross(l, s):
        def piece(there, z, on, dev):
            if straight_cross:
                far_end = jnp.logical_or(
                    jnp.logical_and(z == 0, a + 2 == line), jnp.logical_and(z + 1 == line, a == 1)
                )
                on = jnp.logical_and(on, jnp.logical_not(far_end))

            @pl.when(there)
            def _():
                across_line(l, z, dev).wait_recv()
                pl.when(on)(lambda: across_line(l, z, dev).start())

        flows(s, piece)

    def gather_tasks(step, l):
        if line <= 8:
            return [
                functools.partial(step, l, s, g) for s in range(1, line) for g in range(pieces)
            ]

        def everything():
            def go(s):
                for g in range(pieces):
                    step(l, s, g)

            steps(1, line, go)

        return [everything]

    def cross_tasks(l):
        if line <= 8:
            return [functools.partial(own_cross, l)] + [
                functools.partial(step_cross, l, s) for s in range(1, line)
            ]
        return [
            functools.partial(own_cross, l),
            lambda: steps(1, line, lambda s: step_cross(l, s)),
        ]

    def rest_of(l):
        lanes = pl.ds(crossing(l), wide - crossing(l))
        view = wcat.at[pl.ds(0, line - 1), :, lanes]
        return remote(view, view, w_s.at[l, 1], wx_r.at[l, 0], beside)

    def gather_finish(l):
        rest_of(l).wait_recv()

    def gather_drain(l):
        rest_of(l).wait_send()
        aside_own(l, m).wait_send()
        inner = jnp.logical_and(a > 0, a + 1 < line)

        def lines(count):
            view = wcat.at[pl.ds(0, count)]
            remote(view, view, w_s.at[l, 0], wx_r.at[l, 0], beside).wait_send()

        def crossed(count):
            view = wcat.at[pl.ds(0, count), :, pl.ds(0, crossing(l))]
            remote(view, view, w_s.at[l, 3], wx_r.at[l, 0], beside).wait_send()

        for at, count in ((inner, line + 1), (jnp.logical_not(inner), 1)):
            pl.when(at)(functools.partial(lines, count))
        counts = (line, 2) if straight_cross else (line + 1, 1)
        for at, count in zip((inner, jnp.logical_not(inner)), counts):
            pl.when(at)(functools.partial(crossed, count))

    def stat_send(e):
        view = stat.at[e, m]

        def send(peer):
            remote(view, view, st_s.at[e], st_r.at[e], (peer, c)).start()

        def go(d):
            @pl.when(a + line - d < line)
            def _():
                first = jnp.minimum(a + line - d, line - 1) * 2
                send(first + 1 - b)
                send(first + b)

            @pl.when(a >= line - d)
            def _():
                first = jnp.maximum(a - line + d, 0) * 2
                send(first + 1 - b)
                send(first + b)

        steps(1, line, go)
        send(m + 1 - 2 * b)

    def stat_all(e):
        view = stat.at[e, pl.ds(0, maps - 1)]
        return remote(view, view, st_s.at[e], st_r.at[e], beside)

    def stat_wait(e):
        stat_all(e).wait_recv()

    def stat_drain(e):
        stat_all(e).wait_send()

    lane_own = pl.ds(pl.multiple_of(c * LANES, LANES), LANES)

    def lanes_of(owner):
        return pl.ds(pl.multiple_of(owner * LANES, LANES), LANES)

    def act_copy(l, n, owner, dev, place):
        rows = pl.ds(n * map_rows, map_rows)
        view = act.at[0, rows, lanes_of(owner)] if l == 0 else raw.at[l - 1, owner, rows]
        return remote(view, view, ag_s.at[l], ag_r.at[l, place], dev)

    def act_blocks(l, count, place):
        view = act.at[0, :, pl.ds(0, count * LANES)] if l == 0 else raw.at[l - 1, pl.ds(0, count)]
        return remote(view, view, ag_s.at[l], ag_r.at[l, place], (m, core))

    def act_send(l, n):
        act_copy(l, n, c, (m, far), n).start()
        act_copy(l, n, c, (m, core), nm).start()

    def act_forward(l, n):
        act_copy(l, n, far, (m, far), n).wait_recv()
        act_copy(l, n, far, (m, core), nm + 1).start()

    def act_near(l):
        act_blocks(l, 1, nm).wait_recv()

    def act_across(l):
        act_blocks(l, 1, nm + 1).wait_recv()

    def act_drain(l):
        act_blocks(l, 3, 0).wait_send()

    def scale_copy(l, owner, dev, ssem):
        view = scale_ref.at[l, owner]
        return remote(view, view, ssem, sc_r.at[l, owner], dev)

    def scale_send(l):
        for other in (core, far, across):
            scale_copy(l, c, (m, other), sc_s.at[l]).start()

    def scale_wait(l, owner):
        scale_copy(l, owner, (m, core), sc_s.at[l]).wait_recv()

    def scale_drain(l):
        view = scale_ref.at[l, pl.ds(0, 3)]
        remote(view, view, sc_s.at[l], sc_r.at[l, core], (m, core)).wait_send()

    own_along(0)
    own_aside_late(0, 0)

    loads[2].wait()
    col_of = lax.broadcasted_iota(jnp.int32, (width, width), 0)
    diagonal = col_of == lax.broadcasted_iota(jnp.int32, (width, width), 1)
    for n in range(nm):

        @pl.loop(0, height)
        def _(h):
            line_n = jnp.broadcast_to(mask_in[h, n : n + 1, :].astype(F32), (width, width))
            r = pl.ds(pl.multiple_of(n * map_rows + h * width, 8), width)
            conv[r, 0:width] = jnp.where(diagonal, line_n, 0.0)

    mask_ref[...] = jnp.dot(
        conv[:, 0:width].astype(BF16), jnp.ones((width, LANES), BF16), preferred_element_type=F32
    )
    loads[1].wait()

    @pl.loop(0, chunks)
    def _(i):
        r = rows_of(i)
        act[0, r, lane_own] = (x_in[r, :].astype(F32) * mask_ref[r, :]).astype(BF16)

    for n in range(nm):
        act_send(0, n)

    own_aside_late(0, 1)

    for n in range(nm):
        for i in range(3):
            for j in range(3):
                prod[i, j, n, 0:PAD, :] = jnp.zeros((PAD, LANES), F32)
                prod[i, j, n, PAD + map_rows :, :] = jnp.zeros((PAD, LANES), F32)
        zpad[n, 0:PAD, :] = jnp.zeros((PAD, LANES), F32)
        zpad[n, PAD + map_rows :, :] = jnp.zeros((PAD, LANES), F32)

    col_chunk = lax.broadcasted_iota(jnp.int32, (6, width, LANES), 1).reshape(chunk, LANES)
    has_left = jnp.where(col_chunk > 0, 1.0, 0.0)
    has_right = jnp.where(col_chunk < width - 1, 1.0, 0.0)

    loads[3].wait()
    loads[4].wait()
    half_h, half_w = height // 2, width // 2

    @pl.loop(0, half_h)
    def _(h):
        pool32[...] = grad_in[h].astype(F32)
        for n in range(nm):
            pick = pl.ds(n, half_w, stride=nm)
            kept = index_in[h, pick, :]
            value = pool32[pick, :]
            base = n * map_rows + 2 * h * width
            for r in range(2):
                for s in range(2):
                    spread[pl.ds(base + r * width + s, half_w, stride=2), :] = jnp.where(
                        kept == 2 * r + s, value, 0.0
                    )

    tasks = gather_tasks(step_both, 0)
    z_tasks = {l: gather_tasks(step_along, l) for l in range(1, layers)}
    x_tasks = {l: gather_tasks(step_aside, l) for l in range(1, layers)}
    c_tasks = {l: cross_tasks(l) for l in range(layers)}
    with scope("gather0"):
        run(tasks, pieces)
        run(c_tasks[0], 1)
        run(tasks, pieces)
        if layers > 1:
            own_along(1)
        run(c_tasks[0], 1)
        run(tasks)
    if layers > 1:
        own_aside_late(1, 0)
    for n in range(nm):
        act_forward(0, n)
    if layers > 1:
        with scope("along_1"):
            run(z_tasks[1], pieces)
    with scope("gather0_cross"):
        run(c_tasks[0])
    with scope("gather0_end"):
        gather_finish(0)
    if layers > 1:
        own_aside_late(1, 1)
    act_near(0)
    act_across(0)
    for cp in loads[5:]:
        cp.wait()

    for l in range(layers):
        z_near, x_near = z_tasks.get(l + 1, []), x_tasks.get(l + 1, [])
        z_next = z_tasks.get(l + 2, [])

        kernel = wcat[l * maps : (l + 1) * maps, :, :].reshape(maps * rows_w, wide)
        for n in range(nm):
            out = jnp.dot(
                act[l, pl.ds(n * map_rows, map_rows), :], kernel, preferred_element_type=F32
            )
            for i in range(3):
                for j in range(3):
                    t = 3 * i + j
                    prod[i, j, n, PAD : PAD + map_rows, :] = out[:, t * LANES : (t + 1) * LANES]

        def conv_chunk(i, carry):
            total, count = carry
            r = rows_of(i)
            value = None
            for j in range(3):
                side = None
                for k in range(3):
                    n, pr = padded_rows(i, width * (k - 1) + (j - 1))
                    term = prod[k, j, n, pr, :]
                    side = term if side is None else side + term
                if j == 0:
                    side = side * has_left
                if j == 2:
                    side = side * has_right
                value = side if value is None else value + side
            conv[r, :] = value
            valid = mask_ref[r, :]
            return total + tile8(value * valid), count + tile8(valid)

        zero8 = jnp.zeros((8, LANES), F32)
        total, count = lax.fori_loop(0, chunks, conv_chunk, (zero8, zero8))
        total = jnp.sum(total, axis=0, keepdims=True)
        count = jnp.sum(count, axis=0, keepdims=True)
        mean = total / jnp.maximum(count, 1.0)

        def dev_chunk(i, carry):
            r = rows_of(i)
            delta = conv[r, :] - mean
            if l + 1 < layers:
                raw[l, c, r, :] = delta.astype(BF16)
            return carry + tile8(delta * delta * mask_ref[r, :])

        spread_sum = zero8
        for n in range(nm):
            spread_sum = lax.fori_loop(n * per_map, (n + 1) * per_map, dev_chunk, spread_sum)
            if l + 1 < layers:
                act_send(l + 1, n)
        spread_sum = jnp.sum(spread_sum, axis=0, keepdims=True)
        stat[l, m] = jnp.concatenate(
            [total, spread_sum, count, mean, jnp.zeros((4, LANES), F32)], axis=0
        )
        stat_send(l)
        with scope("gather_a"):
            run(x_near, len(x_near) - len(z_near))
            if len(z_near) > pieces:
                run(z_near, pieces)
                run(x_near, pieces)
        with scope("turn"):
            slots = LANES // rows_w
            for i, owner in enumerate((across, far, core, c)):
                rows = wcat[pl.ds(l * maps + owner * slots, slots), :, :].reshape(LANES, wide)
                turned[l, :, i * LANES : (i + 1) * LANES] = rows.T
        if l + 1 < layers:
            with scope("gather_own_cross"):
                run(c_tasks[l + 1], 1)
                if l + 2 < layers:
                    own_along(l + 2)
        with scope("stat_wait"):
            stat_wait(l)

        def add_totals(s, carry):
            block = stat[l, s]
            return carry[0] + block[0:1, :], carry[1] + block[2:3, :]

        zero1 = jnp.zeros((1, LANES), F32)
        total, count = lax.fori_loop(0, maps, add_totals, (zero1, zero1))
        center = total / count

        def add_spread(s, carry):
            block = stat[l, s]
            delta = block[3:4, :] - center
            return carry + block[1:2, :] + block[2:3, :] * delta * delta

        variance = lax.fori_loop(0, maps, add_spread, zero1) / count
        inv_std = lax.rsqrt(variance + norm_epsilon)
        gain = gain_in[l : l + 1, :]
        bias = bias_in[l : l + 1, :]
        if l == 0:
            count_all = count
            scales = []
        scales.append(gain * inv_std)

        if l + 1 < layers:
            factor = gain * inv_std
            scale_ref[l, c] = jnp.concatenate(
                [factor, bias + factor * (mean - center), jnp.zeros((6, LANES), F32)], axis=0
            )
            scale_send(l)

        def own_chunk(i, carry):
            r = rows_of(i)
            unit = (conv[r, :] - center) * inv_std
            pre = gain * unit + bias
            sigma = 1.0 / (1.0 + jnp.exp(-pre))
            valid = mask_ref[r, :]
            result = pre * sigma * valid
            slant = sigma * (1.0 + pre * (1.0 - sigma)) * valid
            normed[l, r, :] = unit
            if l + 1 < layers:
                slope[l, r, :] = slant
                act[l + 1, r, lane_own] = result.astype(BF16)
                return carry
            result_ref[r, :] = result
            value = spread[r, :] * slant
            conv[r, :] = value
            return carry[0] + tile8(value * unit), carry[1] + tile8(value)

        grad_sums = lax.fori_loop(0, chunks, own_chunk, (zero8, zero8))

        def activate(owner, first, last):
            pair = scale_ref[l, owner]
            factor, offset = pair[0:1, :], pair[1:2, :]
            lanes = lanes_of(owner)

            @pl.loop(first * per_map, last * per_map)
            def _(i):
                r = rows_of(i)
                pre = factor * raw[l, owner, r, :].astype(F32) + offset
                result = pre / (1.0 + jnp.exp(-pre)) * mask_ref[r, :]
                act[l + 1, r, lanes] = result.astype(BF16)

        if l + 1 < layers:
            with scope("act_near"):
                act_near(l + 1)
                scale_wait(l, core)
                activate(core, 0, nm)
            with scope("gather_b"):
                run(z_near)
                run(x_near)
                run(c_tasks[l + 1], 1)
            with scope("act_far"):
                for n in range(nm):
                    act_forward(l + 1, n)
                    if n == 0:
                        scale_wait(l, far)
                    activate(far, n, n + 1)
            with scope("gather_c"):
                run(c_tasks[l + 1], 1)
                if l + 2 < layers:
                    own_aside(l + 2)
                run(z_next, pieces)
            with scope("act_across"):
                act_across(l + 1)
                scale_wait(l, across)
                activate(across, 0, nm)
            with scope("gather_cross"):
                run(c_tasks[l + 1])
            with scope("gather_end"):
                gather_finish(l + 1)

    def pool():
        @pl.loop(0, half_h)
        def _(h):
            for n in range(nm):
                pick = pl.ds(n, half_w, stride=nm)
                kept = index_in[h, pick, :]
                base = n * map_rows + 2 * h * width
                total = jnp.zeros((half_w, LANES), F32)
                for r in range(2):
                    for s in range(2):
                        total = total + jnp.where(
                            kept == 2 * r + s,
                            result_ref[pl.ds(base + r * width + s, half_w, stride=2), :],
                            0.0,
                        )
                pool32[pick, :] = total
            pooled_ref[h] = pool32[...].astype(BF16)

    def place_of(k):
        before, after = a, line - 1 - a
        spare = jnp.maximum(before, after) - jnp.minimum(before, after)
        q = jnp.maximum(k - spare, 0)
        near, side = q // 2, q % 2
        low = jnp.where(before > after, spare, 0) + near
        high = line - 1 - jnp.where(before < after, spare, 0) - near
        outer = jnp.where(before > after, k, line - 1 - k)
        return jnp.where(k < spare, outer, jnp.where(side == 0, high, low))

    places = {False: [place_of(k) for k in range(line)] if line <= 8 else []}
    places[True] = list(places[False])
    if 2 < line <= 8:
        ends = jnp.logical_or(a == 0, a + 1 == line)
        places[True][0] = jnp.where(ends, places[False][1], places[False][0])
        places[True][1] = jnp.where(ends, places[False][0], places[False][1])

    def kth_place(k, l):
        return places[straight(l)][k] if line <= 8 else place_of(k)

    parts = grad_parts(layers, rows_w)

    def part_of(l, g):
        rows = rows_w // parts[l]
        return pl.ds(g * rows, rows)

    def gx_copy(l, z, g):
        return remote(
            gx_out.at[l, z, part_of(l, g)], gx_in.at[l, z, part_of(l, g)],
            gx_s.at[l], gx_r.at[line * sum(parts[:l]) + z * parts[l] + g], beside,
        )

    def gz_copy(l, z, g, slot, dev):
        return remote(
            gz_out.at[l, z, part_of(l, g)], gz_in.at[l, slot, part_of(l, g)],
            gz_s.at[l], gz_r.at[(line + 2) * sum(parts[:l]) + slot * parts[l] + g], dev,
        )

    def shard(l, slot, g):
        rows = rows_w // parts[l]
        first = pl.multiple_of(slot * rows_w, 8) + g * rows
        return grad_w[l, pl.ds(first, rows), :]

    tile = 2 * rows_w
    fine = tile % LANES == 0

    def kernel_grad(l, first, amount):
        rows = pl.ds(pl.multiple_of(first, LANES), amount)
        grad_w[l, rows, :] = lax.dot_general(
            act[l, :, rows], dcat[...], (((0,), (0,)), ((), ())), preferred_element_type=F32
        )

    def kernel_grads(l, low=0, high=None):
        high = line if high is None else high
        if not fine and low == 0:
            coarse = (maps * rows_w) // 4
            pl.loop(0, 4)(lambda i: kernel_grad(l, i * coarse, coarse))

        def go(k):
            z = kth_place(k, l)
            if fine:
                kernel_grad(l, z * tile, tile)
            for g in range(parts[l]):
                gx_out[l, z, part_of(l, g)] = shard(l, z * 2 + 1 - b, g).astype(BF16)
            if l == 0 and line <= 8 and k == line - 1 and layers > 1:
                for g in range(parts[1]):
                    if is_late(1, k, g):
                        gx_copy(1, a, g).start()
            for g in range(parts[l]):
                if line > 8 or is_early(l, k, g):
                    gx_copy(l, z, g).start()

        steps(low, high, go)

    def is_late(l, k, g):
        return l == 1 and line <= 8 and k == line - 1 and g >= (parts[l] + 1) // 2

    def is_early(l, k, g):
        return l == 0 or k < 2

    def scatter_x(l):
        if line <= 8:
            for k in range(line):
                for g in range(parts[l]):
                    if not is_early(l, k, g) and not is_late(l, k, g):
                        gx_copy(l, kth_place(k, l), g).start()

    def pair_sum(l, z, g):
        gx_copy(l, z, g).wait_recv()
        return shard(l, z * 2 + b, g) + gx_in[l, z, part_of(l, g)].astype(F32)

    def onward(l, z, g, fed, dev, slot):
        value = pair_sum(l, z, g)
        if fed:
            gz_copy(l, z, g, z, dev).wait_recv()
            value = value + gz_in[l, z, part_of(l, g)].astype(F32)
        gz_out[l, z, part_of(l, g)] = value.astype(BF16)
        gz_copy(l, z, g, slot, dev).start()

    def straight(l):
        return False

    def scatter_step(l, d, g, fed):
        ends = straight(l) and d == line - 1
        zr, zl = jnp.minimum(a + d, line - 1), jnp.maximum(a - d, 0)
        more_r, more_l = a > 0, a + 1 < line
        if straight(l):
            more_r = jnp.where(zr == line - 1, a > 1, more_r)
            more_l = jnp.where(zl == 0, a + 2 < line, more_l)
        for there, z, more, dev, slot in (
            (a + d < line, zr, more_r, right, zr),
            (a >= d, zl, more_l, left, jnp.where(zl == a - 1, line, zl)),
        ):
            if ends:
                dev, slot = (z * 2 + b, c), line + 1
            now = jnp.logical_and(there, more if fed else jnp.logical_not(more))
            pl.when(now)(functools.partial(onward, l, z, g, fed, dev, slot))

    def scatter_own(l, g):
        r = part_of(l, g)
        total_w[r, :] = pair_sum(l, a, g)

        def add(slot):
            gz_copy(l, a, g, slot, left).wait_recv()
            total_w[r, :] += gz_in[l, slot, r].astype(F32)

        pl.when(a > 0)(lambda: add(a))
        pl.when(a + 1 < line)(lambda: add(line))
        if straight(l):
            pl.when(jnp.logical_or(a == 0, a + 1 == line))(lambda: add(line + 1))
        for t in range(taps):
            gradient = total_w[r, t * LANES : (t + 1) * LANES]
            new, first, second = adamw_update(
                weight_in[l, t, r], gradient, first_in[l, t, r], second_in[l, t, r], rate_conv
            )
            wgrad_ref[l, t, r] = gradient
            wfirst_ref[l, t, r] = first
            wsecond_ref[l, t, r] = second
            wnew_ref[l, t, r] = new
            wcopy_ref[l, t, r] = new.astype(BF16)

    def scatter_tasks(l):
        owns = [functools.partial(scatter_own, l, g) for g in range(parts[l])]
        if line <= 8:
            first, fed = (
                [
                    functools.partial(scatter_step, l, line - e, g, kind)
                    for e in ((2, 1, *range(3, line)) if straight(l) else range(1, line))
                    if e > kind + (kind and straight(l))
                    for g in range(parts[l])
                ]
                for kind in (False, True)
            )
            return first, fed, owns

        def everything():
            def go(e):
                for g in range(parts[l]):
                    scatter_step(l, line - e, g, False)
                    scatter_step(l, line - e, g, True)

            steps(1, line, go)

        return [everything], [], owns

    def scatter_drain(l):
        remote(gx_out.at[l], gx_in.at[l], gx_s.at[l], gx_r.at[0], beside).wait_send()
        view = pl.ds(0, line - 1)
        remote(
            gz_out.at[l, view], gz_in.at[l, view], gz_s.at[l], gz_r.at[0], beside
        ).wait_send()

    def layer_drain(l):
        stat_drain(layers + l)
        remote(pair_out.at[l], pair_in.at[l], pr_s.at[l], pr_r.at[l, 0], (m, core)).wait_send()
        remote(far_out.at[l], far_in.at[l], fr_s.at[l], fr_r.at[l, 0], (m, far)).wait_send()

    half = 2 * LANES
    def pair_copy(l, h, n):
        return remote(
            pair_out.at[l, h, pl.ds(n * map_rows, map_rows), :],
            pair_in.at[l, h, pl.ds(n * map_rows, map_rows), :],
            pr_s.at[l], pr_r.at[l, n if h == 0 else nm], (m, core),
        )

    def far_copy(l, n):
        return remote(
            far_out.at[l, pl.ds(n * map_rows, map_rows), :],
            far_in.at[l, pl.ds(n * map_rows, map_rows), :],
            fr_s.at[l], fr_r.at[l, n], (m, far),
        )

    todo, fed, owns = {}, {}, {}
    for l in reversed(range(layers)):
        e = layers + l
        gain_sum, bias_sum = grad_sums
        stat[e, m] = jnp.concatenate(
            [
                jnp.sum(gain_sum, axis=0, keepdims=True),
                jnp.sum(bias_sum, axis=0, keepdims=True),
                jnp.zeros((6, LANES), F32),
            ],
            axis=0,
        )
        stat_send(e)
        if l + 1 < layers:
            scatter_x(l + 1)
        else:
            pool()
        if l + 1 < layers:
            todo[l + 1], fed[l + 1], owns[l + 1] = scatter_tasks(l + 1)
        if l + 2 < layers:
            run(todo[l + 2])
            run(fed[l + 2])
        if l + 1 < layers:
            with scope("scatter_a"):
                run(todo[l + 1], parts[l + 1] if l > 0 else 2 * parts[l + 1])
        with scope("stat_wait_back"):
            stat_wait(e)

        def add_sums(s, carry):
            return carry + stat[e, s]

        sums = lax.fori_loop(0, maps, add_sums, jnp.zeros((8, LANES), F32))
        ngrad_ref[l] = sums[0:2, :]
        gain_grad = sums[0:1, :]
        bias_grad = sums[1:2, :]
        scale = scales[l]

        def conv_grad(n):
            @pl.loop(n * per_map, (n + 1) * per_map)
            def _(i):
                r = rows_of(i)
                value = (
                    mask_ref[r, :]
                    * scale
                    * (conv[r, :] - (bias_grad + normed[l, r, :] * gain_grad) / count_all)
                )
                pr = pl.ds(pl.multiple_of((i - n * per_map) * chunk, 16) + PAD, chunk)
                zpad[n, pr, :] = value

            @pl.loop(n * per_map, (n + 1) * per_map)
            def _(i):
                r = rows_of(i)
                for k in range(3):
                    for j in range(3):
                        shift = PAD - (width * (k - 1) + (j - 1))
                        pr = pl.ds(pl.multiple_of((i - n * per_map) * chunk, 16) + shift, chunk)
                        term = zpad[n, pr, :]
                        if j == 0:
                            term = term * has_right
                        if j == 2:
                            term = term * has_left
                        t = 3 * k + j
                        dcat[r, t * LANES : (t + 1) * LANES] = term.astype(BF16)

        def input_grad(h, first, last):
            r = pl.ds(first * map_rows, (last - first) * map_rows)
            out = jnp.dot(
                dcat[r, :], turned[l, :, h * half : (h + 1) * half], preferred_element_type=F32
            )
            pair_out[l, h, r, :] = out[:, :LANES].astype(BF16)
            for n in range(first, last):
                pair_copy(l, h, n).start()
            part[h, r, :] = out[:, LANES:]

        def to_far(n):
            r = pl.ds(n * map_rows, map_rows)
            pair_copy(l, 0, n).wait_recv()
            far_out[l, r, :] = (part[0, r, :] + pair_in[l, 0, r, :].astype(F32)).astype(BF16)
            far_copy(l, n).start()

        if l > 0:
            for n in range(nm):
                with scope("conv_grad"):
                    conv_grad(n)
                with scope("input_grad"):
                    input_grad(0, n, n + 1)
                if n > 0:
                    with scope("to_far"):
                        to_far(n - 1)
            if l + 1 < layers:
                with scope("scatter_b"):
                    run(todo[l + 1], parts[l + 1])
                    run(fed[l + 1], parts[l + 1])
            with scope("kernel_grad"):
                kernel_grads(l, 0, line // 2)
            with scope("to_far"):
                to_far(nm - 1)
            if l + 1 < layers:
                with scope("scatter_c"):
                    run(todo[l + 1])
            with scope("kernel_grad"):
                kernel_grads(l, line // 2)
            with scope("input_grad"):
                input_grad(1, 0, nm)
            with scope("drain"):
                if l + 1 == layers:
                    for k in range(layers):
                        gather_drain(k)
                        act_drain(k)
                        stat_drain(k)
                        if k + 1 < layers:
                            scale_drain(k)
                else:
                    layer_drain(l + 1)
        else:
            for n in range(nm):
                with scope("conv_grad"):
                    conv_grad(n)
            with scope("kernel_grad"):
                kernel_grads(0)
            todo[0], fed[0], owns[0] = scatter_tasks(0)
            with scope("scatter_1c"):
                run(todo[1])
                run(fed[1], parts[1])
            with scope("input_grad"):
                input_grad(0, 0, nm)
            with scope("to_far"):
                for n in range(nm):
                    to_far(n)
            with scope("scatter_0a"):
                run(todo[0], parts[0])
            with scope("scatter_1d"):
                run(fed[1])
            with scope("input_grad"):
                input_grad(1, 0, nm)
            with scope("scatter_0b"):
                run(todo[0], parts[0])
                run(fed[0], parts[0])
            with scope("owns_2"):
                for k in range(layers - 1, 1, -1):
                    run(owns[k])

        zero8 = jnp.zeros((8, LANES), F32)
        grad_sums = (zero8, zero8)
        for n in range(nm):
            r = pl.ds(n * map_rows, map_rows)
            with scope("far_wait"):
                if n == 0:
                    remote(
                        pair_out.at[l, 1], pair_in.at[l, 1], pr_s.at[l], pr_r.at[l, nm], (m, core)
                    ).wait_recv()
                far_copy(l, n).wait_recv()
            if n == 0 and l > 0 and l + 1 < layers:
                with scope("scatter_d"):
                    run(fed[l + 1])

            def back_chunk(i, carry):
                r = rows_of(i)
                value = part[1, r, :] + pair_in[l, 1, r, :].astype(F32) + far_in[l, r, :].astype(F32)
                if l == 0:
                    back[r, :] = value * mask_ref[r, :]
                    return carry
                value = value * slope[l - 1, r, :]
                conv[r, :] = value
                return carry[0] + tile8(value * normed[l - 1, r, :]), carry[1] + tile8(value)

            grad_sums = lax.fori_loop(n * per_map, (n + 1) * per_map, back_chunk, grad_sums)

    with scope("norms"):
        for values, place in ((gain_in, 0), (bias_in, 1)):
            new, first, second = adamw_update(
                values[...], ngrad_ref[:, place, :], norm_first_in[:, place, :],
                norm_second_in[:, place, :], rate_norm,
            )
            nfirst_ref[:, place, :] = first
            nsecond_ref[:, place, :] = second
            nnew_ref[:, place, :] = new
    with scope("scatter_end"):
        run(todo[0])
        run(fed[0])
    with scope("owns_1"):
        for k in range(1, min(2, layers)):
            run(owns[k])
    with scope("drain"):
        for k in range(1, layers):
            scatter_drain(k)
        layer_drain(1)
    with scope("owns"):
        run(owns[0])

    with scope("drain_end"):
        layer_drain(0)
        scatter_drain(0)


def store_kernel(count, *refs):
    copies = [
        pltpu.make_async_copy(refs[i], refs[count + i], refs[2 * count].at[i]) for i in range(count)
    ]
    for cp in copies:
        cp.start()
    for cp in copies:
        cp.wait()


def store_results(results):
    any_spec = pl.BlockSpec(memory_space=pl.ANY)
    count = len(results)
    return pl.pallas_call(
        functools.partial(store_kernel, count),
        out_shape=tuple(jax.ShapeDtypeStruct(r.shape, r.dtype) for r in results),
        in_specs=[any_spec] * count,
        out_specs=(any_spec,) * count,
        scratch_shapes=[pltpu.SemaphoreType.DMA((count,))],
        compiler_params=pltpu.CompilerParams(vmem_limit_bytes=1 << 20),
    )(*results)


def block_call(maps, chans, x, mask, index, grad, weights, gain, bias, *moments):
    nm, height, width, lanes = x.shape
    layers, taps, rows_w, _ = weights.shape
    pixels = nm * height * width
    line = maps // 2
    wide = taps * LANES
    channels = chans * LANES
    map_rows = height * width
    sizes = (maps, chans, layers, taps, nm, height, width)
    pieces = 2 if rows_w % 32 == 0 else 1
    vm = pltpu.VMEM
    dma = pltpu.SemaphoreType.DMA
    hbm = pl.BlockSpec(memory_space=pltpu.HBM)
    scratch = [
        vm((pixels, LANES), BF16), vm(mask.shape, jnp.int32), vm(index.shape, jnp.int32),
        vm(grad.shape, BF16), vm(weights.shape, F32), vm(gain.shape, F32), vm(bias.shape, F32),
        *(vm(v.shape, F32) for v in moments),
        vm((pixels, LANES), F32),
        vm((layers * maps, rows_w, wide), BF16),
        vm((layers, wide, channels), BF16),
        vm((layers, pixels, channels), BF16),
        vm((layers - 1, chans, pixels, LANES), BF16),
        vm((layers - 1, chans, 8, LANES), F32),
        vm((3, 3, nm, map_rows + 2 * PAD, LANES), F32),
        vm((pixels, LANES), F32),
        vm((layers, pixels, LANES), F32),
        vm((layers, pixels, LANES), F32),
        vm((pixels, LANES), F32),
        vm((pixels, LANES), F32),
        vm((nm * (width // 2), LANES), F32),
        vm((nm, map_rows + 2 * PAD, LANES), F32),
        vm((pixels, wide), BF16),
        vm((layers, channels, wide), F32),
        vm((2, pixels, LANES), F32),
        vm((2 * layers, maps, 8, LANES), F32),
        vm((layers, 2, pixels, LANES), BF16), vm((layers, 2, pixels, LANES), BF16),
        vm((layers, pixels, LANES), BF16), vm((layers, pixels, LANES), BF16),
        vm((layers, line, rows_w, wide), BF16), vm((layers, line, rows_w, wide), BF16),
        vm((layers, line, rows_w, wide), BF16), vm((layers, line + 2, rows_w, wide), BF16),
        vm((rows_w, wide), F32),
        dma((11,)),
        dma((layers, 4)), dma((layers, line, pieces)), dma((layers, 2)), dma((layers, line)),
        dma((2 * layers,)), dma((2 * layers,)),
        dma((layers,)), dma((layers, nm + 2)),
        dma((layers - 1,)), dma((layers - 1, chans)),
        dma((layers,)), dma((layers, nm + 1)),
        dma((layers,)), dma((layers, nm)),
        dma((layers,)), dma((line * sum(grad_parts(layers, rows_w)),)),
        dma((layers,)), dma(((line + 2) * sum(grad_parts(layers, rows_w)),)),
    ]
    arrays = (
        [(index.shape, BF16), ((pixels, LANES), F32)]
        + [(weights.shape, F32)] * 4
        + [(weights.shape, BF16)]
        + [((layers, 2, LANES), F32)] * 4
    )
    return pl.pallas_call(
        functools.partial(block_kernel, sizes),
        out_shape=tuple(jax.ShapeDtypeStruct(*kind) for kind in arrays),
        in_specs=[hbm] * 11,
        out_specs=(pl.BlockSpec(memory_space=pltpu.VMEM),) * len(arrays),
        scratch_shapes=scratch,
        compiler_params=pltpu.CompilerParams(
            collective_id=0, has_side_effects=True, vmem_limit_bytes=48 << 20
        ),
    )(*(
        pltpu.with_memory_space_constraint(v, pltpu.HBM)
        for v in (x.reshape(pixels, LANES), mask, index, grad, weights, gain, bias, *moments)
    ))


def local(
    maps, chans,
    input_maps, valid_mask, pool_index, out_grad, conv_weights, weight_first, weight_second,
    norm_gain, norm_bias, norm_first, norm_second,
):
    nm, half_h, half_w, lanes = pool_index.shape
    by_row = (half_h, half_w * nm, lanes)
    pooled, image, *updates = store_results(
        block_call(
            maps, chans, input_maps, valid_mask.transpose(1, 0, 2),
            pool_index.transpose(1, 2, 0, 3).reshape(by_row),
            out_grad.transpose(1, 2, 0, 3).reshape(by_row),
            conv_weights, norm_gain, norm_bias, weight_first, weight_second, norm_first, norm_second,
        )
    )
    pooled = pooled.reshape(half_h, half_w, nm, lanes).transpose(2, 0, 1, 3)
    return (pooled, image.reshape(input_maps.shape), *updates)


def solution(mesh):
    return jax.shard_map(
        functools.partial(local, mesh.shape["maps"], mesh.shape["chan"]),
        mesh=mesh,
        in_specs=(
            P("maps", None, None, "chan"),
            P("maps", None, None),
            P("maps", None, None, "chan"),
            P("maps", None, None, "chan"),
            P(None, None, "maps", "chan"),
            P(None, None, "maps", "chan"),
            P(None, None, "maps", "chan"),
            P(None, "chan"),
            P(None, "chan"),
            P(None, None, "chan"),
            P(None, None, "chan"),
        ),
        out_specs=(
            P("maps", None, None, "chan"),
            P("maps", None, None, "chan"),
            P(None, None, "maps", "chan"),
            P(None, None, "maps", "chan"),
            P(None, None, "maps", "chan"),
            P(None, None, "maps", "chan"),
            P(None, None, "maps", "chan"),
            P(None, None, "chan"),
            P(None, None, "chan"),
            P(None, None, "chan"),
            P(None, None, "chan"),
        ),
        check_vma=False,
    )
```

```python
import functools

import jax
import jax.numpy as jnp
from jax import lax
from jax.experimental import pallas as pl
from jax.experimental.pallas import tpu as pltpu
from jax.sharding import PartitionSpec as P

beta_first = 0.5
beta_second = 0.5
rate_conv = 0.01
rate_norm = 0.2
decay_rate = 0.01
adam_epsilon = 1e-08
norm_epsilon = 1e-05
step_count = 5.0
first_scale = 1.0 / (1.0 - beta_first**step_count)
second_scale = 1.0 / (1.0 - beta_second**step_count)

MESH = pl.DeviceIdType.MESH
F32 = jnp.float32
BF16 = jnp.bfloat16
LANES = 128
PAD = 32


def adamw_update(parameter, gradient, first_moment, second_moment, step_rate):
    first_new = beta_first * first_moment + (1.0 - beta_first) * gradient
    second_new = beta_second * second_moment + (1.0 - beta_second) * gradient * gradient
    step = first_new * first_scale / (jnp.sqrt(second_new * second_scale) + adam_epsilon)
    return (parameter - step_rate * (step + decay_rate * parameter), first_new, second_new)


def steps(low, high, body):
    if high - low <= 8:
        for index in range(low, high):
            body(index)
    else:
        pl.loop(low, high)(body)


class scope:
    def __init__(self, name): pass
    def __enter__(self): return self
    def __exit__(self, *a): return False


def run(tasks, amount=None):
    for _ in range(len(tasks) if amount is None else min(amount, len(tasks))):
        tasks.pop(0)()


def grad_parts(layers, rows_w):
    pieces = 2 if rows_w % 32 == 0 else 1
    return [4 if l == 0 and rows_w % 64 == 0 else pieces for l in range(layers)]


def tile8(values):
    rows = values.shape[0]
    return jnp.sum(values.reshape(rows // 8, 8, LANES), axis=0)


def block_kernel(
    sizes,
    x_hbm, mask_hbm, index_hbm, grad_hbm, weight_hbm, gain_hbm, bias_hbm,
    first_hbm, second_hbm, norm_first_hbm, norm_second_hbm,
    pooled_ref, back, wgrad_ref, wfirst_ref, wsecond_ref, wnew_ref, wcopy_ref,
    ngrad_ref, nfirst_ref, nsecond_ref, nnew_ref,
    x_in, mask_in, index_in, grad_in, weight_in, gain_in, bias_in,
    first_in, second_in, norm_first_in, norm_second_in,
    mask_ref, wcat, turned, act, raw, scale_ref, prod, conv, normed, slope, result_ref, spread, pool32, zpad, dcat,
    grad_w, part, stat, pair_out, pair_in, far_out, far_in,
    gx_out, gx_in, gz_out, gz_in, total_w,
    in_sem,
    w_s, wz_r, wx_r, wc_r, st_s, st_r, ag_s, ag_r, sc_s, sc_r, pr_s, pr_r, fr_s, fr_r,
    gx_s, gx_r, gz_s, gz_r,
):
    maps, chans, layers, taps, nm, height, width = sizes
    line = maps // 2
    m = lax.axis_index("maps")
    c = lax.axis_index("chan")
    a = m // 2
    b = m % 2
    core = c + 1 - 2 * (c % 2)
    far = lax.rem(c + 2, 4)
    across = core + 2 - 4 * (core // 2)
    map_rows = height * width
    pixels = nm * map_rows
    rows_w = wcat.shape[1]
    wide = taps * LANES
    chunk = 6 * width
    chunks = pixels // chunk
    per_map = map_rows // chunk

    def rows_of(i):
        return pl.ds(pl.multiple_of(i * chunk, 16), chunk)

    def padded_rows(i, shift):
        n = i // per_map
        return n, pl.ds(pl.multiple_of((i - n * per_map) * chunk, 8) + (PAD + shift), chunk)

    def remote(src, dst, ssem, rsem, dev):
        return pltpu.make_async_remote_copy(
            src_ref=src, dst_ref=dst, send_sem=ssem, recv_sem=rsem,
            device_id=dev, device_id_type=MESH,
        )

    loads = []
    for i, (src, dst) in enumerate(
        (
            (weight_hbm, weight_in), (x_hbm, x_in), (mask_hbm, mask_in),
            (index_hbm, index_in), (grad_hbm, grad_in), (gain_hbm, gain_in), (bias_hbm, bias_in),
            (first_hbm, first_in), (second_hbm, second_in),
            (norm_first_hbm, norm_first_in), (norm_second_hbm, norm_second_in),
        )
    ):
        cp = pltpu.make_async_copy(src, dst, in_sem.at[i])
        cp.start()
        loads.append(cp)

    barrier = pltpu.get_barrier_semaphore()

    def greet(d):
        peer = lax.rem(m + d, maps)
        pl.semaphore_signal(barrier, inc=1, device_id=(peer, c), device_id_type=MESH)

    steps(1, maps, greet)
    for other in (core, far, across):
        pl.semaphore_signal(barrier, inc=1, device_id=(m, other), device_id_type=MESH)

    with scope("load"):
        loads[0].wait()
    for l in range(layers):
        for t in range(taps):
            wcat[l * maps + m, :, t * LANES : (t + 1) * LANES] = weight_in[l, t].astype(BF16)

    with scope("barrier"):
        pl.semaphore_wait(barrier, maps + 2)

    pieces = wz_r.shape[2]
    piece_rows = rows_w // pieces
    right = (jnp.minimum(m + 2, maps - 1), c)
    left = (jnp.maximum(m - 2, 0), c)
    beside = (m + 1 - 2 * b, c)
    opposite = ((line - 1 - a) * 2 + b, c)
    straight_cross = line == 4

    def crossing(l):
        return (1 if l == 0 else 2) * LANES

    def along(l, z, g, dev):
        view = wcat.at[l * maps + z * 2 + b, pl.ds(g * piece_rows, piece_rows)]
        return remote(view, view, w_s.at[l, 0], wz_r.at[l, z, g], dev)

    def aside(l, z, g):
        lanes = pl.ds(crossing(l), wide - crossing(l))
        view = wcat.at[l * maps + z * 2 + b, pl.ds(g * piece_rows, piece_rows), lanes]
        return remote(view, view, w_s.at[l, 1], wx_r.at[l, 0], beside)

    def aside_own(l, slot):
        view = wcat.at[l * maps + slot]
        return remote(view, view, w_s.at[l, 2], wx_r.at[l, 1], beside)

    def across_line(l, z, dev):
        view = wcat.at[l * maps + z * 2 + 1 - b, :, pl.ds(0, crossing(l))]
        return remote(view, view, w_s.at[l, 3], wc_r.at[l, z], dev)

    def own_along(l):
        for g in range(pieces):
            pl.when(a + 1 < line)(lambda: along(l, a, g, right).start())
            pl.when(a > 0)(lambda: along(l, a, g, left).start())

    def own_aside(l):
        aside_own(l, m).start()

    def own_aside_late(l, late):
        pl.when(c % 2 == late)(lambda: own_aside(l))

    def flows(s, body):
        body(a >= s, jnp.maximum(a - s, 0), a + 1 < line, right)
        body(a + s < line, jnp.minimum(a + s, line - 1), a > 0, left)

    def step_along(l, s, g, both=False):
        def piece(there, z, on, dev):
            @pl.when(there)
            def _():
                along(l, z, g, dev).wait_recv()
                pl.when(on)(lambda: along(l, z, g, dev).start())
                if both:
                    aside(l, z, g).start()

        flows(s, piece)

    def step_aside(l, s, g):
        flows(s, lambda there, z, on, dev: pl.when(there)(lambda: aside(l, z, g).start()))

    def step_both(l, s, g):
        step_along(l, s, g, True)

    def own_cross(l):
        aside_own(l, m + 1 - 2 * b).wait_recv()
        pl.when(a + 1 < line)(lambda: across_line(l, a, right).start())
        pl.when(a > 0)(lambda: across_line(l, a, left).start())
        if straight_cross:
            pl.when(jnp.logical_or(a == 0, a + 1 == line))(
                lambda: across_line(l, a, opposite).start()
            )

    def step_cross(l, s):
        def piece(there, z, on, dev):
            if straight_cross:
                far_end = jnp.logical_or(
                    jnp.logical_and(z == 0, a + 2 == line), jnp.logical_and(z + 1 == line, a == 1)
                )
                on = jnp.logical_and(on, jnp.logical_not(far_end))

            @pl.when(there)
            def _():
                across_line(l, z, dev).wait_recv()
                pl.when(on)(lambda: across_line(l, z, dev).start())

        flows(s, piece)

    def gather_tasks(step, l):
        if line <= 8:
            return [
                functools.partial(step, l, s, g) for s in range(1, line) for g in range(pieces)
            ]

        def everything():
            def go(s):
                for g in range(pieces):
                    step(l, s, g)

            steps(1, line, go)

        return [everything]

    def cross_tasks(l):
        if line <= 8:
            return [functools.partial(own_cross, l)] + [
                functools.partial(step_cross, l, s) for s in range(1, line)
            ]
        return [
            functools.partial(own_cross, l),
            lambda: steps(1, line, lambda s: step_cross(l, s)),
        ]

    def rest_of(l):
        lanes = pl.ds(crossing(l), wide - crossing(l))
        view = wcat.at[pl.ds(0, line - 1), :, lanes]
        return remote(view, view, w_s.at[l, 1], wx_r.at[l, 0], beside)

    def gather_finish(l):
        rest_of(l).wait_recv()

    def gather_drain(l):
        rest_of(l).wait_send()
        aside_own(l, m).wait_send()
        inner = jnp.logical_and(a > 0, a + 1 < line)

        def lines(count):
            view = wcat.at[pl.ds(0, count)]
            remote(view, view, w_s.at[l, 0], wx_r.at[l, 0], beside).wait_send()

        def crossed(count):
            view = wcat.at[pl.ds(0, count), :, pl.ds(0, crossing(l))]
            remote(view, view, w_s.at[l, 3], wx_r.at[l, 0], beside).wait_send()

        for at, count in ((inner, line + 1), (jnp.logical_not(inner), 1)):
            pl.when(at)(functools.partial(lines, count))
        counts = (line, 2) if straight_cross else (line + 1, 1)
        for at, count in zip((inner, jnp.logical_not(inner)), counts):
            pl.when(at)(functools.partial(crossed, count))

    exchanged = []

    def stat_send(e):
        if exchanged:
            stat_all(exchanged[-1]).wait_send()
        exchanged.append(e)
        view = stat.at[e, m]

        def send(peer):
            remote(view, view, st_s.at[0], st_r.at[len(exchanged) % 2], (peer, c)).start()

        def go(d):
            @pl.when(a + line - d < line)
            def _():
                first = jnp.minimum(a + line - d, line - 1) * 2
                send(first + 1 - b)
                send(first + b)

            @pl.when(a >= line - d)
            def _():
                first = jnp.maximum(a - line + d, 0) * 2
                send(first + 1 - b)
                send(first + b)

        steps(1, line, go)
        send(m + 1 - 2 * b)

    def stat_all(e):
        view = stat.at[e, pl.ds(0, maps - 1)]
        return remote(view, view, st_s.at[0], st_r.at[(exchanged.index(e) + 1) % 2], beside)

    def stat_wait(e):
        stat_all(e).wait_recv()

    lane_own = pl.ds(pl.multiple_of(c * LANES, LANES), LANES)

    def lanes_of(owner):
        return pl.ds(pl.multiple_of(owner * LANES, LANES), LANES)

    def act_copy(l, n, owner, dev, place):
        rows = pl.ds(n * map_rows, map_rows)
        view = act.at[0, rows, lanes_of(owner)] if l == 0 else raw.at[l - 1, owner, rows]
        return remote(view, view, ag_s.at[l], ag_r.at[l, place], dev)

    def act_blocks(l, count, place):
        view = act.at[0, :, pl.ds(0, count * LANES)] if l == 0 else raw.at[l - 1, pl.ds(0, count)]
        return remote(view, view, ag_s.at[l], ag_r.at[l, place], (m, core))

    def act_send(l, n):
        act_copy(l, n, c, (m, far), n).start()
        act_copy(l, n, c, (m, core), nm).start()

    def act_forward(l, n):
        act_copy(l, n, far, (m, far), n).wait_recv()
        act_copy(l, n, far, (m, core), nm + 1).start()

    def act_near(l):
        act_blocks(l, 1, nm).wait_recv()

    def act_across(l):
        act_blocks(l, 1, nm + 1).wait_recv()

    def act_drain(l):
        act_blocks(l, 3, 0).wait_send()

    def scale_copy(l, owner, dev, ssem):
        view = scale_ref.at[l, owner]
        return remote(view, view, ssem, sc_r.at[l, owner], dev)

    def scale_send(l):
        for other in (core, far, across):
            scale_copy(l, c, (m, other), sc_s.at[l]).start()

    def scale_wait(l, owner):
        scale_copy(l, owner, (m, core), sc_s.at[l]).wait_recv()

    def scale_drain(l):
        view = scale_ref.at[l, pl.ds(0, 3)]
        remote(view, view, sc_s.at[l], sc_r.at[l, core], (m, core)).wait_send()

    own_along(0)
    own_aside_late(0, 0)

    loads[2].wait()
    col_of = lax.broadcasted_iota(jnp.int32, (width, width), 0)
    diagonal = col_of == lax.broadcasted_iota(jnp.int32, (width, width), 1)
    for n in range(nm):

        @pl.loop(0, height)
        def _(h):
            line_n = jnp.broadcast_to(mask_in[h, n : n + 1, :].astype(F32), (width, width))
            r = pl.ds(pl.multiple_of(n * map_rows + h * width, 8), width)
            conv[r, 0:width] = jnp.where(diagonal, line_n, 0.0)

    mask_ref[...] = jnp.dot(
        conv[:, 0:width].astype(BF16), jnp.ones((width, LANES), BF16), preferred_element_type=F32
    )
    loads[1].wait()

    @pl.loop(0, chunks)
    def _(i):
        r = rows_of(i)
        act[0, r, lane_own] = (x_in[r, :].astype(F32) * mask_ref[r, :]).astype(BF16)

    for n in range(nm):
        act_send(0, n)

    own_aside_late(0, 1)

    for n in range(nm):
        for i in range(3):
            for j in range(3):
                prod[i, j, n, 0:PAD, :] = jnp.zeros((PAD, LANES), F32)
                prod[i, j, n, PAD + map_rows :, :] = jnp.zeros((PAD, LANES), F32)
        zpad[n, 0:PAD, :] = jnp.zeros((PAD, LANES), F32)
        zpad[n, PAD + map_rows :, :] = jnp.zeros((PAD, LANES), F32)

    col_chunk = lax.broadcasted_iota(jnp.int32, (6, width, LANES), 1).reshape(chunk, LANES)
    has_left = jnp.where(col_chunk > 0, 1.0, 0.0)
    has_right = jnp.where(col_chunk < width - 1, 1.0, 0.0)

    loads[3].wait()
    loads[4].wait()
    half_h, half_w = height // 2, width // 2

    @pl.loop(0, half_h)
    def _(h):
        pool32[...] = grad_in[h].astype(F32)
        for n in range(nm):
            pick = pl.ds(n, half_w, stride=nm)
            kept = index_in[h, pick, :]
            value = pool32[pick, :]
            base = n * map_rows + 2 * h * width
            for r in range(2):
                for s in range(2):
                    spread[pl.ds(base + r * width + s, half_w, stride=2), :] = jnp.where(
                        kept == 2 * r + s, value, 0.0
                    )

    tasks = gather_tasks(step_both, 0)
    z_tasks = {l: gather_tasks(step_along, l) for l in range(1, layers)}
    x_tasks = {l: gather_tasks(step_aside, l) for l in range(1, layers)}
    c_tasks = {l: cross_tasks(l) for l in range(layers)}
    with scope("gather0"):
        run(tasks, pieces)
        run(c_tasks[0], 1)
        run(tasks, pieces)
        if layers > 1:
            own_along(1)
        run(c_tasks[0], 1)
        run(tasks)
    if layers > 1:
        own_aside_late(1, 0)
    for n in range(nm):
        act_forward(0, n)
    if layers > 1:
        with scope("along_1"):
            run(z_tasks[1], pieces)
    with scope("gather0_cross"):
        run(c_tasks[0])
    with scope("gather0_end"):
        gather_finish(0)
    if layers > 1:
        own_aside_late(1, 1)
    act_near(0)
    act_across(0)
    for cp in loads[5:]:
        cp.wait()

    for l in range(layers):
        z_near, x_near = z_tasks.get(l + 1, []), x_tasks.get(l + 1, [])
        z_next = z_tasks.get(l + 2, [])

        kernel = wcat[l * maps : (l + 1) * maps, :, :].reshape(maps * rows_w, wide)
        for n in range(nm):
            out = jnp.dot(
                act[l, pl.ds(n * map_rows, map_rows), :], kernel, preferred_element_type=F32
            )
            for i in range(3):
                for j in range(3):
                    t = 3 * i + j
                    prod[i, j, n, PAD : PAD + map_rows, :] = out[:, t * LANES : (t + 1) * LANES]

        def conv_chunk(i, carry):
            total, count = carry
            r = rows_of(i)
            value = None
            for j in range(3):
                side = None
                for k in range(3):
                    n, pr = padded_rows(i, width * (k - 1) + (j - 1))
                    term = prod[k, j, n, pr, :]
                    side = term if side is None else side + term
                if j == 0:
                    side = side * has_left
                if j == 2:
                    side = side * has_right
                value = side if value is None else value + side
            conv[r, :] = value
            valid = mask_ref[r, :]
            return total + tile8(value * valid), count + tile8(valid)

        zero8 = jnp.zeros((8, LANES), F32)
        total, count = lax.fori_loop(0, chunks, conv_chunk, (zero8, zero8))
        total = jnp.sum(total, axis=0, keepdims=True)
        count = jnp.sum(count, axis=0, keepdims=True)
        mean = total / jnp.maximum(count, 1.0)

        def dev_chunk(i, carry):
            r = rows_of(i)
            delta = conv[r, :] - mean
            if l + 1 < layers:
                raw[l, c, r, :] = delta.astype(BF16)
            return carry + tile8(delta * delta * mask_ref[r, :])

        spread_sum = zero8
        for n in range(nm):
            spread_sum = lax.fori_loop(n * per_map, (n + 1) * per_map, dev_chunk, spread_sum)
            if l + 1 < layers:
                act_send(l + 1, n)
        spread_sum = jnp.sum(spread_sum, axis=0, keepdims=True)
        stat[l, m] = jnp.concatenate(
            [total, spread_sum, count, mean, jnp.zeros((4, LANES), F32)], axis=0
        )
        stat_send(l)
        with scope("gather_a"):
            run(x_near, len(x_near) - len(z_near))
            if len(z_near) > pieces:
                run(z_near, pieces)
                run(x_near, pieces)
        with scope("turn"):
            slots = LANES // rows_w
            for i, owner in enumerate((across, far, core, c)):
                rows = wcat[pl.ds(l * maps + owner * slots, slots), :, :].reshape(LANES, wide)
                turned[l, :, i * LANES : (i + 1) * LANES] = rows.T
        if l + 1 < layers:
            with scope("gather_own_cross"):
                run(c_tasks[l + 1], 1)
                if l + 2 < layers:
                    own_along(l + 2)
        with scope("stat_wait"):
            stat_wait(l)

        def add_totals(s, carry):
            block = stat[l, s]
            return carry[0] + block[0:1, :], carry[1] + block[2:3, :]

        zero1 = jnp.zeros((1, LANES), F32)
        total, count = lax.fori_loop(0, maps, add_totals, (zero1, zero1))
        center = total / count

        def add_spread(s, carry):
            block = stat[l, s]
            delta = block[3:4, :] - center
            return carry + block[1:2, :] + block[2:3, :] * delta * delta

        variance = lax.fori_loop(0, maps, add_spread, zero1) / count
        inv_std = lax.rsqrt(variance + norm_epsilon)
        gain = gain_in[l : l + 1, :]
        bias = bias_in[l : l + 1, :]
        if l == 0:
            count_all = count
            scales = []
        scales.append(gain * inv_std)

        if l + 1 < layers:
            factor = gain * inv_std
            scale_ref[l, c] = jnp.concatenate(
                [factor, bias + factor * (mean - center), jnp.zeros((6, LANES), F32)], axis=0
            )
            scale_send(l)

        def own_chunk(i, carry):
            r = rows_of(i)
            unit = (conv[r, :] - center) * inv_std
            pre = gain * unit + bias
            sigma = 1.0 / (1.0 + jnp.exp(-pre))
            valid = mask_ref[r, :]
            result = pre * sigma * valid
            slant = sigma * (1.0 + pre * (1.0 - sigma)) * valid
            normed[l, r, :] = unit
            if l + 1 < layers:
                slope[l, r, :] = slant
                act[l + 1, r, lane_own] = result.astype(BF16)
                return carry
            result_ref[r, :] = result
            value = spread[r, :] * slant
            conv[r, :] = value
            return carry[0] + tile8(value * unit), carry[1] + tile8(value)

        grad_sums = lax.fori_loop(0, chunks, own_chunk, (zero8, zero8))

        def activate(owner, first, last):
            pair = scale_ref[l, owner]
            factor, offset = pair[0:1, :], pair[1:2, :]
            lanes = lanes_of(owner)

            @pl.loop(first * per_map, last * per_map)
            def _(i):
                r = rows_of(i)
                pre = factor * raw[l, owner, r, :].astype(F32) + offset
                result = pre / (1.0 + jnp.exp(-pre)) * mask_ref[r, :]
                act[l + 1, r, lanes] = result.astype(BF16)

        if l + 1 < layers:
            with scope("act_near"):
                act_near(l + 1)
                scale_wait(l, core)
                activate(core, 0, nm)
            with scope("gather_b"):
                run(z_near)
                run(x_near)
                run(c_tasks[l + 1], 1)
            with scope("act_far"):
                for n in range(nm):
                    act_forward(l + 1, n)
                    if n == 0:
                        scale_wait(l, far)
                    activate(far, n, n + 1)
            with scope("gather_c"):
                run(c_tasks[l + 1], 1)
                if l + 2 < layers:
                    own_aside(l + 2)
                run(z_next, pieces)
            with scope("act_across"):
                act_across(l + 1)
                scale_wait(l, across)
                activate(across, 0, nm)
            with scope("gather_cross"):
                run(c_tasks[l + 1])
            with scope("gather_end"):
                gather_finish(l + 1)

    def pool():
        @pl.loop(0, half_h)
        def _(h):
            for n in range(nm):
                pick = pl.ds(n, half_w, stride=nm)
                kept = index_in[h, pick, :]
                base = n * map_rows + 2 * h * width
                total = jnp.zeros((half_w, LANES), F32)
                for r in range(2):
                    for s in range(2):
                        total = total + jnp.where(
                            kept == 2 * r + s,
                            result_ref[pl.ds(base + r * width + s, half_w, stride=2), :],
                            0.0,
                        )
                pool32[pick, :] = total
            pooled_ref[h] = pool32[...].astype(BF16)

    def place_of(k):
        before, after = a, line - 1 - a
        spare = jnp.maximum(before, after) - jnp.minimum(before, after)
        q = jnp.maximum(k - spare, 0)
        near, side = q // 2, q % 2
        low = jnp.where(before > after, spare, 0) + near
        high = line - 1 - jnp.where(before < after, spare, 0) - near
        outer = jnp.where(before > after, k, line - 1 - k)
        return jnp.where(k < spare, outer, jnp.where(side == 0, high, low))

    places = {False: [place_of(k) for k in range(line)] if line <= 8 else []}
    places[True] = list(places[False])
    if 2 < line <= 8:
        ends = jnp.logical_or(a == 0, a + 1 == line)
        places[True][0] = jnp.where(ends, places[False][1], places[False][0])
        places[True][1] = jnp.where(ends, places[False][0], places[False][1])

    def kth_place(k, l):
        return places[straight(l)][k] if line <= 8 else place_of(k)

    parts = grad_parts(layers, rows_w)

    def part_of(l, g):
        rows = rows_w // parts[l]
        return pl.ds(g * rows, rows)

    def gx_copy(l, z, g):
        return remote(
            gx_out.at[l, z, part_of(l, g)], gx_in.at[l, z, part_of(l, g)],
            gx_s.at[l], gx_r.at[line * sum(parts[:l]) + z * parts[l] + g], beside,
        )

    def gz_copy(l, z, g, slot, dev):
        return remote(
            gz_out.at[l, z, part_of(l, g)], gz_in.at[l, slot, part_of(l, g)],
            gz_s.at[l], gz_r.at[(line + 1) * sum(parts[:l]) + slot * parts[l] + g], dev,
        )

    def shard(l, slot, g):
        rows = rows_w // parts[l]
        first = pl.multiple_of(slot * rows_w, 8) + g * rows
        return grad_w[l, pl.ds(first, rows), :]

    tile = 2 * rows_w
    fine = tile % LANES == 0

    def kernel_grad(l, first, amount):
        rows = pl.ds(pl.multiple_of(first, LANES), amount)
        grad_w[l, rows, :] = lax.dot_general(
            act[l, :, rows], dcat[...], (((0,), (0,)), ((), ())), preferred_element_type=F32
        )

    def kernel_grads(l, low=0, high=None):
        high = line if high is None else high
        if not fine and low == 0:
            coarse = (maps * rows_w) // 4
            pl.loop(0, 4)(lambda i: kernel_grad(l, i * coarse, coarse))

        def go(k):
            z = kth_place(k, l)
            if fine:
                kernel_grad(l, z * tile, tile)
            for g in range(parts[l]):
                gx_out[l, z, part_of(l, g)] = shard(l, z * 2 + 1 - b, g).astype(BF16)
            if l == 0 and line <= 8 and k == line - 1 and layers > 1:
                for g in range(parts[1]):
                    if is_late(1, k, g):
                        gx_copy(1, a, g).start()
            for g in range(parts[l]):
                if line > 8 or is_early(l, k, g):
                    gx_copy(l, z, g).start()

        steps(low, high, go)

    def is_late(l, k, g):
        return l == 1 and line <= 8 and k == line - 1 and g >= (parts[l] + 1) // 2

    def is_early(l, k, g):
        return l == 0 or k < 2

    def scatter_x(l):
        if line <= 8:
            for k in range(line):
                for g in range(parts[l]):
                    if not is_early(l, k, g) and not is_late(l, k, g):
                        gx_copy(l, kth_place(k, l), g).start()

    def pair_sum(l, z, g):
        gx_copy(l, z, g).wait_recv()
        return shard(l, z * 2 + b, g) + gx_in[l, z, part_of(l, g)].astype(F32)

    def onward(l, z, g, fed, dev, slot):
        value = pair_sum(l, z, g)
        if fed:
            gz_copy(l, z, g, z, dev).wait_recv()
            value = value + gz_in[l, z, part_of(l, g)].astype(F32)
        gz_out[l, z, part_of(l, g)] = value.astype(BF16)
        gz_copy(l, z, g, slot, dev).start()

    def straight(l):
        return False

    def scatter_step(l, d, g, fed):
        ends = straight(l) and d == line - 1
        zr, zl = jnp.minimum(a + d, line - 1), jnp.maximum(a - d, 0)
        more_r, more_l = a > 0, a + 1 < line
        if straight(l):
            more_r = jnp.where(zr == line - 1, a > 1, more_r)
            more_l = jnp.where(zl == 0, a + 2 < line, more_l)
        for there, z, more, dev, slot in (
            (a + d < line, zr, more_r, right, zr),
            (a >= d, zl, more_l, left, jnp.where(zl == a - 1, line, zl)),
        ):
            if ends:
                dev, slot = (z * 2 + b, c), line + 1
            now = jnp.logical_and(there, more if fed else jnp.logical_not(more))
            pl.when(now)(functools.partial(onward, l, z, g, fed, dev, slot))

    def scatter_own(l, g):
        r = part_of(l, g)
        total_w[r, :] = pair_sum(l, a, g)

        def add(slot):
            gz_copy(l, a, g, slot, left).wait_recv()
            total_w[r, :] += gz_in[l, slot, r].astype(F32)

        pl.when(a > 0)(lambda: add(a))
        pl.when(a + 1 < line)(lambda: add(line))
        if straight(l):
            pl.when(jnp.logical_or(a == 0, a + 1 == line))(lambda: add(line + 1))
        for t in range(taps):
            gradient = total_w[r, t * LANES : (t + 1) * LANES]
            new, first, second = adamw_update(
                weight_in[l, t, r], gradient, first_in[l, t, r], second_in[l, t, r], rate_conv
            )
            wgrad_ref[l, t, r] = gradient
            wfirst_ref[l, t, r] = first
            wsecond_ref[l, t, r] = second
            wnew_ref[l, t, r] = new
            wcopy_ref[l, t, r] = new.astype(BF16)

    def scatter_tasks(l):
        owns = [functools.partial(scatter_own, l, g) for g in range(parts[l])]
        if line <= 8:
            first, fed = (
                [
                    functools.partial(scatter_step, l, line - e, g, kind)
                    for e in ((2, 1, *range(3, line)) if straight(l) else range(1, line))
                    if e > kind + (kind and straight(l))
                    for g in range(parts[l])
                ]
                for kind in (False, True)
            )
            return first, fed, owns

        def everything():
            def go(e):
                for g in range(parts[l]):
                    scatter_step(l, line - e, g, False)
                    scatter_step(l, line - e, g, True)

            steps(1, line, go)

        return [everything], [], owns

    def scatter_drain(l):
        remote(gx_out.at[l], gx_in.at[l], gx_s.at[l], gx_r.at[0], beside).wait_send()
        view = pl.ds(0, line - 1)
        remote(
            gz_out.at[l, view], gz_in.at[l, view], gz_s.at[l], gz_r.at[0], beside
        ).wait_send()

    def layer_drain(l):
        remote(pair_out.at[l], pair_in.at[l], pr_s.at[l], pr_r.at[l, 0], (m, core)).wait_send()
        remote(far_out.at[l], far_in.at[l], fr_s.at[l], fr_r.at[l, 0], (m, far)).wait_send()

    half = 2 * LANES
    def pair_copy(l, h, n):
        return remote(
            pair_out.at[l, h, pl.ds(n * map_rows, map_rows), :],
            pair_in.at[l, h, pl.ds(n * map_rows, map_rows), :],
            pr_s.at[l], pr_r.at[l, n if h == 0 else nm], (m, core),
        )

    def far_copy(l, n):
        return remote(
            far_out.at[l, pl.ds(n * map_rows, map_rows), :],
            far_in.at[l, pl.ds(n * map_rows, map_rows), :],
            fr_s.at[l], fr_r.at[l, n], (m, far),
        )

    todo, fed, owns = {}, {}, {}
    for l in reversed(range(layers)):
        e = layers + l
        gain_sum, bias_sum = grad_sums
        stat[e, m] = jnp.concatenate(
            [
                jnp.sum(gain_sum, axis=0, keepdims=True),
                jnp.sum(bias_sum, axis=0, keepdims=True),
                jnp.zeros((6, LANES), F32),
            ],
            axis=0,
        )
        stat_send(e)
        if l + 1 < layers:
            scatter_x(l + 1)
        else:
            pool()
        if l + 1 < layers:
            todo[l + 1], fed[l + 1], owns[l + 1] = scatter_tasks(l + 1)
        if l + 2 < layers:
            run(todo[l + 2])
            run(fed[l + 2])
        if l + 1 < layers:
            with scope("scatter_a"):
                run(todo[l + 1], parts[l + 1] if l > 0 else 2 * parts[l + 1])
        with scope("stat_wait_back"):
            stat_wait(e)

        def add_sums(s, carry):
            return carry + stat[e, s]

        sums = lax.fori_loop(0, maps, add_sums, jnp.zeros((8, LANES), F32))
        ngrad_ref[l] = sums[0:2, :]
        gain_grad = sums[0:1, :]
        bias_grad = sums[1:2, :]
        scale = scales[l]

        def conv_grad(n):
            @pl.loop(n * per_map, (n + 1) * per_map)
            def _(i):
                r = rows_of(i)
                value = (
                    mask_ref[r, :]
                    * scale
                    * (conv[r, :] - (bias_grad + normed[l, r, :] * gain_grad) / count_all)
                )
                pr = pl.ds(pl.multiple_of((i - n * per_map) * chunk, 16) + PAD, chunk)
                zpad[n, pr, :] = value

            @pl.loop(n * per_map, (n + 1) * per_map)
            def _(i):
                r = rows_of(i)
                for k in range(3):
                    for j in range(3):
                        shift = PAD - (width * (k - 1) + (j - 1))
                        pr = pl.ds(pl.multiple_of((i - n * per_map) * chunk, 16) + shift, chunk)
                        term = zpad[n, pr, :]
                        if j == 0:
                            term = term * has_right
                        if j == 2:
                            term = term * has_left
                        t = 3 * k + j
                        dcat[r, t * LANES : (t + 1) * LANES] = term.astype(BF16)

        def input_grad(h, first, last):
            r = pl.ds(first * map_rows, (last - first) * map_rows)
            out = jnp.dot(
                dcat[r, :], turned[l, :, h * half : (h + 1) * half], preferred_element_type=F32
            )
            pair_out[l, h, r, :] = out[:, :LANES].astype(BF16)
            for n in range(first, last):
                pair_copy(l, h, n).start()
            part[h, r, :] = out[:, LANES:]

        def to_far(n):
            r = pl.ds(n * map_rows, map_rows)
            pair_copy(l, 0, n).wait_recv()
            far_out[l, r, :] = (part[0, r, :] + pair_in[l, 0, r, :].astype(F32)).astype(BF16)
            far_copy(l, n).start()

        if l > 0:
            for n in range(nm):
                with scope("conv_grad"):
                    conv_grad(n)
                with scope("input_grad"):
                    input_grad(0, n, n + 1)
                if n > 0:
                    with scope("to_far"):
                        to_far(n - 1)
            if l + 1 < layers:
                with scope("scatter_b"):
                    run(todo[l + 1], parts[l + 1])
                    run(fed[l + 1], parts[l + 1])
            with scope("kernel_grad"):
                kernel_grads(l, 0, line // 2)
            with scope("to_far"):
                to_far(nm - 1)
            if l + 1 < layers:
                with scope("scatter_c"):
                    run(todo[l + 1])
            with scope("kernel_grad"):
                kernel_grads(l, line // 2)
            with scope("input_grad"):
                input_grad(1, 0, nm)
            with scope("drain"):
                if l + 1 == layers:
                    for k in range(layers):
                        gather_drain(k)
                        act_drain(k)
                        if k + 1 < layers:
                            scale_drain(k)
                else:
                    layer_drain(l + 1)
        else:
            for n in range(nm):
                with scope("conv_grad"):
                    conv_grad(n)
            with scope("kernel_grad"):
                kernel_grads(0)
            todo[0], fed[0], owns[0] = scatter_tasks(0)
            with scope("scatter_1c"):
                run(todo[1])
                run(fed[1], parts[1])
            with scope("input_grad"):
                input_grad(0, 0, nm)
            with scope("to_far"):
                for n in range(nm):
                    to_far(n)
            with scope("scatter_0a"):
                run(todo[0], parts[0])
            with scope("scatter_1d"):
                run(fed[1])
            with scope("input_grad"):
                input_grad(1, 0, nm)
            with scope("scatter_0b"):
                run(todo[0], parts[0])
                run(fed[0], parts[0])
            with scope("owns_2"):
                for k in range(layers - 1, 1, -1):
                    run(owns[k])

        zero8 = jnp.zeros((8, LANES), F32)
        grad_sums = (zero8, zero8)
        for n in range(nm):
            r = pl.ds(n * map_rows, map_rows)
            with scope("far_wait"):
                if n == 0:
                    remote(
                        pair_out.at[l, 1], pair_in.at[l, 1], pr_s.at[l], pr_r.at[l, nm], (m, core)
                    ).wait_recv()
                far_copy(l, n).wait_recv()
            if n == 0 and l > 0 and l + 1 < layers:
                with scope("scatter_d"):
                    run(fed[l + 1])

            def back_chunk(i, carry):
                r = rows_of(i)
                value = part[1, r, :] + pair_in[l, 1, r, :].astype(F32) + far_in[l, r, :].astype(F32)
                if l == 0:
                    back[r, :] = value * mask_ref[r, :]
                    return carry
                value = value * slope[l - 1, r, :]
                conv[r, :] = value
                return carry[0] + tile8(value * normed[l - 1, r, :]), carry[1] + tile8(value)

            grad_sums = lax.fori_loop(n * per_map, (n + 1) * per_map, back_chunk, grad_sums)

    with scope("norms"):
        for values, place in ((gain_in, 0), (bias_in, 1)):
            new, first, second = adamw_update(
                values[...], ngrad_ref[:, place, :], norm_first_in[:, place, :],
                norm_second_in[:, place, :], rate_norm,
            )
            nfirst_ref[:, place, :] = first
            nsecond_ref[:, place, :] = second
            nnew_ref[:, place, :] = new
    with scope("scatter_end"):
        run(todo[0])
        run(fed[0])
    with scope("owns_1"):
        for k in range(1, min(2, layers)):
            run(owns[k])
    with scope("drain"):
        for k in range(1, layers):
            scatter_drain(k)
        layer_drain(1)
    with scope("owns"):
        run(owns[0])

    with scope("drain_end"):
        layer_drain(0)
        scatter_drain(0)
        stat_all(exchanged[-1]).wait_send()


def store_kernel(count, *refs):
    copies = [
        pltpu.make_async_copy(refs[i], refs[count + i], refs[2 * count].at[i]) for i in range(count)
    ]
    for cp in copies:
        cp.start()
    for cp in copies:
        cp.wait()


def store_results(results):
    any_spec = pl.BlockSpec(memory_space=pl.ANY)
    count = len(results)
    return pl.pallas_call(
        functools.partial(store_kernel, count),
        out_shape=tuple(jax.ShapeDtypeStruct(r.shape, r.dtype) for r in results),
        in_specs=[any_spec] * count,
        out_specs=(any_spec,) * count,
        scratch_shapes=[pltpu.SemaphoreType.DMA((count,))],
        compiler_params=pltpu.CompilerParams(vmem_limit_bytes=1 << 20),
    )(*results)


def block_call(maps, chans, x, mask, index, grad, weights, gain, bias, *moments):
    nm, height, width, lanes = x.shape
    layers, taps, rows_w, _ = weights.shape
    pixels = nm * height * width
    line = maps // 2
    wide = taps * LANES
    channels = chans * LANES
    map_rows = height * width
    sizes = (maps, chans, layers, taps, nm, height, width)
    pieces = 2 if rows_w % 32 == 0 else 1
    vm = pltpu.VMEM
    dma = pltpu.SemaphoreType.DMA
    hbm = pl.BlockSpec(memory_space=pltpu.HBM)
    scratch = [
        vm((pixels, LANES), BF16), vm(mask.shape, jnp.int32), vm(index.shape, jnp.int32),
        vm(grad.shape, BF16), vm(weights.shape, F32), vm(gain.shape, F32), vm(bias.shape, F32),
        *(vm(v.shape, F32) for v in moments),
        vm((pixels, LANES), F32),
        vm((layers * maps, rows_w, wide), BF16),
        vm((layers, wide, channels), BF16),
        vm((layers, pixels, channels), BF16),
        vm((layers - 1, chans, pixels, LANES), BF16),
        vm((layers - 1, chans, 8, LANES), F32),
        vm((3, 3, nm, map_rows + 2 * PAD, LANES), F32),
        vm((pixels, LANES), F32),
        vm((layers, pixels, LANES), F32),
        vm((layers, pixels, LANES), F32),
        vm((pixels, LANES), F32),
        vm((pixels, LANES), F32),
        vm((nm * (width // 2), LANES), F32),
        vm((nm, map_rows + 2 * PAD, LANES), F32),
        vm((pixels, wide), BF16),
        vm((layers, channels, wide), F32),
        vm((2, pixels, LANES), F32),
        vm((2 * layers, maps, 8, LANES), F32),
        vm((layers, 2, pixels, LANES), BF16), vm((layers, 2, pixels, LANES), BF16),
        vm((layers, pixels, LANES), BF16), vm((layers, pixels, LANES), BF16),
        vm((layers, line, rows_w, wide), BF16), vm((layers, line, rows_w, wide), BF16),
        vm((layers, line, rows_w, wide), BF16), vm((layers, line + 1, rows_w, wide), BF16),
        vm((rows_w, wide), F32),
        dma((11,)),
        dma((layers, 4)), dma((layers, line, pieces)), dma((layers, 2)), dma((layers, line)),
        dma((1,)), dma((2,)),
        dma((layers,)), dma((layers, nm + 2)),
        dma((layers - 1,)), dma((layers - 1, chans)),
        dma((layers,)), dma((layers, nm + 1)),
        dma((layers,)), dma((layers, nm)),
        dma((layers,)), dma((line * sum(grad_parts(layers, rows_w)),)),
        dma((layers,)), dma(((line + 1) * sum(grad_parts(layers, rows_w)),)),
    ]
    arrays = (
        [(index.shape, BF16), ((pixels, LANES), F32)]
        + [(weights.shape, F32)] * 4
        + [(weights.shape, BF16)]
        + [((layers, 2, LANES), F32)] * 4
    )
    return pl.pallas_call(
        functools.partial(block_kernel, sizes),
        out_shape=tuple(jax.ShapeDtypeStruct(*kind) for kind in arrays),
        in_specs=[hbm] * 11,
        out_specs=(pl.BlockSpec(memory_space=pltpu.VMEM),) * len(arrays),
        scratch_shapes=scratch,
        compiler_params=pltpu.CompilerParams(
            collective_id=0, has_side_effects=True, vmem_limit_bytes=48 << 20
        ),
    )(*(
        pltpu.with_memory_space_constraint(v, pltpu.HBM)
        for v in (x.reshape(pixels, LANES), mask, index, grad, weights, gain, bias, *moments)
    ))


def local(
    maps, chans,
    input_maps, valid_mask, pool_index, out_grad, conv_weights, weight_first, weight_second,
    norm_gain, norm_bias, norm_first, norm_second,
):
    nm, half_h, half_w, lanes = pool_index.shape
    by_row = (half_h, half_w * nm, lanes)
    pooled, image, *updates = store_results(
        block_call(
            maps, chans, input_maps, valid_mask.transpose(1, 0, 2),
            pool_index.transpose(1, 2, 0, 3).reshape(by_row),
            out_grad.transpose(1, 2, 0, 3).reshape(by_row),
            conv_weights, norm_gain, norm_bias, weight_first, weight_second, norm_first, norm_second,
        )
    )
    pooled = pooled.reshape(half_h, half_w, nm, lanes).transpose(2, 0, 1, 3)
    return (pooled, image.reshape(input_maps.shape), *updates)


def solution(mesh):
    return jax.shard_map(
        functools.partial(local, mesh.shape["maps"], mesh.shape["chan"]),
        mesh=mesh,
        in_specs=(
            P("maps", None, None, "chan"),
            P("maps", None, None),
            P("maps", None, None, "chan"),
            P("maps", None, None, "chan"),
            P(None, None, "maps", "chan"),
            P(None, None, "maps", "chan"),
            P(None, None, "maps", "chan"),
            P(None, "chan"),
            P(None, "chan"),
            P(None, None, "chan"),
            P(None, None, "chan"),
        ),
        out_specs=(
            P("maps", None, None, "chan"),
            P("maps", None, None, "chan"),
            P(None, None, "maps", "chan"),
            P(None, None, "maps", "chan"),
            P(None, None, "maps", "chan"),
            P(None, None, "maps", "chan"),
            P(None, None, "maps", "chan"),
            P(None, None, "chan"),
            P(None, None, "chan"),
            P(None, None, "chan"),
            P(None, None, "chan"),
        ),
        check_vma=False,
    )
```

```python
import functools

import jax
import jax.numpy as jnp
from jax import lax
from jax.experimental import pallas as pl
from jax.experimental.pallas import tpu as pltpu
from jax.sharding import PartitionSpec as P

beta_first = 0.5
beta_second = 0.5
rate_conv = 0.01
rate_norm = 0.2
decay_rate = 0.01
adam_epsilon = 1e-08
norm_epsilon = 1e-05
step_count = 5.0
first_scale = 1.0 / (1.0 - beta_first**step_count)
second_scale = 1.0 / (1.0 - beta_second**step_count)

MESH = pl.DeviceIdType.MESH
F32 = jnp.float32
BF16 = jnp.bfloat16
LANES = 128
PAD = 32


def adamw_update(parameter, gradient, first_moment, second_moment, step_rate):
    first_new = beta_first * first_moment + (1.0 - beta_first) * gradient
    second_new = beta_second * second_moment + (1.0 - beta_second) * gradient * gradient
    step = first_new * first_scale / (jnp.sqrt(second_new * second_scale) + adam_epsilon)
    return (parameter - step_rate * (step + decay_rate * parameter), first_new, second_new)


def steps(low, high, body):
    if high - low <= 8:
        for index in range(low, high):
            body(index)
    else:
        pl.loop(low, high)(body)


class scope:
    def __init__(self, name): pass
    def __enter__(self): return self
    def __exit__(self, *a): return False


def run(tasks, amount=None):
    for _ in range(len(tasks) if amount is None else min(amount, len(tasks))):
        tasks.pop(0)()


def grad_parts(layers, rows_w):
    pieces = 2 if rows_w % 32 == 0 else 1
    return [4 if l == 0 and rows_w % 64 == 0 else pieces for l in range(layers)]


def tile8(values):
    rows = values.shape[0]
    return jnp.sum(values.reshape(rows // 8, 8, LANES), axis=0)


def block_kernel(
    sizes,
    x_hbm, mask_hbm, index_hbm, grad_hbm, weight_hbm, gain_hbm, bias_hbm,
    first_hbm, second_hbm, norm_first_hbm, norm_second_hbm,
    pooled_ref, back, wgrad_ref, wfirst_ref, wsecond_ref, wnew_ref, wcopy_ref,
    ngrad_ref, nfirst_ref, nsecond_ref, nnew_ref,
    x_in, mask_in, index_in, grad_in, weight_in, gain_in, bias_in,
    first_in, second_in, norm_first_in, norm_second_in,
    mask_ref, wcat, turned, act, raw, scale_ref, prod, conv, normed, slope, result_ref, spread, pool32, zpad, dcat,
    grad_w, part, stat, pair_out, pair_in, far_out, far_in,
    gx_out, gx_in, gz_out, gz_in, total_w,
    in_sem,
    w_s, wz_r, wx_r, wc_r, st_s, st_r, ag_s, ag_r, sc_s, sc_r, pr_s, pr_r, fr_s, fr_r,
    gx_s, gx_r, gz_s, gz_r,
):
    maps, chans, layers, taps, nm, height, width = sizes
    line = maps // 2
    m = lax.axis_index("maps")
    c = lax.axis_index("chan")
    a = m // 2
    b = m % 2
    core = c + 1 - 2 * (c % 2)
    far = lax.rem(c + 2, 4)
    across = core + 2 - 4 * (core // 2)
    map_rows = height * width
    pixels = nm * map_rows
    rows_w = wcat.shape[1]
    wide = taps * LANES
    chunk = 6 * width
    chunks = pixels // chunk
    per_map = map_rows // chunk

    def rows_of(i):
        return pl.ds(pl.multiple_of(i * chunk, 16), chunk)

    def padded_rows(i, shift):
        n = i // per_map
        return n, pl.ds(pl.multiple_of((i - n * per_map) * chunk, 8) + (PAD + shift), chunk)

    def remote(src, dst, ssem, rsem, dev):
        return pltpu.make_async_remote_copy(
            src_ref=src, dst_ref=dst, send_sem=ssem, recv_sem=rsem,
            device_id=dev, device_id_type=MESH,
        )

    loads = []
    for i, (src, dst) in enumerate(
        (
            (weight_hbm, weight_in), (x_hbm, x_in), (mask_hbm, mask_in),
            (index_hbm, index_in), (grad_hbm, grad_in), (gain_hbm, gain_in), (bias_hbm, bias_in),
            (first_hbm, first_in), (second_hbm, second_in),
            (norm_first_hbm, norm_first_in), (norm_second_hbm, norm_second_in),
        )
    ):
        cp = pltpu.make_async_copy(src, dst, in_sem.at[i])
        cp.start()
        loads.append(cp)

    barrier = pltpu.get_barrier_semaphore()

    def greet(d):
        peer = lax.rem(m + d, maps)
        pl.semaphore_signal(barrier, inc=1, device_id=(peer, c), device_id_type=MESH)

    steps(1, maps, greet)
    for other in (core, far, across):
        pl.semaphore_signal(barrier, inc=1, device_id=(m, other), device_id_type=MESH)

    with scope("load"):
        loads[0].wait()
    for l in range(layers):
        for t in range(taps):
            wcat[l * maps + m, :, t * LANES : (t + 1) * LANES] = weight_in[l, t].astype(BF16)

    with scope("barrier"):
        pl.semaphore_wait(barrier, maps + 2)

    pieces = wz_r.shape[2]
    piece_rows = rows_w // pieces
    right = (jnp.minimum(m + 2, maps - 1), c)
    left = (jnp.maximum(m - 2, 0), c)
    beside = (m + 1 - 2 * b, c)
    opposite = ((line - 1 - a) * 2 + b, c)
    straight_cross = line == 4

    def crossing(l):
        return (1 if l == 0 else 2) * LANES

    def along(l, z, g, dev):
        view = wcat.at[l * maps + z * 2 + b, pl.ds(g * piece_rows, piece_rows)]
        return remote(view, view, w_s.at[l, 0], wz_r.at[l, z, g], dev)

    def aside(l, z, g):
        lanes = pl.ds(crossing(l), wide - crossing(l))
        view = wcat.at[l * maps + z * 2 + b, pl.ds(g * piece_rows, piece_rows), lanes]
        return remote(view, view, w_s.at[l, 1], wx_r.at[l, 0], beside)

    def aside_own(l, slot):
        view = wcat.at[l * maps + slot]
        return remote(view, view, w_s.at[l, 2], wx_r.at[l, 1], beside)

    def across_line(l, z, dev):
        view = wcat.at[l * maps + z * 2 + 1 - b, :, pl.ds(0, crossing(l))]
        return remote(view, view, w_s.at[l, 3], wc_r.at[l, z], dev)

    def own_along(l):
        for g in range(pieces):
            pl.when(a + 1 < line)(lambda: along(l, a, g, right).start())
            pl.when(a > 0)(lambda: along(l, a, g, left).start())

    def own_aside(l):
        aside_own(l, m).start()

    def own_aside_late(l, late):
        pl.when(c % 2 == late)(lambda: own_aside(l))

    def flows(s, body):
        body(a >= s, jnp.maximum(a - s, 0), a + 1 < line, right)
        body(a + s < line, jnp.minimum(a + s, line - 1), a > 0, left)

    def step_along(l, s, g, both=False):
        def piece(there, z, on, dev):
            @pl.when(there)
            def _():
                along(l, z, g, dev).wait_recv()
                pl.when(on)(lambda: along(l, z, g, dev).start())
                if both:
                    aside(l, z, g).start()

        flows(s, piece)

    def step_aside(l, s, g):
        flows(s, lambda there, z, on, dev: pl.when(there)(lambda: aside(l, z, g).start()))

    def step_both(l, s, g):
        step_along(l, s, g, True)

    def own_cross(l):
        aside_own(l, m + 1 - 2 * b).wait_recv()
        pl.when(a + 1 < line)(lambda: across_line(l, a, right).start())
        pl.when(a > 0)(lambda: across_line(l, a, left).start())
        if straight_cross:
            pl.when(jnp.logical_or(a == 0, a + 1 == line))(
                lambda: across_line(l, a, opposite).start()
            )

    def step_cross(l, s):
        def piece(there, z, on, dev):
            if straight_cross:
                far_end = jnp.logical_or(
                    jnp.logical_and(z == 0, a + 2 == line), jnp.logical_and(z + 1 == line, a == 1)
                )
                on = jnp.logical_and(on, jnp.logical_not(far_end))

            @pl.when(there)
            def _():
                across_line(l, z, dev).wait_recv()
                pl.when(on)(lambda: across_line(l, z, dev).start())

        flows(s, piece)

    def gather_tasks(step, l):
        if line <= 8:
            return [
                functools.partial(step, l, s, g) for s in range(1, line) for g in range(pieces)
            ]

        def everything():
            def go(s):
                for g in range(pieces):
                    step(l, s, g)

            steps(1, line, go)

        return [everything]

    def cross_tasks(l):
        if line <= 8:
            return [functools.partial(own_cross, l)] + [
                functools.partial(step_cross, l, s) for s in range(1, line)
            ]
        return [
            functools.partial(own_cross, l),
            lambda: steps(1, line, lambda s: step_cross(l, s)),
        ]

    def rest_of(l):
        lanes = pl.ds(crossing(l), wide - crossing(l))
        view = wcat.at[pl.ds(0, line - 1), :, lanes]
        return remote(view, view, w_s.at[l, 1], wx_r.at[l, 0], beside)

    def gather_finish(l):
        rest_of(l).wait_recv()

    def gather_drain(l):
        rest_of(l).wait_send()
        aside_own(l, m).wait_send()
        inner = jnp.logical_and(a > 0, a + 1 < line)

        def lines(count):
            view = wcat.at[pl.ds(0, count)]
            remote(view, view, w_s.at[l, 0], wx_r.at[l, 0], beside).wait_send()

        def crossed(count):
            view = wcat.at[pl.ds(0, count), :, pl.ds(0, crossing(l))]
            remote(view, view, w_s.at[l, 3], wx_r.at[l, 0], beside).wait_send()

        for at, count in ((inner, line + 1), (jnp.logical_not(inner), 1)):
            pl.when(at)(functools.partial(lines, count))
        counts = (line, 2) if straight_cross else (line + 1, 1)
        for at, count in zip((inner, jnp.logical_not(inner)), counts):
            pl.when(at)(functools.partial(crossed, count))

    exchanged = []

    def stat_send(e):
        if exchanged:
            stat_all(exchanged[-1]).wait_send()
        exchanged.append(e)
        view = stat.at[e, m]

        def send(peer):
            remote(view, view, st_s.at[0], st_r.at[len(exchanged) % 2], (peer, c)).start()

        def go(d):
            @pl.when(a + line - d < line)
            def _():
                first = jnp.minimum(a + line - d, line - 1) * 2
                send(first + 1 - b)
                send(first + b)

            @pl.when(a >= line - d)
            def _():
                first = jnp.maximum(a - line + d, 0) * 2
                send(first + 1 - b)
                send(first + b)

        steps(1, line, go)
        send(m + 1 - 2 * b)

    def stat_all(e):
        view = stat.at[e, pl.ds(0, maps - 1)]
        return remote(view, view, st_s.at[0], st_r.at[(exchanged.index(e) + 1) % 2], beside)

    def stat_wait(e):
        stat_all(e).wait_recv()

    lane_own = pl.ds(pl.multiple_of(c * LANES, LANES), LANES)

    def lanes_of(owner):
        return pl.ds(pl.multiple_of(owner * LANES, LANES), LANES)

    def act_copy(l, n, owner, dev, place):
        rows = pl.ds(n * map_rows, map_rows)
        view = act.at[0, rows, lanes_of(owner)] if l == 0 else raw.at[l - 1, owner, rows]
        return remote(view, view, ag_s.at[0], ag_r.at[l, place], dev)

    def act_blocks(l, count, place):
        view = act.at[0, :, pl.ds(0, count * LANES)] if l == 0 else raw.at[l - 1, pl.ds(0, count)]
        return remote(view, view, ag_s.at[0], ag_r.at[l, place], (m, core))

    def act_send(l, n):
        if l > 0 and n == 0:
            act_drain(l - 1)
        act_copy(l, n, c, (m, far), n).start()
        act_copy(l, n, c, (m, core), nm).start()

    def act_forward(l, n):
        act_copy(l, n, far, (m, far), n).wait_recv()
        act_copy(l, n, far, (m, core), nm + 1).start()

    def act_near(l):
        act_blocks(l, 1, nm).wait_recv()

    def act_across(l):
        act_blocks(l, 1, nm + 1).wait_recv()

    def act_drain(l):
        act_blocks(l, 3, 0).wait_send()

    def scale_copy(l, owner, dev, ssem):
        view = scale_ref.at[l, owner]
        return remote(view, view, ssem, sc_r.at[l, owner], dev)

    def scale_send(l):
        if l > 0:
            scale_drain(l - 1)
        for other in (core, far, across):
            scale_copy(l, c, (m, other), sc_s.at[0]).start()

    def scale_wait(l, owner):
        scale_copy(l, owner, (m, core), sc_s.at[0]).wait_recv()

    def scale_drain(l):
        view = scale_ref.at[l, pl.ds(0, 3)]
        remote(view, view, sc_s.at[0], sc_r.at[l, core], (m, core)).wait_send()

    own_along(0)
    own_aside_late(0, 0)

    loads[2].wait()
    col_of = lax.broadcasted_iota(jnp.int32, (width, width), 0)
    diagonal = col_of == lax.broadcasted_iota(jnp.int32, (width, width), 1)
    for n in range(nm):

        @pl.loop(0, height)
        def _(h):
            line_n = jnp.broadcast_to(mask_in[h, n : n + 1, :].astype(F32), (width, width))
            r = pl.ds(pl.multiple_of(n * map_rows + h * width, 8), width)
            conv[r, 0:width] = jnp.where(diagonal, line_n, 0.0)

    mask_ref[...] = jnp.dot(
        conv[:, 0:width].astype(BF16), jnp.ones((width, LANES), BF16), preferred_element_type=F32
    )
    loads[1].wait()

    @pl.loop(0, chunks)
    def _(i):
        r = rows_of(i)
        act[0, r, lane_own] = (x_in[r, :].astype(F32) * mask_ref[r, :]).astype(BF16)

    for n in range(nm):
        act_send(0, n)

    own_aside_late(0, 1)

    for n in range(nm):
        for i in range(3):
            for j in range(3):
                prod[i, j, n, 0:PAD, :] = jnp.zeros((PAD, LANES), F32)
                prod[i, j, n, PAD + map_rows :, :] = jnp.zeros((PAD, LANES), F32)
        zpad[n, 0:PAD, :] = jnp.zeros((PAD, LANES), F32)
        zpad[n, PAD + map_rows :, :] = jnp.zeros((PAD, LANES), F32)

    col_chunk = lax.broadcasted_iota(jnp.int32, (6, width, LANES), 1).reshape(chunk, LANES)
    has_left = jnp.where(col_chunk > 0, 1.0, 0.0)
    has_right = jnp.where(col_chunk < width - 1, 1.0, 0.0)

    loads[3].wait()
    loads[4].wait()
    half_h, half_w = height // 2, width // 2

    @pl.loop(0, half_h)
    def _(h):
        pool32[...] = grad_in[h].astype(F32)
        for n in range(nm):
            pick = pl.ds(n, half_w, stride=nm)
            kept = index_in[h, pick, :]
            value = pool32[pick, :]
            base = n * map_rows + 2 * h * width
            for r in range(2):
                for s in range(2):
                    spread[pl.ds(base + r * width + s, half_w, stride=2), :] = jnp.where(
                        kept == 2 * r + s, value, 0.0
                    )

    tasks = gather_tasks(step_both, 0)
    z_tasks = {l: gather_tasks(step_along, l) for l in range(1, layers)}
    x_tasks = {l: gather_tasks(step_aside, l) for l in range(1, layers)}
    c_tasks = {l: cross_tasks(l) for l in range(layers)}
    with scope("gather0"):
        run(tasks, pieces)
        run(c_tasks[0], 1)
        run(tasks, pieces)
        if layers > 1:
            own_along(1)
        run(c_tasks[0], 1)
        run(tasks)
    if layers > 1:
        own_aside_late(1, 0)
    for n in range(nm):
        act_forward(0, n)
    if layers > 1:
        with scope("along_1"):
            run(z_tasks[1], pieces)
    with scope("gather0_cross"):
        run(c_tasks[0])
    with scope("gather0_end"):
        gather_finish(0)
    if layers > 1:
        own_aside_late(1, 1)
    act_near(0)
    act_across(0)
    for cp in loads[5:]:
        cp.wait()

    for l in range(layers):
        z_near, x_near = z_tasks.get(l + 1, []), x_tasks.get(l + 1, [])
        z_next = z_tasks.get(l + 2, [])

        kernel = wcat[l * maps : (l + 1) * maps, :, :].reshape(maps * rows_w, wide)
        for n in range(nm):
            out = jnp.dot(
                act[l, pl.ds(n * map_rows, map_rows), :], kernel, preferred_element_type=F32
            )
            for i in range(3):
                for j in range(3):
                    t = 3 * i + j
                    prod[i, j, n, PAD : PAD + map_rows, :] = out[:, t * LANES : (t + 1) * LANES]

        def conv_chunk(i, carry):
            total, count = carry
            r = rows_of(i)
            value = None
            for j in range(3):
                side = None
                for k in range(3):
                    n, pr = padded_rows(i, width * (k - 1) + (j - 1))
                    term = prod[k, j, n, pr, :]
                    side = term if side is None else side + term
                if j == 0:
                    side = side * has_left
                if j == 2:
                    side = side * has_right
                value = side if value is None else value + side
            conv[r, :] = value
            valid = mask_ref[r, :]
            return total + tile8(value * valid), count + tile8(valid)

        zero8 = jnp.zeros((8, LANES), F32)
        total, count = lax.fori_loop(0, chunks, conv_chunk, (zero8, zero8))
        total = jnp.sum(total, axis=0, keepdims=True)
        count = jnp.sum(count, axis=0, keepdims=True)
        mean = total / jnp.maximum(count, 1.0)

        def dev_chunk(i, carry):
            r = rows_of(i)
            delta = conv[r, :] - mean
            if l + 1 < layers:
                raw[l, c, r, :] = delta.astype(BF16)
            return carry + tile8(delta * delta * mask_ref[r, :])

        spread_sum = zero8
        for n in range(nm):
            spread_sum = lax.fori_loop(n * per_map, (n + 1) * per_map, dev_chunk, spread_sum)
            if l + 1 < layers:
                act_send(l + 1, n)
        spread_sum = jnp.sum(spread_sum, axis=0, keepdims=True)
        stat[l, m] = jnp.concatenate(
            [total, spread_sum, count, mean, jnp.zeros((4, LANES), F32)], axis=0
        )
        stat_send(l)
        with scope("gather_a"):
            run(x_near, len(x_near) - len(z_near))
            if len(z_near) > pieces:
                run(z_near, pieces)
                run(x_near, pieces)
        with scope("turn"):
            slots = LANES // rows_w
            for i, owner in enumerate((across, far, core, c)):
                rows = wcat[pl.ds(l * maps + owner * slots, slots), :, :].reshape(LANES, wide)
                turned[l, :, i * LANES : (i + 1) * LANES] = rows.T
        if l + 1 < layers:
            with scope("gather_own_cross"):
                run(c_tasks[l + 1], 1)
                if l + 2 < layers:
                    own_along(l + 2)
        with scope("stat_wait"):
            stat_wait(l)

        def add_totals(s, carry):
            block = stat[l, s]
            return carry[0] + block[0:1, :], carry[1] + block[2:3, :]

        zero1 = jnp.zeros((1, LANES), F32)
        total, count = lax.fori_loop(0, maps, add_totals, (zero1, zero1))
        center = total / count

        def add_spread(s, carry):
            block = stat[l, s]
            delta = block[3:4, :] - center
            return carry + block[1:2, :] + block[2:3, :] * delta * delta

        variance = lax.fori_loop(0, maps, add_spread, zero1) / count
        inv_std = lax.rsqrt(variance + norm_epsilon)
        gain = gain_in[l : l + 1, :]
        bias = bias_in[l : l + 1, :]
        if l == 0:
            count_all = count
            scales = []
        scales.append(gain * inv_std)

        if l + 1 < layers:
            factor = gain * inv_std
            scale_ref[l, c] = jnp.concatenate(
                [factor, bias + factor * (mean - center), jnp.zeros((6, LANES), F32)], axis=0
            )
            scale_send(l)

        def own_chunk(i, carry):
            r = rows_of(i)
            unit = (conv[r, :] - center) * inv_std
            pre = gain * unit + bias
            sigma = 1.0 / (1.0 + jnp.exp(-pre))
            valid = mask_ref[r, :]
            result = pre * sigma * valid
            slant = sigma * (1.0 + pre * (1.0 - sigma)) * valid
            normed[l, r, :] = unit
            if l + 1 < layers:
                slope[l, r, :] = slant
                act[l + 1, r, lane_own] = result.astype(BF16)
                return carry
            result_ref[r, :] = result
            value = spread[r, :] * slant
            conv[r, :] = value
            return carry[0] + tile8(value * unit), carry[1] + tile8(value)

        grad_sums = lax.fori_loop(0, chunks, own_chunk, (zero8, zero8))

        def activate(owner, first, last):
            pair = scale_ref[l, owner]
            factor, offset = pair[0:1, :], pair[1:2, :]
            lanes = lanes_of(owner)

            @pl.loop(first * per_map, last * per_map)
            def _(i):
                r = rows_of(i)
                pre = factor * raw[l, owner, r, :].astype(F32) + offset
                result = pre / (1.0 + jnp.exp(-pre)) * mask_ref[r, :]
                act[l + 1, r, lanes] = result.astype(BF16)

        if l + 1 < layers:
            with scope("act_near"):
                act_near(l + 1)
                scale_wait(l, core)
                activate(core, 0, nm)
            with scope("gather_b"):
                run(z_near)
                run(x_near)
                run(c_tasks[l + 1], 1)
            with scope("act_far"):
                for n in range(nm):
                    act_forward(l + 1, n)
                    if n == 0:
                        scale_wait(l, far)
                    activate(far, n, n + 1)
            with scope("gather_c"):
                run(c_tasks[l + 1], 1)
                if l + 2 < layers:
                    own_aside(l + 2)
                run(z_next, pieces)
            with scope("act_across"):
                act_across(l + 1)
                scale_wait(l, across)
                activate(across, 0, nm)
            with scope("gather_cross"):
                run(c_tasks[l + 1])
            with scope("gather_end"):
                gather_finish(l + 1)

    def pool():
        @pl.loop(0, half_h)
        def _(h):
            for n in range(nm):
                pick = pl.ds(n, half_w, stride=nm)
                kept = index_in[h, pick, :]
                base = n * map_rows + 2 * h * width
                total = jnp.zeros((half_w, LANES), F32)
                for r in range(2):
                    for s in range(2):
                        total = total + jnp.where(
                            kept == 2 * r + s,
                            result_ref[pl.ds(base + r * width + s, half_w, stride=2), :],
                            0.0,
                        )
                pool32[pick, :] = total
            pooled_ref[h] = pool32[...].astype(BF16)

    def place_of(k):
        before, after = a, line - 1 - a
        spare = jnp.maximum(before, after) - jnp.minimum(before, after)
        q = jnp.maximum(k - spare, 0)
        near, side = q // 2, q % 2
        low = jnp.where(before > after, spare, 0) + near
        high = line - 1 - jnp.where(before < after, spare, 0) - near
        outer = jnp.where(before > after, k, line - 1 - k)
        return jnp.where(k < spare, outer, jnp.where(side == 0, high, low))

    places = {False: [place_of(k) for k in range(line)] if line <= 8 else []}
    places[True] = list(places[False])
    if 2 < line <= 8:
        ends = jnp.logical_or(a == 0, a + 1 == line)
        places[True][0] = jnp.where(ends, places[False][1], places[False][0])
        places[True][1] = jnp.where(ends, places[False][0], places[False][1])

    def kth_place(k, l):
        return places[straight(l)][k] if line <= 8 else place_of(k)

    parts = grad_parts(layers, rows_w)

    def part_of(l, g):
        rows = rows_w // parts[l]
        return pl.ds(g * rows, rows)

    def gx_copy(l, z, g):
        return remote(
            gx_out.at[l, z, part_of(l, g)], gx_in.at[l, z, part_of(l, g)],
            gx_s.at[l], gx_r.at[line * sum(parts[:l]) + z * parts[l] + g], beside,
        )

    def gz_copy(l, z, g, slot, dev):
        return remote(
            gz_out.at[l, z, part_of(l, g)], gz_in.at[l, slot, part_of(l, g)],
            gz_s.at[l], gz_r.at[(line + 1) * sum(parts[:l]) + slot * parts[l] + g], dev,
        )

    def shard(l, slot, g):
        rows = rows_w // parts[l]
        first = pl.multiple_of(slot * rows_w, 8) + g * rows
        return grad_w[l, pl.ds(first, rows), :]

    tile = 2 * rows_w
    fine = tile % LANES == 0

    def kernel_grad(l, first, amount):
        rows = pl.ds(pl.multiple_of(first, LANES), amount)
        grad_w[l, rows, :] = lax.dot_general(
            act[l, :, rows], dcat[...], (((0,), (0,)), ((), ())), preferred_element_type=F32
        )

    def kernel_grads(l, low=0, high=None):
        high = line if high is None else high
        if not fine and low == 0:
            coarse = (maps * rows_w) // 4
            pl.loop(0, 4)(lambda i: kernel_grad(l, i * coarse, coarse))

        def go(k):
            z = kth_place(k, l)
            if fine:
                kernel_grad(l, z * tile, tile)
            for g in range(parts[l]):
                gx_out[l, z, part_of(l, g)] = shard(l, z * 2 + 1 - b, g).astype(BF16)
            if l == 0 and line <= 8 and k == line - 1 and layers > 1:
                for g in range(parts[1]):
                    if is_late(1, k, g):
                        gx_copy(1, a, g).start()
            for g in range(parts[l]):
                if line > 8 or is_early(l, k, g):
                    gx_copy(l, z, g).start()

        steps(low, high, go)

    def is_late(l, k, g):
        return l == 1 and line <= 8 and k == line - 1 and g >= (parts[l] + 1) // 2

    def is_early(l, k, g):
        return l == 0 or k < 2

    def scatter_x(l):
        if line <= 8:
            for k in range(line):
                for g in range(parts[l]):
                    if not is_early(l, k, g) and not is_late(l, k, g):
                        gx_copy(l, kth_place(k, l), g).start()

    def pair_sum(l, z, g):
        gx_copy(l, z, g).wait_recv()
        return shard(l, z * 2 + b, g) + gx_in[l, z, part_of(l, g)].astype(F32)

    def onward(l, z, g, fed, dev, slot):
        value = pair_sum(l, z, g)
        if fed:
            gz_copy(l, z, g, z, dev).wait_recv()
            value = value + gz_in[l, z, part_of(l, g)].astype(F32)
        gz_out[l, z, part_of(l, g)] = value.astype(BF16)
        gz_copy(l, z, g, slot, dev).start()

    def straight(l):
        return False

    def scatter_step(l, d, g, fed):
        ends = straight(l) and d == line - 1
        zr, zl = jnp.minimum(a + d, line - 1), jnp.maximum(a - d, 0)
        more_r, more_l = a > 0, a + 1 < line
        if straight(l):
            more_r = jnp.where(zr == line - 1, a > 1, more_r)
            more_l = jnp.where(zl == 0, a + 2 < line, more_l)
        for there, z, more, dev, slot in (
            (a + d < line, zr, more_r, right, zr),
            (a >= d, zl, more_l, left, jnp.where(zl == a - 1, line, zl)),
        ):
            if ends:
                dev, slot = (z * 2 + b, c), line + 1
            now = jnp.logical_and(there, more if fed else jnp.logical_not(more))
            pl.when(now)(functools.partial(onward, l, z, g, fed, dev, slot))

    def scatter_own(l, g):
        r = part_of(l, g)
        total_w[r, :] = pair_sum(l, a, g)

        def add(slot):
            gz_copy(l, a, g, slot, left).wait_recv()
            total_w[r, :] += gz_in[l, slot, r].astype(F32)

        pl.when(a > 0)(lambda: add(a))
        pl.when(a + 1 < line)(lambda: add(line))
        if straight(l):
            pl.when(jnp.logical_or(a == 0, a + 1 == line))(lambda: add(line + 1))
        for t in range(taps):
            gradient = total_w[r, t * LANES : (t + 1) * LANES]
            new, first, second = adamw_update(
                weight_in[l, t, r], gradient, first_in[l, t, r], second_in[l, t, r], rate_conv
            )
            wgrad_ref[l, t, r] = gradient
            wfirst_ref[l, t, r] = first
            wsecond_ref[l, t, r] = second
            wnew_ref[l, t, r] = new
            wcopy_ref[l, t, r] = new.astype(BF16)

    def scatter_tasks(l):
        owns = [functools.partial(scatter_own, l, g) for g in range(parts[l])]
        if line <= 8:
            first, fed = (
                [
                    functools.partial(scatter_step, l, line - e, g, kind)
                    for e in ((2, 1, *range(3, line)) if straight(l) else range(1, line))
                    if e > kind + (kind and straight(l))
                    for g in range(parts[l])
                ]
                for kind in (False, True)
            )
            return first, fed, owns

        def everything():
            def go(e):
                for g in range(parts[l]):
                    scatter_step(l, line - e, g, False)
                    scatter_step(l, line - e, g, True)

            steps(1, line, go)

        return [everything], [], owns

    def scatter_drain(l):
        remote(gx_out.at[l], gx_in.at[l], gx_s.at[l], gx_r.at[0], beside).wait_send()
        view = pl.ds(0, line - 1)
        remote(
            gz_out.at[l, view], gz_in.at[l, view], gz_s.at[l], gz_r.at[0], beside
        ).wait_send()

    def layer_drain(l):
        remote(pair_out.at[l], pair_in.at[l], pr_s.at[l], pr_r.at[l, 0], (m, core)).wait_send()
        remote(far_out.at[l], far_in.at[l], fr_s.at[l], fr_r.at[l, 0], (m, far)).wait_send()

    half = 2 * LANES
    def pair_copy(l, h, n):
        return remote(
            pair_out.at[l, h, pl.ds(n * map_rows, map_rows), :],
            pair_in.at[l, h, pl.ds(n * map_rows, map_rows), :],
            pr_s.at[l], pr_r.at[l, n if h == 0 else nm], (m, core),
        )

    def far_copy(l, n):
        return remote(
            far_out.at[l, pl.ds(n * map_rows, map_rows), :],
            far_in.at[l, pl.ds(n * map_rows, map_rows), :],
            fr_s.at[l], fr_r.at[l, n], (m, far),
        )

    todo, fed, owns = {}, {}, {}
    for l in reversed(range(layers)):
        e = layers + l
        gain_sum, bias_sum = grad_sums
        stat[e, m] = jnp.concatenate(
            [
                jnp.sum(gain_sum, axis=0, keepdims=True),
                jnp.sum(bias_sum, axis=0, keepdims=True),
                jnp.zeros((6, LANES), F32),
            ],
            axis=0,
        )
        stat_send(e)
        if l + 1 < layers:
            scatter_x(l + 1)
        else:
            pool()
        if l + 1 < layers:
            todo[l + 1], fed[l + 1], owns[l + 1] = scatter_tasks(l + 1)
        if l + 2 < layers:
            run(todo[l + 2])
            run(fed[l + 2])
        if l + 1 < layers:
            with scope("scatter_a"):
                run(todo[l + 1], parts[l + 1] if l > 0 else 2 * parts[l + 1])
        with scope("stat_wait_back"):
            stat_wait(e)

        def add_sums(s, carry):
            return carry + stat[e, s]

        sums = lax.fori_loop(0, maps, add_sums, jnp.zeros((8, LANES), F32))
        ngrad_ref[l] = sums[0:2, :]
        gain_grad = sums[0:1, :]
        bias_grad = sums[1:2, :]
        scale = scales[l]

        def conv_grad(n):
            @pl.loop(n * per_map, (n + 1) * per_map)
            def _(i):
                r = rows_of(i)
                value = (
                    mask_ref[r, :]
                    * scale
                    * (conv[r, :] - (bias_grad + normed[l, r, :] * gain_grad) / count_all)
                )
                pr = pl.ds(pl.multiple_of((i - n * per_map) * chunk, 16) + PAD, chunk)
                zpad[n, pr, :] = value

            @pl.loop(n * per_map, (n + 1) * per_map)
            def _(i):
                r = rows_of(i)
                for k in range(3):
                    for j in range(3):
                        shift = PAD - (width * (k - 1) + (j - 1))
                        pr = pl.ds(pl.multiple_of((i - n * per_map) * chunk, 16) + shift, chunk)
                        term = zpad[n, pr, :]
                        if j == 0:
                            term = term * has_right
                        if j == 2:
                            term = term * has_left
                        t = 3 * k + j
                        dcat[r, t * LANES : (t + 1) * LANES] = term.astype(BF16)

        def input_grad(h, first, last):
            r = pl.ds(first * map_rows, (last - first) * map_rows)
            out = jnp.dot(
                dcat[r, :], turned[l, :, h * half : (h + 1) * half], preferred_element_type=F32
            )
            pair_out[l, h, r, :] = out[:, :LANES].astype(BF16)
            for n in range(first, last):
                pair_copy(l, h, n).start()
            part[h, r, :] = out[:, LANES:]

        def to_far(n):
            r = pl.ds(n * map_rows, map_rows)
            pair_copy(l, 0, n).wait_recv()
            far_out[l, r, :] = (part[0, r, :] + pair_in[l, 0, r, :].astype(F32)).astype(BF16)
            far_copy(l, n).start()

        if l > 0:
            for n in range(nm):
                with scope("conv_grad"):
                    conv_grad(n)
                with scope("input_grad"):
                    input_grad(0, n, n + 1)
                if n > 0:
                    with scope("to_far"):
                        to_far(n - 1)
            if l + 1 < layers:
                with scope("scatter_b"):
                    run(todo[l + 1], parts[l + 1])
                    run(fed[l + 1], parts[l + 1])
            with scope("kernel_grad"):
                kernel_grads(l, 0, line // 2)
            with scope("to_far"):
                to_far(nm - 1)
            if l + 1 < layers:
                with scope("scatter_c"):
                    run(todo[l + 1])
            with scope("kernel_grad"):
                kernel_grads(l, line // 2)
            with scope("input_grad"):
                input_grad(1, 0, nm)
            with scope("drain"):
                if l + 1 == layers:
                    for k in range(layers):
                        gather_drain(k)
                    act_drain(layers - 1)
                    if layers > 1:
                        scale_drain(layers - 2)
                else:
                    layer_drain(l + 1)
        else:
            for n in range(nm):
                with scope("conv_grad"):
                    conv_grad(n)
            with scope("kernel_grad"):
                kernel_grads(0)
            todo[0], fed[0], owns[0] = scatter_tasks(0)
            with scope("scatter_1c"):
                run(todo[1])
                run(fed[1], parts[1])
            with scope("input_grad"):
                input_grad(0, 0, nm)
            with scope("to_far"):
                for n in range(nm):
                    to_far(n)
            with scope("scatter_0a"):
                run(todo[0], parts[0])
            with scope("scatter_1d"):
                run(fed[1])
            with scope("input_grad"):
                input_grad(1, 0, nm)
            with scope("scatter_0b"):
                run(todo[0], parts[0])
                run(fed[0], parts[0])
            with scope("owns_2"):
                for k in range(layers - 1, 1, -1):
                    run(owns[k])

        zero8 = jnp.zeros((8, LANES), F32)
        grad_sums = (zero8, zero8)
        for n in range(nm):
            r = pl.ds(n * map_rows, map_rows)
            with scope("far_wait"):
                if n == 0:
                    remote(
                        pair_out.at[l, 1], pair_in.at[l, 1], pr_s.at[l], pr_r.at[l, nm], (m, core)
                    ).wait_recv()
                far_copy(l, n).wait_recv()
            if n == 0 and l > 0 and l + 1 < layers:
                with scope("scatter_d"):
                    run(fed[l + 1])

            def back_chunk(i, carry):
                r = rows_of(i)
                value = part[1, r, :] + pair_in[l, 1, r, :].astype(F32) + far_in[l, r, :].astype(F32)
                if l == 0:
                    back[r, :] = value * mask_ref[r, :]
                    return carry
                value = value * slope[l - 1, r, :]
                conv[r, :] = value
                return carry[0] + tile8(value * normed[l - 1, r, :]), carry[1] + tile8(value)

            grad_sums = lax.fori_loop(n * per_map, (n + 1) * per_map, back_chunk, grad_sums)

    with scope("norms"):
        for values, place in ((gain_in, 0), (bias_in, 1)):
            new, first, second = adamw_update(
                values[...], ngrad_ref[:, place, :], norm_first_in[:, place, :],
                norm_second_in[:, place, :], rate_norm,
            )
            nfirst_ref[:, place, :] = first
            nsecond_ref[:, place, :] = second
            nnew_ref[:, place, :] = new
    with scope("scatter_end"):
        run(todo[0])
        run(fed[0])
    with scope("owns_1"):
        for k in range(1, min(2, layers)):
            run(owns[k])
    with scope("drain"):
        for k in range(1, layers):
            scatter_drain(k)
        layer_drain(1)
    with scope("owns"):
        run(owns[0])

    with scope("drain_end"):
        layer_drain(0)
        scatter_drain(0)
        stat_all(exchanged[-1]).wait_send()


def store_kernel(count, *refs):
    copies = [
        pltpu.make_async_copy(refs[i], refs[count + i], refs[2 * count].at[i]) for i in range(count)
    ]
    for cp in copies:
        cp.start()
    for cp in copies:
        cp.wait()


def store_results(results):
    any_spec = pl.BlockSpec(memory_space=pl.ANY)
    count = len(results)
    return pl.pallas_call(
        functools.partial(store_kernel, count),
        out_shape=tuple(jax.ShapeDtypeStruct(r.shape, r.dtype) for r in results),
        in_specs=[any_spec] * count,
        out_specs=(any_spec,) * count,
        scratch_shapes=[pltpu.SemaphoreType.DMA((count,))],
        compiler_params=pltpu.CompilerParams(vmem_limit_bytes=1 << 20),
    )(*results)


def block_call(maps, chans, x, mask, index, grad, weights, gain, bias, *moments):
    nm, height, width, lanes = x.shape
    layers, taps, rows_w, _ = weights.shape
    pixels = nm * height * width
    line = maps // 2
    wide = taps * LANES
    channels = chans * LANES
    map_rows = height * width
    sizes = (maps, chans, layers, taps, nm, height, width)
    pieces = 2 if rows_w % 32 == 0 else 1
    vm = pltpu.VMEM
    dma = pltpu.SemaphoreType.DMA
    hbm = pl.BlockSpec(memory_space=pltpu.HBM)
    scratch = [
        vm((pixels, LANES), BF16), vm(mask.shape, jnp.int32), vm(index.shape, jnp.int32),
        vm(grad.shape, BF16), vm(weights.shape, F32), vm(gain.shape, F32), vm(bias.shape, F32),
        *(vm(v.shape, F32) for v in moments),
        vm((pixels, LANES), F32),
        vm((layers * maps, rows_w, wide), BF16),
        vm((layers, wide, channels), BF16),
        vm((layers, pixels, channels), BF16),
        vm((layers - 1, chans, pixels, LANES), BF16),
        vm((layers - 1, chans, 8, LANES), F32),
        vm((3, 3, nm, map_rows + 2 * PAD, LANES), F32),
        vm((pixels, LANES), F32),
        vm((layers, pixels, LANES), F32),
        vm((layers, pixels, LANES), F32),
        vm((pixels, LANES), F32),
        vm((pixels, LANES), F32),
        vm((nm * (width // 2), LANES), F32),
        vm((nm, map_rows + 2 * PAD, LANES), F32),
        vm((pixels, wide), BF16),
        vm((layers, channels, wide), F32),
        vm((2, pixels, LANES), F32),
        vm((2 * layers, maps, 8, LANES), F32),
        vm((layers, 2, pixels, LANES), BF16), vm((layers, 2, pixels, LANES), BF16),
        vm((layers, pixels, LANES), BF16), vm((layers, pixels, LANES), BF16),
        vm((layers, line, rows_w, wide), BF16), vm((layers, line, rows_w, wide), BF16),
        vm((layers, line, rows_w, wide), BF16), vm((layers, line + 1, rows_w, wide), BF16),
        vm((rows_w, wide), F32),
        dma((11,)),
        dma((layers, 4)), dma((layers, line, pieces)), dma((layers, 2)), dma((layers, line)),
        dma((1,)), dma((2,)),
        dma((1,)), dma((layers, nm + 2)),
        dma((1,)), dma((layers - 1, chans)),
        dma((layers,)), dma((layers, nm + 1)),
        dma((layers,)), dma((layers, nm)),
        dma((layers,)), dma((line * sum(grad_parts(layers, rows_w)),)),
        dma((layers,)), dma(((line + 1) * sum(grad_parts(layers, rows_w)),)),
    ]
    arrays = (
        [(index.shape, BF16), ((pixels, LANES), F32)]
        + [(weights.shape, F32)] * 4
        + [(weights.shape, BF16)]
        + [((layers, 2, LANES), F32)] * 4
    )
    return pl.pallas_call(
        functools.partial(block_kernel, sizes),
        out_shape=tuple(jax.ShapeDtypeStruct(*kind) for kind in arrays),
        in_specs=[hbm] * 11,
        out_specs=(pl.BlockSpec(memory_space=pltpu.VMEM),) * len(arrays),
        scratch_shapes=scratch,
        compiler_params=pltpu.CompilerParams(
            collective_id=0, has_side_effects=True, vmem_limit_bytes=48 << 20
        ),
    )(*(
        pltpu.with_memory_space_constraint(v, pltpu.HBM)
        for v in (x.reshape(pixels, LANES), mask, index, grad, weights, gain, bias, *moments)
    ))


def local(
    maps, chans,
    input_maps, valid_mask, pool_index, out_grad, conv_weights, weight_first, weight_second,
    norm_gain, norm_bias, norm_first, norm_second,
):
    nm, half_h, half_w, lanes = pool_index.shape
    by_row = (half_h, half_w * nm, lanes)
    pooled, image, *updates = store_results(
        block_call(
            maps, chans, input_maps, valid_mask.transpose(1, 0, 2),
            pool_index.transpose(1, 2, 0, 3).reshape(by_row),
            out_grad.transpose(1, 2, 0, 3).reshape(by_row),
            conv_weights, norm_gain, norm_bias, weight_first, weight_second, norm_first, norm_second,
        )
    )
    pooled = pooled.reshape(half_h, half_w, nm, lanes).transpose(2, 0, 1, 3)
    return (pooled, image.reshape(input_maps.shape), *updates)


def solution(mesh):
    return jax.shard_map(
        functools.partial(local, mesh.shape["maps"], mesh.shape["chan"]),
        mesh=mesh,
        in_specs=(
            P("maps", None, None, "chan"),
            P("maps", None, None),
            P("maps", None, None, "chan"),
            P("maps", None, None, "chan"),
            P(None, None, "maps", "chan"),
            P(None, None, "maps", "chan"),
            P(None, None, "maps", "chan"),
            P(None, "chan"),
            P(None, "chan"),
            P(None, None, "chan"),
            P(None, None, "chan"),
        ),
        out_specs=(
            P("maps", None, None, "chan"),
            P("maps", None, None, "chan"),
            P(None, None, "maps", "chan"),
            P(None, None, "maps", "chan"),
            P(None, None, "maps", "chan"),
            P(None, None, "maps", "chan"),
            P(None, None, "maps", "chan"),
            P(None, None, "chan"),
            P(None, None, "chan"),
            P(None, None, "chan"),
            P(None, None, "chan"),
        ),
        check_vma=False,
    )
```
